32 devices in a mesh: dp: 4 (over y, x), tm: 2 (over core), space: 4 (over z).
Axes of the slice: x: 2, y: 2, z: 4, core: 2. Of those that a mesh axis runs over, the one named last changes fastest.
Arguments:
- video: bfloat16 [4, 8, 64, 128, 128], P('dp', 'tm', 'space'), may hold values from -6 to 6
- lengths: int32 [4], P('dp'), may hold values from 2 to 8
- norm_gain: float32 [128], replicated, may hold values from 0.25 to 1.75
- norm_shift: float32 [128], replicated, may hold values from -3 to 3
- kernel: bfloat16 [3, 3, 3, 128, 128], replicated, may hold values from -0.109375 to 0.109375
- conv_bias: float32 [128], replicated, may hold values from -3 to 3
- cotangent: bfloat16 [4, 8, 64, 128, 128], P('dp', 'tm', 'space'), may hold values from -0.01171875 to 0.01171875
Outputs:
- output: bfloat16 [4, 8, 64, 128, 128], P('dp', 'tm', 'space')
- grad_kernel: float32 [3, 3, 3, 128, 128], replicated
- grad_bias: float32 [128], replicated
The draws below stay inside these ranges and needn't reach their ends.
All inputs are finite; a program needn't handle non-finite values.
Results may differ from the reference program's by a relative error of at most 0.0032.
Values may be sent and summed in bfloat16 or wider, within the bound.
No kernel may reach another device: no remote copies, remote signals or barrier semaphores. Data moves between devices by JAX's collectives and lax.ppermute only.
A program may use at most 128 MiB of HBM per device.

```python
import jax
import jax.numpy as jnp
from jax import lax

C = 128
GROUPS = 32
WIDTH = 128
CLIPS = 4
FRAMES = 8
HEIGHT = 64


def plant(entries, key, low, largest):
    longest = entries.shape.index(max(entries.shape))
    spots = []
    for shift in (0, 1):
        where = [jax.random.randint(jax.random.fold_in(key, axis), (), 0, length) for axis, length in enumerate(entries.shape)]
        where[longest] = (where[longest] + shift) % entries.shape[longest]
        spots.append(tuple(where))
    return entries.at[spots[0]].set(low).at[spots[1]].set(largest)


def level_of(stream_key, extent, pieces, least, top_value):
    loudness = 1.0
    for position, shards_of in pieces:
        draws = jax.random.uniform(jax.random.fold_in(jax.random.fold_in(stream_key, 6), position), (shards_of,), jnp.float32, least / len(pieces), top_value / len(pieces))
        loudness = loudness * jnp.repeat(jnp.exp(draws), extent[position] // shards_of).reshape((-1,) + (1,) * (len(extent) - 1 - position))
    return loudness


def centred(key, dims, deviation, reach, split=(), kind=jnp.bfloat16):
    level = level_of(key, dims, split, -0.22, 0.18) if split else 1.0
    result = jax.random.normal(key, dims, jnp.float32) * deviation * level
    return jnp.minimum(jnp.maximum(result, -reach), reach).astype(kind)


def setup_inputs(seed: int = 0) -> dict:
    splits = jax.random.split(jax.random.key(seed), 8)
    video = centred(splits[0], (CLIPS, FRAMES, HEIGHT, WIDTH, C), 1.0, 6.0, ((0, 4), (1, 2), (2, 4)))
    lengths = plant(jax.random.randint(splits[1], (CLIPS,), FRAMES // 4, FRAMES + 1), jax.random.fold_in(splits[1], 1), FRAMES // 4, FRAMES).astype(jnp.int32)
    norm_gain = jnp.clip(1.0 + 0.15 * jax.random.normal(splits[2], (C,), jnp.float32), 0.25, 1.75)
    norm_shift = centred(splits[3], (C,), 0.5, 3.0, (), jnp.float32)
    kernel = centred(splits[4], (3, 3, 3, C, C), (27 * C) ** -0.5, 0.109375)
    conv_bias = centred(splits[5], (C,), 0.5, 3.0, (), jnp.float32)
    cotangent = centred(splits[6], (CLIPS, FRAMES, HEIGHT, WIDTH, C), (CLIPS * FRAMES * HEIGHT * WIDTH) ** -0.5, 0.01171875, ((0, 4), (1, 2), (2, 4)))
    return {"video": video, "lengths": lengths, "norm_gain": norm_gain, "norm_shift": norm_shift, "kernel": kernel, "conv_bias": conv_bias, "cotangent": cotangent}


def one_clip(video, length, norm_gain, norm_shift, kernel, conv_bias, cotangent):
    frames = video.shape[0]
    rows = video.shape[1]
    cols = video.shape[2]
    chans = video.shape[3]
    per = chans // GROUPS
    valid = (jnp.arange(frames, dtype=jnp.int32) < length).astype(jnp.float32)
    mask = valid[:, None, None, None, None]
    grouped = video.astype(jnp.float32).reshape(frames, rows, cols, GROUPS, per)
    count = length.astype(jnp.float32) * rows * cols * per
    mean = lax.optimization_barrier(jnp.sum(grouped * mask, axis=(0, 1, 2, 4))) / count
    spread = (grouped - mean[:, None]) * mask
    variance = lax.optimization_barrier(jnp.sum(spread * spread, axis=(0, 1, 2, 4))) / count
    normed = (grouped - mean[:, None]) * lax.rsqrt(variance + 1e-05)[:, None]
    normed = normed.reshape(frames, rows, cols, chans) * norm_gain + norm_shift
    activated = (jax.nn.silu(normed) * valid[:, None, None, None]).astype(jnp.bfloat16)
    padded = jnp.pad(activated, ((2, 0), (1, 1), (1, 1), (0, 0)))
    masked = (cotangent.astype(jnp.float32) * valid[:, None, None, None]).astype(jnp.bfloat16)
    flat_grad = masked.reshape(-1, chans)
    conv = jnp.zeros((frames * rows * cols, chans), jnp.float32)
    grads = []
    for kt in range(3):
        for ky in range(3):
            for kx in range(3):
                window = padded[kt:kt + frames, ky:ky + rows, kx:kx + cols].reshape(-1, chans)
                conv = conv + jnp.dot(window, kernel[kt, ky, kx], preferred_element_type=jnp.float32)
                grads.append(jnp.dot(window.T, flat_grad, preferred_element_type=jnp.float32))
    conv = conv.reshape(frames, rows, cols, chans)
    output = ((video.astype(jnp.float32) + conv + conv_bias) * valid[:, None, None, None]).astype(jnp.bfloat16)
    grad_kernel = jnp.stack(grads).reshape(3, 3, 3, chans, chans)
    grad_bias = lax.optimization_barrier(jnp.sum(flat_grad.astype(jnp.float32), axis=0))
    return (output, grad_kernel, grad_bias)

def reference(video, lengths, norm_gain, norm_shift, kernel, conv_bias, cotangent):

    def clip_step(items):
        return one_clip(items[0], items[1], norm_gain, norm_shift, kernel, conv_bias, items[2])
    output, grad_kernel, grad_bias = lax.map(clip_step, (video, lengths, cotangent))
    return (output, lax.optimization_barrier(jnp.sum(grad_kernel, axis=0)), lax.optimization_barrier(jnp.sum(grad_bias, axis=0)))
```

```python
import functools

import jax
import jax.numpy as jnp
from jax import lax
from jax.experimental import pallas as pl
from jax.experimental.pallas import tpu as pltpu
from jax.sharding import PartitionSpec as P

GROUPS = 32
TILE = 16
F32 = jnp.float32
BF16 = jnp.bfloat16
VMEM = pl.BlockSpec(memory_space=pltpu.VMEM)
SMEM = pl.BlockSpec(memory_space=pltpu.SMEM)


def params(mib):
    return pltpu.CompilerParams(vmem_limit_bytes=mib * 1024 * 1024)


def swap(array, axis, by):
    length = lax.axis_size(axis)
    assert length & (length - 1) == 0
    return lax.ppermute(array, axis, [(i, i ^ by) for i in range(length)])


def shifted(array, axis, by):
    length = lax.axis_size(axis)
    return lax.ppermute(array, axis, [(i, i + by) for i in range(length) if 0 <= i + by < length])


def group_sum(row, per):
    value = jnp.broadcast_to(row, (8, row.shape[1]))
    lane = lax.broadcasted_iota(jnp.int32, value.shape, 1)
    size = value.shape[1]
    step = 1
    while step < per:
        up = pltpu.roll(value, size - step, 1)
        down = pltpu.roll(value, step, 1)
        value = value + jnp.where((lane & step) == 0, up, down)
        step *= 2
    return value[0:1]


def merged(parts):
    count = sum(part[0:1] for part in parts)
    total = sum(part[1:2] for part in parts)
    mean = total / jnp.maximum(count, 1.0)
    squares = jnp.zeros_like(mean)
    for part in parts:
        away = part[1:2] / jnp.maximum(part[0:1], 1.0) - mean
        squares = squares + (part[2:3] + part[0:1] * (away * away))
    return count, total, mean, squares


def stats_kernel(per, info_ref, video_ref, out_ref, sums, squares):
    frames = pl.num_programs(0)
    t = pl.program_id(0)
    rows, cols, chans = video_ref.shape[2:]
    size = float(rows * cols * per)

    def add(y, acc):
        return acc + jnp.sum(video_ref[0, 0, y].astype(F32).reshape(cols // 8, 8, chans), axis=0)

    acc = lax.fori_loop(0, rows, add, jnp.zeros((8, chans), F32), unroll=4)
    total = group_sum(jnp.sum(acc, axis=0, keepdims=True), per)
    mean = total / size

    def deviate(y, acc):
        away = video_ref[0, 0, y].astype(F32).reshape(cols // 8, 8, chans) - mean
        return acc + jnp.sum(away * away, axis=0)

    acc = lax.fori_loop(0, rows, deviate, jnp.zeros((8, chans), F32), unroll=4)
    sums[t] = jnp.broadcast_to(total, (8, chans))
    squares[t] = jnp.broadcast_to(group_sum(jnp.sum(acc, axis=0, keepdims=True), per), (8, chans))

    @pl.when(t == frames - 1)
    def _():
        inside = info_ref[0]
        parts = []
        for f in range(sums.shape[0]):
            keep = (f < inside).astype(F32)
            parts.append(
                jnp.concatenate(
                    [jnp.full((1, chans), size, F32), sums[f, 0:1], squares[f, 0:1]], axis=0
                )
                * keep
            )
        count, total, _, deviations = merged(parts)
        out_ref[...] = jnp.concatenate(
            [count, total, deviations, jnp.zeros((5, chans), F32)], axis=0
        )


def merge_kernel(*refs):
    count, total, _, deviations = merged([ref[...] for ref in refs[:-1]])
    refs[-1][...] = jnp.concatenate(
        [count, total, deviations, jnp.zeros((5, count.shape[1]), F32)], axis=0
    )


def cotangent_kernel(info_ref, cot_ref, turned_ref, bias_ref, wide):
    t = pl.program_id(0)
    rows, cols, chans = cot_ref.shape[2:]
    step = cols // TILE
    keep = (t < info_ref[0]).astype(F32)

    @pl.when(t == 0)
    def _():
        bias_ref[...] = jnp.zeros_like(bias_ref)

    def row(y, acc):
        value = cot_ref[0, 0, y].astype(F32) * keep
        slot = wide.at[y % wide.shape[0]]
        slot[...] = value
        order = jnp.concatenate(
            [slot[pl.ds(r, TILE, stride=step), :] for r in range(step)], axis=0
        )
        turned_ref[0, y] = order.T.astype(BF16)
        return acc + jnp.sum(value.reshape(cols // 8, 8, chans), axis=0)

    acc = lax.fori_loop(0, rows, row, jnp.zeros((8, chans), F32), unroll=4)
    bias_ref[0:1, :] += jnp.sum(acc, axis=0, keepdims=True)


def activate_kernel(
    parts_n, info_ref, video_ref, early_ref, low_ref, high_ref, gain_ref, shift_ref, *refs
):
    parts, out_ref, wide = refs[:parts_n], refs[parts_n], refs[parts_n + 1]
    frames, rows, cols, chans = video_ref.shape[1:]
    before = early_ref.shape[1]
    step = cols // TILE
    inside, first, has_low, has_high = info_ref[0], info_ref[1], info_ref[2], info_ref[3]
    count, _, mean, squares = merged([ref[...] for ref in parts])
    scale = 0.5 * lax.rsqrt(squares / count + 1e-05) * gain_ref[...]
    offset = 0.5 * shift_ref[...] - mean * scale
    slots = wide.shape[0]
    wide[:, 0:8, :] = jnp.zeros((slots, 8, chans), F32)
    wide[:, 8 + cols : 16 + cols, :] = jnp.zeros((slots, 8, chans), F32)

    def row(values, keep, slot, f, y):
        half = values.astype(F32) * (scale * keep) + offset * keep
        wide[slot, 8 : 8 + cols, :] = half + half * jnp.tanh(half)
        for r in range(-1, step + 1):
            out_ref[f, y, r + 1] = wide[slot, pl.ds(8 + r, TILE, stride=step), :].astype(BF16)

    for f in range(frames + before):
        local = f - before
        ok = (local < inside) & (first + local >= 0)
        keep = ok.astype(F32)
        source = early_ref.at[0, f] if local < 0 else video_ref.at[0, local]

        def inner(y, carry, source=source, keep=keep, f=f):
            row(source[y], keep, y % slots, f, y + 1)
            return carry

        lax.fori_loop(0, rows, inner, 0, unroll=4)
        row(low_ref[0, f, 0], keep * has_low.astype(F32), 0, f, 0)
        row(high_ref[0, f, 0], keep * has_high.astype(F32), 1, f, rows + 1)


def packed(value):
    per = value.shape[0] - TILE
    total = value[per : per + 1] + value[per + 1 : per + 2] + value[per + 2 : per + 3]
    top = total.astype(BF16).astype(F32)
    mid = (total - top).astype(BF16).astype(F32)
    rest = total - top - mid
    tail = jnp.concatenate([top, mid, rest, jnp.zeros((TILE - 3, value.shape[1]), F32)], axis=0)
    return jnp.concatenate([value[:per].astype(BF16), tail.astype(BF16)], axis=0)


def weights_kernel(info_ref, turned_ref, act_ref, bias_ref, keep_ref, *refs):
    send_refs, acc = refs[:-2], refs[-2:]
    acc, shards = acc
    frames, rows = turned_ref.shape[:2]
    chans = turned_ref.shape[2]
    k = turned_ref.shape[3]
    step = act_ref.shape[2] - 2
    taps = [(kt, ky, kx) for kt in range(3) for ky in range(3) for kx in range(3)]
    pair = 2

    def frame(t, carry):
        left = jnp.concatenate([turned_ref[t, y] for y in range(rows)], axis=1)
        for j in range(0, len(taps), pair):
            chosen = taps[j : j + pair]
            right = jnp.concatenate(
                [
                    act_ref[t + kt, ky : ky + rows, kx : kx + step].reshape(rows * k, chans)
                    for kt, ky, kx in chosen
                ],
                axis=1,
            )
            product = jnp.dot(left, right, preferred_element_type=F32)
            where = slice(j * chans, (j + len(chosen)) * chans)
            acc[:, where] = jnp.where(t == 0, product, acc[:, where] + product)
        return carry

    lax.fori_loop(0, frames, frame, 0)
    tms, dps, per = shards.shape[:3]
    per -= TILE
    for tap in range(len(taps)):
        block = acc[:, tap * chans : (tap + 1) * chans].T
        done = 0
        while done < chans:
            shard, at = divmod(tap * chans + done, per)
            take = min(chans - done, per - at)
            shards[shard // dps, shard % dps, at : at + take, :] = block[done : done + take]
            done += take
    tail = jnp.concatenate([bias_ref[0:1], jnp.zeros((TILE - 1, chans), F32)], axis=0)
    for i in range(tms):
        for j in range(dps):
            shards[i, j, per : per + TILE, :] = tail
    me = info_ref[4]
    keep_ref[...] = shards[me]
    for r in range(1, tms):
        send_refs[r - 1][...] = shards[me ^ r]


def spread_kernel(count, info_ref, keep_ref, *refs):
    incoming, own_ref, send_refs = refs[:count], refs[count], refs[count + 1 :]
    me = info_ref[5]
    for r in range(len(send_refs) + 1):
        value = keep_ref[me ^ r]
        for ref in incoming:
            value = value + ref[me ^ r]
        if r == 0:
            own_ref[...] = value
        else:
            send_refs[r - 1][...] = packed(value)


def add_kernel(*refs):
    value = refs[0][...].astype(F32)
    for ref in refs[1:-1]:
        value = value + ref[...].astype(F32)
    refs[-1][...] = packed(value) if refs[-1].dtype == BF16 else value


def conv_kernel(t0, info_ref, act_ref, taps_ref, video_ref, bias_ref, out_ref, wide):
    block = pl.program_id(0)
    frames_out, rows, cols, chans = out_ref.shape[1:]
    step = cols // TILE
    y0 = block * rows
    left = jnp.concatenate(
        [
            act_ref[f, pl.ds(y0 + ky, rows), kx : kx + step].reshape(rows * cols, chans)
            for f in range(frames_out + 2)
            for ky in range(3)
            for kx in range(3)
        ],
        axis=1,
    )
    result = jnp.dot(left, taps_ref[...], preferred_element_type=F32)
    for f in range(frames_out):
        keep = (t0 + f < info_ref[0]).astype(F32)
        for y in range(rows):
            slot = f * rows + y
            for r in range(step):
                at = y * cols + r * TILE
                wide[slot, pl.ds(r, TILE, stride=step), :] = result[
                    at : at + TILE, f * chans : (f + 1) * chans
                ]
            value = video_ref[0, f, y].astype(F32) + wide[slot] + bias_ref[...]
            out_ref[0, f, y] = (value * keep).astype(BF16)


def body(video, lengths, norm_gain, norm_shift, kernel, conv_bias, cotangent):
    frames, rows, cols, chans = video.shape[1:]
    per = chans // GROUPS
    step = cols // TILE
    before = kernel.shape[0] - 1
    tms, dps, spaces = (lax.axis_size(axis) for axis in ("tm", "dp", "space"))
    tm, dp, space = (lax.axis_index(axis) for axis in ("tm", "dp", "space"))
    first = tm * frames
    inside = jnp.clip(lengths[0] - first, -before, frames)
    info = jnp.stack(
        [
            inside,
            first,
            (space > 0).astype(jnp.int32),
            (space < spaces - 1).astype(jnp.int32),
            tm,
            dp,
        ]
    ).astype(jnp.int32)

    early = shifted(video[:, frames - before :], "tm", 1)

    frame_spec = pl.BlockSpec((1, 1, rows, cols, chans), lambda t: (0, t, 0, 0, 0))
    stats = pl.pallas_call(
        functools.partial(stats_kernel, per),
        grid=(frames,),
        in_specs=[SMEM, frame_spec],
        out_specs=pl.BlockSpec((8, chans), lambda t: (0, 0)),
        out_shape=jax.ShapeDtypeStruct((8, chans), F32),
        scratch_shapes=[pltpu.VMEM((frames, 8, chans), F32), pltpu.VMEM((frames, 8, chans), F32)],
        name="stats",
    )(info, video)
    stats = pl.pallas_call(
        merge_kernel,
        in_specs=[VMEM] * tms,
        out_specs=VMEM,
        out_shape=jax.ShapeDtypeStruct((8, chans), F32),
        name="merge",
    )(stats, *[swap(stats, "tm", r) for r in range(1, tms)])
    parts = [stats] + [swap(stats, "space", r) for r in range(1, spaces)]

    edge_low = jnp.concatenate([early[:, :, rows - 1 :], video[:, :, rows - 1 :]], axis=1)
    edge_high = jnp.concatenate([early[:, :, :1], video[:, :, :1]], axis=1)
    low = shifted(edge_low, "space", 1)
    high = shifted(edge_high, "space", -1)

    turned, bias = pl.pallas_call(
        cotangent_kernel,
        grid=(frames,),
        in_specs=[SMEM, frame_spec],
        out_specs=[
            pl.BlockSpec((1, rows, chans, cols), lambda t: (t, 0, 0, 0)),
            pl.BlockSpec((8, chans), lambda t: (0, 0)),
        ],
        out_shape=[
            jax.ShapeDtypeStruct((frames, rows, chans, cols), BF16),
            jax.ShapeDtypeStruct((8, chans), F32),
        ],
        scratch_shapes=[pltpu.VMEM((4, cols, chans), F32)],
        name="cotangent",
    )(info, cotangent)

    act = pl.pallas_call(
        functools.partial(activate_kernel, spaces),
        in_specs=[SMEM] + [VMEM] * (6 + spaces),
        out_specs=VMEM,
        out_shape=jax.ShapeDtypeStruct(
            (frames + before, rows + 2, step + 2, TILE, chans), BF16
        ),
        scratch_shapes=[pltpu.VMEM((4, cols + 16, chans), F32)],
        compiler_params=params(24),
        name="activate",
    )(
        info,
        video,
        early,
        low,
        high,
        norm_gain.reshape(1, chans),
        norm_shift.reshape(1, chans),
        *parts,
    )

    count = kernel.shape[0] * kernel.shape[1] * kernel.shape[2] * chans
    shards_n = tms * dps
    assert count % shards_n == 0
    shard = count // shards_n
    full = shard + TILE
    keep, *sends = pl.pallas_call(
        weights_kernel,
        in_specs=[SMEM, VMEM, VMEM, VMEM],
        out_specs=[VMEM] * tms,
        out_shape=[jax.ShapeDtypeStruct((dps, full, chans), F32)] * tms,
        scratch_shapes=[
            pltpu.VMEM((chans, count), F32),
            pltpu.VMEM((tms, dps, full, chans), F32),
        ],
        compiler_params=params(40),
        name="weights",
    )(info, turned, act, bias)

    incoming = [swap(send, "tm", r + 1) for r, send in enumerate(sends)]
    own, *sends = pl.pallas_call(
        functools.partial(spread_kernel, len(incoming)),
        in_specs=[SMEM] + [VMEM] * (1 + len(incoming)),
        out_specs=[VMEM] * dps,
        out_shape=[jax.ShapeDtypeStruct((full, chans), F32)]
        + [jax.ShapeDtypeStruct((full, chans), BF16)] * (dps - 1),
        name="spread",
    )(info, keep, *incoming)

    def added(dtype, *arrays):
        return pl.pallas_call(
            add_kernel,
            in_specs=[VMEM] * len(arrays),
            out_specs=VMEM,
            out_shape=jax.ShapeDtypeStruct((full, chans), dtype),
            name="added",
        )(*arrays)

    total = added(F32, own, *[swap(send, "dp", r + 1) for r, send in enumerate(sends)])
    by = 1
    while by < spaces:
        total = added(F32 if 2 * by < spaces else BF16, total, swap(total, "space", by))
        by *= 2
    mine = [total] + [swap(total, "dp", r) for r in range(1, dps)]
    shards = {(0, r): array for r, array in enumerate(mine)}
    for q in range(1, tms):
        for r, array in enumerate(mine):
            shards[q, r] = swap(array, "tm", q)
    order = list(shards)

    def collect(info_ref, *refs):
        out_ref, sum_ref = refs[-2:]
        for (q, r), ref in zip(order, refs):
            at = (info_ref[4] ^ q) * dps + (info_ref[5] ^ r)
            out_ref[at] = ref[0:shard, :].astype(F32)
        tail = refs[0][shard : shard + TILE, :].astype(F32)
        sum_ref[...] = tail[0:1] + tail[1:2] + tail[2:3]

    grad_kernel, grad_bias = pl.pallas_call(
        collect,
        in_specs=[SMEM] + [VMEM] * len(order),
        out_specs=[VMEM, VMEM],
        out_shape=[
            jax.ShapeDtypeStruct((shards_n, shard, chans), F32),
            jax.ShapeDtypeStruct((1, chans), F32),
        ],
        name="collect",
    )(info, *[shards[key] for key in order])

    zero = jnp.zeros(kernel.shape[1:], BF16)
    taps = jnp.concatenate(
        [
            jnp.concatenate(
                [
                    kernel[f - g] if 0 <= f - g < kernel.shape[0] else zero
                    for g in range(2)
                ],
                axis=-1,
            ).reshape(-1, 2 * chans)
            for f in range(kernel.shape[0] + 1)
        ],
        axis=0,
    )
    block = 4
    outputs = []
    for t0 in range(0, frames, 2):
        outputs.append(
            pl.pallas_call(
                functools.partial(conv_kernel, t0),
                grid=(rows // block,),
                in_specs=[
                    SMEM,
                    VMEM,
                    VMEM,
                    pl.BlockSpec((1, 2, block, cols, chans), lambda y, t0=t0: (0, t0 // 2, y, 0, 0)),
                    VMEM,
                ],
                out_specs=pl.BlockSpec((1, 2, block, cols, chans), lambda y: (0, 0, y, 0, 0)),
                out_shape=jax.ShapeDtypeStruct((1, 2, rows, cols, chans), BF16),
                scratch_shapes=[pltpu.VMEM((2 * block, cols, chans), F32)],
                compiler_params=params(40),
                name="conv",
            )(info, act[t0 : t0 + 4], taps, video, conv_bias.reshape(1, chans))
        )
    output = jnp.concatenate(outputs, axis=1)
    return output, grad_kernel.reshape(kernel.shape), grad_bias.reshape(chans)


def solution(mesh):
    return jax.shard_map(
        body,
        mesh=mesh,
        in_specs=(
            P("dp", "tm", "space", None, None),
            P("dp"),
            P(),
            P(),
            P(),
            P(),
            P("dp", "tm", "space", None, None),
        ),
        out_specs=(P("dp", "tm", "space", None, None), P(), P()),
        check_vma=False,
    )
```

```python
import functools

import jax
import jax.numpy as jnp
from jax import lax
from jax.experimental import pallas as pl
from jax.experimental.pallas import tpu as pltpu
from jax.sharding import PartitionSpec as P

GROUPS = 32
TILE = 16
F32 = jnp.float32
BF16 = jnp.bfloat16
VMEM = pl.BlockSpec(memory_space=pltpu.VMEM)
SMEM = pl.BlockSpec(memory_space=pltpu.SMEM)


def params(mib):
    return pltpu.CompilerParams(vmem_limit_bytes=mib * 1024 * 1024)


def swap(array, axis, by):
    length = lax.axis_size(axis)
    assert length & (length - 1) == 0
    return lax.ppermute(array, axis, [(i, i ^ by) for i in range(length)])


def shifted(array, axis, by):
    length = lax.axis_size(axis)
    return lax.ppermute(array, axis, [(i, i + by) for i in range(length) if 0 <= i + by < length])


def group_sum(row, per):
    value = jnp.broadcast_to(row, (8, row.shape[1]))
    lane = lax.broadcasted_iota(jnp.int32, value.shape, 1)
    size = value.shape[1]
    step = 1
    while step < per:
        up = pltpu.roll(value, size - step, 1)
        down = pltpu.roll(value, step, 1)
        value = value + jnp.where((lane & step) == 0, up, down)
        step *= 2
    return value[0:1]


def merged(parts):
    count = sum(part[0:1] for part in parts)
    total = sum(part[1:2] for part in parts)
    mean = total / jnp.maximum(count, 1.0)
    squares = jnp.zeros_like(mean)
    for part in parts:
        away = part[1:2] / jnp.maximum(part[0:1], 1.0) - mean
        squares = squares + (part[2:3] + part[0:1] * (away * away))
    return count, total, mean, squares


def stats_kernel(per, before, info_ref, video_ref, out_ref, tail_ref, ends_ref, sums, squares):
    frames = pl.num_programs(0)
    t = pl.program_id(0)
    rows, cols, chans = video_ref.shape[2:]
    size = float(rows * cols * per)
    lanes = 4
    split = (cols // (8 * lanes), lanes, 8, chans)

    def add(y, acc):
        return acc + jnp.sum(video_ref[0, 0, y].astype(F32).reshape(split), axis=0)

    start = jnp.zeros((lanes, 8, chans), F32)
    acc = jnp.sum(lax.fori_loop(0, rows, add, start, unroll=4), axis=0)
    total = group_sum(jnp.sum(acc, axis=0, keepdims=True), per)
    mean = total / size

    def deviate(y, acc):
        away = video_ref[0, 0, y].astype(F32).reshape(split) - mean
        return acc + jnp.sum(away * away, axis=0)

    acc = jnp.sum(lax.fori_loop(0, rows, deviate, start, unroll=4), axis=0)
    sums[t] = jnp.broadcast_to(total, (8, chans))
    squares[t] = jnp.broadcast_to(group_sum(jnp.sum(acc, axis=0, keepdims=True), per), (8, chans))
    ends_ref[0, t] = video_ref[0, 0, rows - 1]
    ends_ref[1, t] = video_ref[0, 0, 0]

    @pl.when(t >= frames - before)
    def _():
        tail_ref[0, t - (frames - before)] = video_ref[0, 0]

    @pl.when(t == frames - 1)
    def _():
        inside = info_ref[0]
        parts = []
        for f in range(sums.shape[0]):
            keep = (f < inside).astype(F32)
            parts.append(
                jnp.concatenate(
                    [jnp.full((1, chans), size, F32), sums[f, 0:1], squares[f, 0:1]], axis=0
                )
                * keep
            )
        count, total, _, deviations = merged(parts)
        out_ref[...] = jnp.concatenate(
            [count, total, deviations, jnp.zeros((5, chans), F32)], axis=0
        )


def merge_kernel(parts_n, ends_ref, early_ref, *refs):
    parts, (out_ref, low_ref, high_ref) = refs[:parts_n], refs[parts_n:]
    count, total, _, deviations = merged([ref[...] for ref in parts])
    out_ref[...] = jnp.concatenate(
        [count, total, deviations, jnp.zeros((5, count.shape[1]), F32)], axis=0
    )
    before = early_ref.shape[1]
    for side, ref in enumerate((low_ref, high_ref)):
        ref[0:before] = early_ref[side]
        ref[before:] = ends_ref[side]


def cotangent_kernel(info_ref, cot_ref, turned_ref, bias_ref, wide):
    t = pl.program_id(0)
    rows, cols, chans = cot_ref.shape[2:]
    step = cols // TILE
    keep = (t < info_ref[0]).astype(F32)

    @pl.when(t == 0)
    def _():
        bias_ref[...] = jnp.zeros_like(bias_ref)

    def row(y, acc):
        value = cot_ref[0, 0, y].astype(F32) * keep
        slot = wide.at[y % wide.shape[0]]
        slot[...] = value
        order = jnp.concatenate(
            [slot[pl.ds(r, TILE, stride=step), :] for r in range(step)], axis=0
        )
        turned_ref[0, y] = order.T.astype(BF16)
        return acc + jnp.sum(value.reshape(cols // 8, 8, chans), axis=0)

    acc = lax.fori_loop(0, rows, row, jnp.zeros((8, chans), F32), unroll=4)
    bias_ref[0:1, :] += jnp.sum(acc, axis=0, keepdims=True)


def activate_kernel(
    parts_n, info_ref, video_ref, early_ref, low_ref, high_ref, gain_ref, shift_ref, *refs
):
    parts, out_ref, wide = refs[:parts_n], refs[parts_n], refs[parts_n + 1]
    frames, rows, cols, chans = video_ref.shape[1:]
    before = early_ref.shape[1]
    step = cols // TILE
    inside, first, has_low, has_high = info_ref[0], info_ref[1], info_ref[2], info_ref[3]
    count, _, mean, squares = merged([ref[...] for ref in parts])
    scale = 0.5 * lax.rsqrt(squares / count + 1e-05) * gain_ref[...]
    offset = 0.5 * shift_ref[...] - mean * scale
    slots = wide.shape[0]
    wide[:, 0:8, :] = jnp.zeros((slots, 8, chans), F32)
    wide[:, 8 + cols : 16 + cols, :] = jnp.zeros((slots, 8, chans), F32)

    def row(values, keep, slot, f, y):
        half = values.astype(F32) * (scale * keep) + offset * keep
        wide[slot, 8 : 8 + cols, :] = half + half * jnp.tanh(half)
        for r in range(-1, step + 1):
            out_ref[f, y, r + 1] = wide[slot, pl.ds(8 + r, TILE, stride=step), :].astype(BF16)

    for f in range(frames + before):
        local = f - before
        ok = (local < inside) & (first + local >= 0)
        keep = ok.astype(F32)
        source = early_ref.at[0, f] if local < 0 else video_ref.at[0, local]

        def inner(y, carry, source=source, keep=keep, f=f):
            row(source[y], keep, y % slots, f, y + 1)
            return carry

        lax.fori_loop(0, rows, inner, 0, unroll=4)
        row(low_ref[f], keep * has_low.astype(F32), 0, f, 0)
        row(high_ref[f], keep * has_high.astype(F32), 1, f, rows + 1)


def packed(value):
    per = value.shape[0] - TILE
    total = value[per : per + 1] + value[per + 1 : per + 2] + value[per + 2 : per + 3]
    top = total.astype(BF16).astype(F32)
    mid = (total - top).astype(BF16).astype(F32)
    rest = total - top - mid
    tail = jnp.concatenate([top, mid, rest, jnp.zeros((TILE - 3, value.shape[1]), F32)], axis=0)
    return jnp.concatenate([value[:per].astype(BF16), tail.astype(BF16)], axis=0)


def weights_kernel(info_ref, turned_ref, act_ref, bias_ref, keep_ref, *refs):
    send_refs, acc = refs[:-2], refs[-2:]
    acc, shards = acc
    frames, rows = turned_ref.shape[:2]
    chans = turned_ref.shape[2]
    k = turned_ref.shape[3]
    step = act_ref.shape[2] - 2
    taps = [(kt, ky, kx) for kt in range(3) for ky in range(3) for kx in range(3)]
    pair = 2

    def frame(t, carry):
        left = jnp.concatenate([turned_ref[t, y] for y in range(rows)], axis=1)
        for j in range(0, len(taps), pair):
            chosen = taps[j : j + pair]
            right = jnp.concatenate(
                [
                    act_ref[t + kt, ky : ky + rows, kx : kx + step].reshape(rows * k, chans)
                    for kt, ky, kx in chosen
                ],
                axis=1,
            )
            product = jnp.dot(left, right, preferred_element_type=F32)
            where = slice(j * chans, (j + len(chosen)) * chans)
            acc[:, where] = jnp.where(t == 0, product, acc[:, where] + product)
        return carry

    lax.fori_loop(0, frames, frame, 0)
    tms, dps, per = shards.shape[:3]
    per -= TILE
    for tap in range(len(taps)):
        block = acc[:, tap * chans : (tap + 1) * chans].T
        done = 0
        while done < chans:
            shard, at = divmod(tap * chans + done, per)
            take = min(chans - done, per - at)
            shards[shard // dps, shard % dps, at : at + take, :] = block[done : done + take]
            done += take
    tail = jnp.concatenate([bias_ref[0:1], jnp.zeros((TILE - 1, chans), F32)], axis=0)
    for i in range(tms):
        for j in range(dps):
            shards[i, j, per : per + TILE, :] = tail
    me = info_ref[4]
    keep_ref[...] = shards[me]
    for r in range(1, tms):
        send_refs[r - 1][...] = shards[me ^ r]


def spread_kernel(count, info_ref, after_ref, keep_ref, *refs):
    incoming, own_ref, send_refs = refs[:count], refs[count], refs[count + 1 :]
    me = info_ref[5]
    for r in range(len(send_refs) + 1):
        value = keep_ref[me ^ r]
        for ref in incoming:
            value = value + ref[me ^ r]
        if r == 0:
            own_ref[...] = value
        else:
            send_refs[r - 1][...] = packed(value)


def add_kernel(after_ref, *refs):
    value = refs[0][...].astype(F32)
    for ref in refs[1:-1]:
        value = value + ref[...].astype(F32)
    refs[-1][...] = packed(value) if refs[-1].dtype == BF16 else value


def conv_kernel(t0, y0, info_ref, after_ref, act_ref, kernel_ref, video_ref, bias_ref, *refs):
    out_ref, token_ref, wide = refs[-3:]
    frames_out, rows, cols, chans = out_ref.shape[1:]
    kts, kys, kxs = kernel_ref.shape[:3]
    step = cols // TILE
    start = y0 + pl.program_id(0) * rows
    taps = [(ky, kx) for ky in range(kys) for kx in range(kxs)]
    used = [(f, ky, kx) for f in range(frames_out + kts - 1) for ky, kx in taps]
    left = jnp.concatenate(
        [
            act_ref[t0 + f, pl.ds(start + ky, rows), kx : kx + step].reshape(rows * cols, chans)
            for f, ky, kx in used
        ],
        axis=1,
    )
    zero = jnp.zeros((chans, chans), BF16)
    right = jnp.concatenate(
        [
            jnp.concatenate(
                [
                    kernel_ref[f - g, ky, kx] if 0 <= f - g < kts else zero
                    for g in range(frames_out)
                ],
                axis=1,
            )
            for f, ky, kx in used
        ],
        axis=0,
    )
    result = jnp.dot(left, right, preferred_element_type=F32)
    for f in range(frames_out):
        keep = (t0 + f < info_ref[0]).astype(F32)
        for y in range(rows):
            slot = f * rows + y
            for r in range(step):
                at = y * cols + r * TILE
                wide[slot, pl.ds(r, TILE, stride=step), :] = result[
                    at : at + TILE, f * chans : (f + 1) * chans
                ]
            value = video_ref[0, f, y].astype(F32) + wide[slot] + bias_ref[...]
            out_ref[0, f, y] = (value * keep).astype(BF16)
    token_ref[...] = jnp.zeros_like(token_ref)


def body(video, lengths, norm_gain, norm_shift, kernel, conv_bias, cotangent):
    frames, rows, cols, chans = video.shape[1:]
    per = chans // GROUPS
    step = cols // TILE
    before = kernel.shape[0] - 1
    tms, dps, spaces = (lax.axis_size(axis) for axis in ("tm", "dp", "space"))
    tm, dp, space = (lax.axis_index(axis) for axis in ("tm", "dp", "space"))
    first = tm * frames
    inside = jnp.clip(lengths[0] - first, -before, frames)
    info = jnp.stack(
        [
            inside,
            first,
            (space > 0).astype(jnp.int32),
            (space < spaces - 1).astype(jnp.int32),
            tm,
            dp,
        ]
    ).astype(jnp.int32)

    frame_spec = pl.BlockSpec((1, 1, rows, cols, chans), lambda t: (0, t, 0, 0, 0))
    stats, tail, ends = pl.pallas_call(
        functools.partial(stats_kernel, per, before),
        grid=(frames,),
        in_specs=[SMEM, frame_spec],
        out_specs=[
            pl.BlockSpec((8, chans), lambda t: (0, 0)),
            pl.BlockSpec((1, before, rows, cols, chans), lambda t: (0, 0, 0, 0, 0)),
            pl.BlockSpec((2, frames, cols, chans), lambda t: (0, 0, 0, 0)),
        ],
        out_shape=[
            jax.ShapeDtypeStruct((8, chans), F32),
            jax.ShapeDtypeStruct((1, before, rows, cols, chans), BF16),
            jax.ShapeDtypeStruct((2, frames, cols, chans), BF16),
        ],
        scratch_shapes=[pltpu.VMEM((frames, 8, chans), F32), pltpu.VMEM((frames, 8, chans), F32)],
        compiler_params=params(8),
        name="stats",
    )(info, video)
    gathered = [stats] + [swap(stats, "tm", r) for r in range(1, tms)]
    early_ends = shifted(ends[:, frames - before :], "tm", 1)
    early = shifted(tail, "tm", 1)
    border = jax.ShapeDtypeStruct((before + frames, cols, chans), BF16)
    stats, edge_low, edge_high = pl.pallas_call(
        functools.partial(merge_kernel, tms),
        in_specs=[VMEM] * (2 + tms),
        out_specs=[VMEM] * 3,
        out_shape=[jax.ShapeDtypeStruct((8, chans), F32), border, border],
        compiler_params=params(2),
        name="merge",
    )(ends, early_ends, *gathered)
    parts = [stats] + [swap(stats, "space", r) for r in range(1, spaces)]
    low = shifted(edge_low, "space", 1)
    high = shifted(edge_high, "space", -1)

    turned, bias = pl.pallas_call(
        cotangent_kernel,
        grid=(frames,),
        in_specs=[SMEM, frame_spec],
        out_specs=[
            pl.BlockSpec((1, rows, chans, cols), lambda t: (t, 0, 0, 0)),
            pl.BlockSpec((8, chans), lambda t: (0, 0)),
        ],
        out_shape=[
            jax.ShapeDtypeStruct((frames, rows, chans, cols), BF16),
            jax.ShapeDtypeStruct((8, chans), F32),
        ],
        scratch_shapes=[pltpu.VMEM((4, cols, chans), F32)],
        compiler_params=params(8),
        name="cotangent",
    )(info, cotangent)

    act = pl.pallas_call(
        functools.partial(activate_kernel, spaces),
        in_specs=[SMEM] + [VMEM] * (6 + spaces),
        out_specs=VMEM,
        out_shape=jax.ShapeDtypeStruct(
            (frames + before, rows + 2, step + 2, TILE, chans), BF16
        ),
        scratch_shapes=[pltpu.VMEM((4, cols + 16, chans), F32)],
        compiler_params=params(8),
        name="activate",
    )(
        info,
        video,
        early,
        low,
        high,
        norm_gain.reshape(1, chans),
        norm_shift.reshape(1, chans),
        *parts,
    )

    count = kernel.shape[0] * kernel.shape[1] * kernel.shape[2] * chans
    shards_n = tms * dps
    assert count % shards_n == 0
    shard = count // shards_n
    full = shard + TILE
    keep, *sends = pl.pallas_call(
        weights_kernel,
        in_specs=[SMEM, VMEM, VMEM, VMEM],
        out_specs=[VMEM] * tms,
        out_shape=[jax.ShapeDtypeStruct((dps, full, chans), F32)] * tms,
        scratch_shapes=[
            pltpu.VMEM((chans, count), F32),
            pltpu.VMEM((tms, dps, full, chans), F32),
        ],
        compiler_params=params(16),
        name="weights",
    )(info, turned, act, bias)

    ANY = pl.BlockSpec(memory_space=pl.ANY)
    block = 4
    output = None
    half = rows // 2

    def conv(after, output, t0, y0):
        given = [] if output is None else [output]
        where = lambda y: (0, t0 // 2, y0 // block + y, 0, 0)
        return pl.pallas_call(
            functools.partial(conv_kernel, t0, y0),
            grid=(half // block,),
            in_specs=[
                SMEM,
                ANY,
                VMEM,
                VMEM,
                pl.BlockSpec((1, 2, block, cols, chans), where),
                VMEM,
            ]
            + [ANY] * len(given),
            out_specs=[
                pl.BlockSpec((1, 2, block, cols, chans), where),
                pl.BlockSpec((8, chans), lambda y: (0, 0)),
            ],
            out_shape=[
                jax.ShapeDtypeStruct(video.shape, BF16),
                jax.ShapeDtypeStruct((8, chans), F32),
            ],
            scratch_shapes=[pltpu.VMEM((2 * block, cols, chans), F32)],
            input_output_aliases={6: 0} if given else {},
            compiler_params=params(12),
            name="conv",
        )(info, after, act, kernel, video, conv_bias.reshape(1, chans), *given)

    pieces = [(t0, y0) for t0 in range(0, frames, 2) for y0 in range(0, rows, half)]

    def cover(after, output):
        if not pieces:
            return output, after
        return conv(after, output, *pieces.pop(0))

    incoming = [swap(send, "tm", r + 1) for r, send in enumerate(sends)]
    output, token = cover(keep, output)
    own, *sends = pl.pallas_call(
        functools.partial(spread_kernel, len(incoming)),
        in_specs=[SMEM, ANY] + [VMEM] * (1 + len(incoming)),
        out_specs=[VMEM] * dps,
        out_shape=[jax.ShapeDtypeStruct((full, chans), F32)]
        + [jax.ShapeDtypeStruct((full, chans), BF16)] * (dps - 1),
        compiler_params=params(4),
        name="spread",
    )(info, token, keep, *incoming)

    def added(dtype, after, *arrays):
        return pl.pallas_call(
            add_kernel,
            in_specs=[ANY] + [VMEM] * len(arrays),
            out_specs=VMEM,
            out_shape=jax.ShapeDtypeStruct((full, chans), dtype),
            compiler_params=params(2),
            name="added",
        )(after, *arrays)

    incoming = [swap(send, "dp", r + 1) for r, send in enumerate(sends)]
    output, token = cover(own, output)
    total = added(F32, token, own, *incoming)
    by = 1
    while by < spaces:
        other = swap(total, "space", by)
        output, token = cover(total, output)
        by *= 2
        total = added(F32 if by < spaces else BF16, token, total, other)
    while pieces:
        output, token = cover(total, output)
    mine = [total] + [swap(total, "dp", r) for r in range(1, dps)]
    shards = {(0, r): array for r, array in enumerate(mine)}
    for q in range(1, tms):
        for r, array in enumerate(mine):
            shards[q, r] = swap(array, "tm", q)
    order = list(shards)

    def collect(info_ref, *refs):
        out_ref, sum_ref = refs[-2:]
        for (q, r), ref in zip(order, refs):
            at = (info_ref[4] ^ q) * dps + (info_ref[5] ^ r)
            out_ref[at] = ref[0:shard, :].astype(F32)
        tail = refs[0][shard : shard + TILE, :].astype(F32)
        sum_ref[...] = tail[0:1] + tail[1:2] + tail[2:3]

    grad_kernel, grad_bias = pl.pallas_call(
        collect,
        in_specs=[SMEM] + [VMEM] * len(order),
        out_specs=[VMEM, VMEM],
        out_shape=[
            jax.ShapeDtypeStruct((shards_n, shard, chans), F32),
            jax.ShapeDtypeStruct((1, chans), F32),
        ],
        compiler_params=params(4),
        name="collect",
    )(info, *[shards[key] for key in order])

    return output, grad_kernel.reshape(kernel.shape), grad_bias.reshape(chans)


def solution(mesh):
    return jax.shard_map(
        body,
        mesh=mesh,
        in_specs=(
            P("dp", "tm", "space", None, None),
            P("dp"),
            P(),
            P(),
            P(),
            P(),
            P("dp", "tm", "space", None, None),
        ),
        out_specs=(P("dp", "tm", "space", None, None), P(), P()),
        check_vma=False,
    )
```

```python
import functools

import jax
import jax.numpy as jnp
from jax import lax
from jax.experimental import pallas as pl
from jax.experimental.pallas import tpu as pltpu
from jax.sharding import PartitionSpec as P


GROUPS = 32
TILE = 16
F32 = jnp.float32
BF16 = jnp.bfloat16
VMEM = pl.BlockSpec(memory_space=pltpu.VMEM)
ANY = pl.BlockSpec(memory_space=pl.ANY)
SMEM = pl.BlockSpec(memory_space=pltpu.SMEM)


def params(mib):
    return pltpu.CompilerParams(vmem_limit_bytes=mib * 1024 * 1024)


def swap(array, axis, by):
    length = lax.axis_size(axis)
    assert length & (length - 1) == 0
    return lax.ppermute(array, axis, [(i, i ^ by) for i in range(length)])


def shifted(array, axis, by):
    length = lax.axis_size(axis)
    return lax.ppermute(array, axis, [(i, i + by) for i in range(length) if 0 <= i + by < length])


def group_sum(row, per):
    value = jnp.broadcast_to(row, (8, row.shape[1]))
    lane = lax.broadcasted_iota(jnp.int32, value.shape, 1)
    size = value.shape[1]
    step = 1
    while step < per:
        up = pltpu.roll(value, size - step, 1)
        down = pltpu.roll(value, step, 1)
        value = value + jnp.where((lane & step) == 0, up, down)
        step *= 2
    return value[0:1]


def merged(parts):
    count = sum(part[0:1] for part in parts)
    total = sum(part[1:2] for part in parts)
    mean = total / jnp.maximum(count, 1.0)
    squares = jnp.zeros_like(mean)
    for part in parts:
        away = part[1:2] / jnp.maximum(part[0:1], 1.0) - mean
        squares = squares + (part[2:3] + part[0:1] * (away * away))
    return count, total, mean, squares


def stats_kernel(per, before, info_ref, video_ref, out_ref, tail_ref, ends_ref, sums, squares):
    frames = pl.num_programs(0)
    t = pl.program_id(0)
    rows, cols, chans = video_ref.shape[2:]
    size = float(rows * cols * per)
    lanes = 4
    split = (cols // (8 * lanes), lanes, 8, chans)

    def add(y, acc):
        return acc + jnp.sum(video_ref[0, 0, y].astype(F32).reshape(split), axis=0)

    start = jnp.zeros((lanes, 8, chans), F32)
    acc = jnp.sum(lax.fori_loop(0, rows, add, start, unroll=4), axis=0)
    total = group_sum(jnp.sum(acc, axis=0, keepdims=True), per)
    mean = total / size

    def deviate(y, acc):
        away = video_ref[0, 0, y].astype(F32).reshape(split) - mean
        return acc + jnp.sum(away * away, axis=0)

    acc = jnp.sum(lax.fori_loop(0, rows, deviate, start, unroll=4), axis=0)
    sums[t] = jnp.broadcast_to(total, (8, chans))
    squares[t] = jnp.broadcast_to(group_sum(jnp.sum(acc, axis=0, keepdims=True), per), (8, chans))
    ends_ref[0, t] = video_ref[0, 0, rows - 1]
    ends_ref[1, t] = video_ref[0, 0, 0]

    @pl.when(t >= frames - before)
    def _():
        tail_ref[0, t - (frames - before)] = video_ref[0, 0]

    @pl.when(t == frames - 1)
    def _():
        inside = info_ref[0]
        parts = []
        for f in range(sums.shape[0]):
            keep = (f < inside).astype(F32)
            parts.append(
                jnp.concatenate(
                    [jnp.full((1, chans), size, F32), sums[f, 0:1], squares[f, 0:1]], axis=0
                )
                * keep
            )
        count, total, _, deviations = merged(parts)
        out_ref[...] = jnp.concatenate(
            [count, total, deviations, jnp.zeros((5, chans), F32)], axis=0
        )


def merge_kernel(parts_n, ends_ref, early_ref, *refs):
    parts, (out_ref, low_ref, high_ref) = refs[:parts_n], refs[parts_n:]
    count, total, _, deviations = merged([ref[...] for ref in parts])
    out_ref[...] = jnp.concatenate(
        [count, total, deviations, jnp.zeros((5, count.shape[1]), F32)], axis=0
    )
    before = early_ref.shape[1]
    for side, ref in enumerate((low_ref, high_ref)):
        ref[0:before] = early_ref[side]
        ref[before:] = ends_ref[side]


def cotangent_kernel(info_ref, cot_ref, turned_ref, bias_ref, wide):
    t = pl.program_id(0)
    rows, cols, chans = cot_ref.shape[2:]
    step = cols // TILE
    keep = (t < info_ref[0]).astype(F32)

    @pl.when(t == 0)
    def _():
        bias_ref[...] = jnp.zeros_like(bias_ref)

    def row(y, acc):
        value = cot_ref[0, 0, y].astype(F32) * keep
        slot = wide.at[y % wide.shape[0]]
        slot[...] = value
        order = jnp.concatenate(
            [slot[pl.ds(r, TILE, stride=step), :] for r in range(step)], axis=0
        )
        turned_ref[0, y] = order.T.astype(BF16)
        return acc + jnp.sum(value.reshape(cols // 8, 8, chans), axis=0)

    acc = lax.fori_loop(0, rows, row, jnp.zeros((8, chans), F32), unroll=4)
    bias_ref[0:1, :] += jnp.sum(acc, axis=0, keepdims=True)


def activate_kernel(
    parts_n, info_ref, video_ref, early_ref, low_ref, high_ref, gain_ref, shift_ref, *refs
):
    parts, out_ref, wide = refs[:parts_n], refs[parts_n], refs[parts_n + 1]
    frames, rows, cols, chans = video_ref.shape[1:]
    before = early_ref.shape[1]
    step = cols // TILE
    inside, first, has_low, has_high = info_ref[0], info_ref[1], info_ref[2], info_ref[3]
    count, _, mean, squares = merged([ref[...] for ref in parts])
    scale = 0.5 * lax.rsqrt(squares / count + 1e-05) * gain_ref[...]
    offset = 0.5 * shift_ref[...] - mean * scale
    slots = wide.shape[0]
    wide[:, 0:8, :] = jnp.zeros((slots, 8, chans), F32)
    wide[:, 8 + cols : 16 + cols, :] = jnp.zeros((slots, 8, chans), F32)

    def row(values, keep, slot, f, y):
        half = values.astype(F32) * (scale * keep) + offset * keep
        wide[slot, 8 : 8 + cols, :] = half + half * jnp.tanh(half)
        for r in range(-1, step + 1):
            out_ref[f, y, r + 1] = wide[slot, pl.ds(8 + r, TILE, stride=step), :].astype(BF16)

    for f in range(frames + before):
        local = f - before
        ok = (local < inside) & (first + local >= 0)
        keep = ok.astype(F32)
        source = early_ref.at[0, f] if local < 0 else video_ref.at[0, local]

        def inner(y, carry, source=source, keep=keep, f=f):
            row(source[y], keep, y % slots, f, y + 1)
            return carry

        lax.fori_loop(0, rows, inner, 0, unroll=4)
        row(low_ref[f], keep * has_low.astype(F32), 0, f, 0)
        row(high_ref[f], keep * has_high.astype(F32), 1, f, rows + 1)


def packed(value):
    per = value.shape[0] - TILE
    total = value[per : per + 1] + value[per + 1 : per + 2] + value[per + 2 : per + 3]
    top = total.astype(BF16).astype(F32)
    mid = (total - top).astype(BF16).astype(F32)
    rest = total - top - mid
    tail = jnp.concatenate([top, mid, rest, jnp.zeros((TILE - 3, value.shape[1]), F32)], axis=0)
    return jnp.concatenate([value[:per].astype(BF16), tail.astype(BF16)], axis=0)


def weights_kernel(info_ref, turned_ref, act_ref, bias_ref, keep_ref, *refs):
    send_refs, acc = refs[:-2], refs[-2:]
    acc, shards = acc
    frames, rows = turned_ref.shape[:2]
    chans = turned_ref.shape[2]
    k = turned_ref.shape[3]
    step = act_ref.shape[2] - 2
    taps = [(kt, ky, kx) for kt in range(3) for ky in range(3) for kx in range(3)]
    pair = 2

    def frame(t, carry):
        left = jnp.concatenate([turned_ref[t, y] for y in range(rows)], axis=1)
        for j in range(0, len(taps), pair):
            chosen = taps[j : j + pair]
            right = jnp.concatenate(
                [
                    act_ref[t + kt, ky : ky + rows, kx : kx + step].reshape(rows * k, chans)
                    for kt, ky, kx in chosen
                ],
                axis=1,
            )
            product = jnp.dot(left, right, preferred_element_type=F32)
            where = slice(j * chans, (j + len(chosen)) * chans)
            acc[:, where] = jnp.where(t == 0, product, acc[:, where] + product)
        return carry

    lax.fori_loop(0, frames, frame, 0)
    tms, dps, per = shards.shape[:3]
    per -= TILE
    for tap in range(len(taps)):
        block = acc[:, tap * chans : (tap + 1) * chans].T
        done = 0
        while done < chans:
            shard, at = divmod(tap * chans + done, per)
            take = min(chans - done, per - at)
            shards[shard // dps, shard % dps, at : at + take, :] = block[done : done + take]
            done += take
    tail = jnp.concatenate([bias_ref[0:1], jnp.zeros((TILE - 1, chans), F32)], axis=0)
    for i in range(tms):
        for j in range(dps):
            shards[i, j, per : per + TILE, :] = tail
    me = info_ref[4]
    keep_ref[...] = shards[me]
    for r in range(1, tms):
        send_refs[r - 1][...] = shards[me ^ r]


def spread_kernel(count, info_ref, after_ref, keep_ref, *refs):
    incoming, own_ref, send_refs = refs[:count], refs[count], refs[count + 1 :]
    me = info_ref[5]
    for r in range(len(send_refs) + 1):
        value = keep_ref[me ^ r]
        for ref in incoming:
            value = value + ref[me ^ r]
        if r == 0:
            own_ref[...] = value
        else:
            send_refs[r - 1][...] = packed(value)


def add_kernel(after_ref, *refs):
    value = refs[0][...].astype(F32)
    for ref in refs[1:-1]:
        value = value + ref[...].astype(F32)
    refs[-1][...] = packed(value) if refs[-1].dtype == BF16 else value


def taps_kernel(after_ref, kernel_ref, out_ref):
    kts, kys, kxs, chans = kernel_ref.shape[:4]
    pair = out_ref.shape[1] // chans
    zero = jnp.zeros((kys * kxs * chans, chans), BF16)
    span = kys * kxs * chans
    for f in range(kts + pair - 1):
        for g in range(pair):
            if 0 <= f - g < kts:
                value = kernel_ref[f - g].reshape(span, chans)
            else:
                value = zero
            out_ref[f * span : (f + 1) * span, g * chans : (g + 1) * chans] = value


def conv_kernel(t0, y0, info_ref, after_ref, act_ref, taps_ref, video_ref, bias_ref, *refs):
    out_ref, token_ref, wide = refs[-3:]
    frames_out, rows, cols, chans = out_ref.shape[1:]
    step = cols // TILE
    start = y0 + pl.program_id(0) * rows
    used = [
        (f, ky, kx)
        for f in range(taps_ref.shape[0] // (9 * chans))
        for ky in range(3)
        for kx in range(3)
    ]
    left = jnp.concatenate(
        [
            act_ref[t0 + f, pl.ds(start + ky, rows), kx : kx + step].reshape(rows * cols, chans)
            for f, ky, kx in used
        ],
        axis=1,
    )
    result = jnp.dot(left, taps_ref[...], preferred_element_type=F32)
    for f in range(frames_out):
        keep = (t0 + f < info_ref[0]).astype(F32)
        for y in range(rows):
            slot = f * rows + y
            for r in range(step):
                at = y * cols + r * TILE
                wide[slot, pl.ds(r, TILE, stride=step), :] = result[
                    at : at + TILE, f * chans : (f + 1) * chans
                ]
            value = video_ref[0, f, y].astype(F32) + wide[slot] + bias_ref[...]
            out_ref[0, f, y] = (value * keep).astype(BF16)
    token_ref[...] = jnp.zeros_like(token_ref)


def step_of(video, lengths, norm_gain, norm_shift, kernel, conv_bias, cotangent):
    frames, rows, cols, chans = video.shape[1:]
    per = chans // GROUPS
    step = cols // TILE
    before = kernel.shape[0] - 1
    tms, dps, spaces = (lax.axis_size(axis) for axis in ("tm", "dp", "space"))
    tm, dp, space = (lax.axis_index(axis) for axis in ("tm", "dp", "space"))
    first = tm * frames
    inside = jnp.clip(lengths[0] - first, -before, frames)
    info = jnp.stack(
        [
            inside,
            first,
            (space > 0).astype(jnp.int32),
            (space < spaces - 1).astype(jnp.int32),
            tm,
            dp,
        ]
    ).astype(jnp.int32)

    frame_spec = pl.BlockSpec((1, 1, rows, cols, chans), lambda t: (0, t, 0, 0, 0))
    stats, tail, ends = pl.pallas_call(
        functools.partial(stats_kernel, per, before),
        grid=(frames,),
        in_specs=[SMEM, frame_spec],
        out_specs=[
            pl.BlockSpec((8, chans), lambda t: (0, 0)),
            pl.BlockSpec((1, before, rows, cols, chans), lambda t: (0, 0, 0, 0, 0)),
            pl.BlockSpec((2, frames, cols, chans), lambda t: (0, 0, 0, 0)),
        ],
        out_shape=[
            jax.ShapeDtypeStruct((8, chans), F32),
            jax.ShapeDtypeStruct((1, before, rows, cols, chans), BF16),
            jax.ShapeDtypeStruct((2, frames, cols, chans), BF16),
        ],
        scratch_shapes=[pltpu.VMEM((frames, 8, chans), F32), pltpu.VMEM((frames, 8, chans), F32)],
        compiler_params=params(8),
        name="stats",
    )(info, pltpu.with_memory_space_constraint(video, pltpu.HBM))
    gathered = [stats] + [swap(stats, "tm", r) for r in range(1, tms)]
    early_ends = shifted(ends[:, frames - before :], "tm", 1)
    early = shifted(tail, "tm", 1)
    border = jax.ShapeDtypeStruct((before + frames, cols, chans), BF16)
    stats, edge_low, edge_high = pl.pallas_call(
        functools.partial(merge_kernel, tms),
        in_specs=[VMEM] * (2 + tms),
        out_specs=[VMEM] * 3,
        out_shape=[jax.ShapeDtypeStruct((8, chans), F32), border, border],
        compiler_params=params(2),
        name="merge",
    )(ends, early_ends, *gathered)
    parts = [stats] + [swap(stats, "space", r) for r in range(1, spaces)]
    low = shifted(edge_low, "space", 1)
    high = shifted(edge_high, "space", -1)
    pair = 2
    taps = pl.pallas_call(
        taps_kernel,
        in_specs=[ANY, VMEM],
        out_specs=VMEM,
        out_shape=jax.ShapeDtypeStruct(
            ((kernel.shape[0] + pair - 1) * 9 * chans, pair * chans), BF16
        ),
        compiler_params=params(2),
        name="taps",
    )(ends, kernel)

    turned, bias = pl.pallas_call(
        cotangent_kernel,
        grid=(frames,),
        in_specs=[SMEM, frame_spec],
        out_specs=[
            pl.BlockSpec((1, rows, chans, cols), lambda t: (t, 0, 0, 0)),
            pl.BlockSpec((8, chans), lambda t: (0, 0)),
        ],
        out_shape=[
            jax.ShapeDtypeStruct((frames, rows, chans, cols), BF16),
            jax.ShapeDtypeStruct((8, chans), F32),
        ],
        scratch_shapes=[pltpu.VMEM((4, cols, chans), F32)],
        compiler_params=params(8),
        name="cotangent",
    )(info, pltpu.with_memory_space_constraint(cotangent, pltpu.HBM))

    act = pl.pallas_call(
        functools.partial(activate_kernel, spaces),
        in_specs=[SMEM] + [VMEM] * (6 + spaces),
        out_specs=VMEM,
        out_shape=jax.ShapeDtypeStruct(
            (frames + before, rows + 2, step + 2, TILE, chans), BF16
        ),
        scratch_shapes=[pltpu.VMEM((4, cols + 16, chans), F32)],
        compiler_params=params(8),
        name="activate",
    )(
        info,
        video,
        early,
        low,
        high,
        norm_gain.reshape(1, chans),
        norm_shift.reshape(1, chans),
        *parts,
    )

    count = kernel.shape[0] * kernel.shape[1] * kernel.shape[2] * chans
    shards_n = tms * dps
    assert count % shards_n == 0
    shard = count // shards_n
    full = shard + TILE
    keep, *sends = pl.pallas_call(
        weights_kernel,
        in_specs=[SMEM, VMEM, VMEM, VMEM],
        out_specs=[VMEM] * tms,
        out_shape=[jax.ShapeDtypeStruct((dps, full, chans), F32)] * tms,
        scratch_shapes=[
            pltpu.VMEM((chans, count), F32),
            pltpu.VMEM((tms, dps, full, chans), F32),
        ],
        compiler_params=params(16),
        name="weights",
    )(info, turned, act, bias)

    block = 4
    output = None
    half = block

    def conv(after, output, t0, y0):
        given = [] if output is None else [output]
        where = lambda y: (0, t0 // 2, y0 // block + y, 0, 0)
        return pl.pallas_call(
            functools.partial(conv_kernel, t0, y0),
            grid=(half // block,),
            in_specs=[
                SMEM,
                ANY,
                VMEM,
                VMEM,
                pl.BlockSpec((1, 2, block, cols, chans), where),
                VMEM,
            ]
            + [ANY] * len(given),
            out_specs=[
                pl.BlockSpec((1, 2, block, cols, chans), where),
                pl.BlockSpec((8, chans), lambda y: (0, 0)),
            ],
            out_shape=[
                jax.ShapeDtypeStruct(video.shape, BF16),
                jax.ShapeDtypeStruct((8, chans), F32),
            ],
            scratch_shapes=[pltpu.VMEM((2 * block, cols, chans), F32)],
            input_output_aliases={6: 0} if given else {},
            compiler_params=params(12),
            name="conv",
        )(info, after, act, taps, video, conv_bias.reshape(1, chans), *given)

    pieces = [(t0, y0) for t0 in range(0, frames, 2) for y0 in range(0, rows, half)]

    def cover(after, output, number):
        for _ in range(min(number, len(pieces))):
            output, after = conv(after, output, *pieces.pop(0))
        return output, after

    incoming = [swap(send, "tm", r + 1) for r, send in enumerate(sends)]
    output, token = cover(keep, output, 2)
    own, *sends = pl.pallas_call(
        functools.partial(spread_kernel, len(incoming)),
        in_specs=[SMEM, ANY] + [VMEM] * (1 + len(incoming)),
        out_specs=[VMEM] * dps,
        out_shape=[jax.ShapeDtypeStruct((full, chans), F32)]
        + [jax.ShapeDtypeStruct((full, chans), BF16)] * (dps - 1),
        compiler_params=params(4),
        name="spread",
    )(info, token, keep, *incoming)

    def added(dtype, after, *arrays):
        return pl.pallas_call(
            add_kernel,
            in_specs=[ANY] + [VMEM] * len(arrays),
            out_specs=VMEM,
            out_shape=jax.ShapeDtypeStruct((full, chans), dtype),
            compiler_params=params(2),
            name="added",
        )(after, *arrays)

    incoming = [swap(send, "dp", r + 1) for r, send in enumerate(sends)]
    output, token = cover(own, output, 1)
    total = added(F32 if spaces > 2 else BF16, token, own, *incoming)
    by = 1
    while by < spaces:
        other = swap(total, "space", by)
        output, token = cover(total, output, 2)
        by *= 2
        total = added(F32 if 2 * by < spaces else BF16, token, total, other)
    mine = [total] + [swap(total, "dp", r) for r in range(1, dps)]
    output, token = cover(total, output, len(pieces))
    shards = {(0, r): array for r, array in enumerate(mine)}
    for q in range(1, tms):
        for r, array in enumerate(mine):
            shards[q, r] = swap(array, "tm", q)
    order = list(shards)

    def collect(info_ref, *refs):
        out_ref, sum_ref = refs[-2:]
        for (q, r), ref in zip(order, refs):
            at = (info_ref[4] ^ q) * dps + (info_ref[5] ^ r)
            out_ref[at] = ref[0:shard, :].astype(F32)
        tail = refs[0][shard : shard + TILE, :].astype(F32)
        sum_ref[...] = tail[0:1] + tail[1:2] + tail[2:3]

    grad_kernel, grad_bias = pl.pallas_call(
        collect,
        in_specs=[SMEM] + [VMEM] * len(order),
        out_specs=[VMEM, VMEM],
        out_shape=[
            jax.ShapeDtypeStruct((shards_n, shard, chans), F32),
            jax.ShapeDtypeStruct((1, chans), F32),
        ],
        compiler_params=params(4),
        name="collect",
    )(info, *[shards[key] for key in order])

    return output, grad_kernel.reshape(kernel.shape), grad_bias.reshape(chans)


def solution(mesh):
    return jax.shard_map(
        step_of,
        mesh=mesh,
        in_specs=(
            P("dp", "tm", "space", None, None),
            P("dp"),
            P(),
            P(),
            P(),
            P(),
            P("dp", "tm", "space", None, None),
        ),
        out_specs=(P("dp", "tm", "space", None, None), P(), P()),
        check_vma=False,
    )
```

```python
import functools

import jax
import jax.numpy as jnp
from jax import lax
from jax.experimental import pallas as pl
from jax.experimental.pallas import tpu as pltpu
from jax.sharding import PartitionSpec as P


GROUPS = 32
TILE = 16
F32 = jnp.float32
BF16 = jnp.bfloat16
VMEM = pl.BlockSpec(memory_space=pltpu.VMEM)
ANY = pl.BlockSpec(memory_space=pl.ANY)
SMEM = pl.BlockSpec(memory_space=pltpu.SMEM)


def params(mib):
    return pltpu.CompilerParams(vmem_limit_bytes=mib * 1024 * 1024)


def swap(array, axis, by):
    length = lax.axis_size(axis)
    assert length & (length - 1) == 0
    return lax.ppermute(array, axis, [(i, i ^ by) for i in range(length)])


def shifted(array, axis, by):
    length = lax.axis_size(axis)
    return lax.ppermute(array, axis, [(i, i + by) for i in range(length) if 0 <= i + by < length])


def group_sum(row, per):
    value = jnp.broadcast_to(row, (8, row.shape[1]))
    lane = lax.broadcasted_iota(jnp.int32, value.shape, 1)
    size = value.shape[1]
    step = 1
    while step < per:
        up = pltpu.roll(value, size - step, 1)
        down = pltpu.roll(value, step, 1)
        value = value + jnp.where((lane & step) == 0, up, down)
        step *= 2
    return value[0:1]


def merged(parts):
    count = sum(part[0:1] for part in parts)
    total = sum(part[1:2] for part in parts)
    mean = total / jnp.maximum(count, 1.0)
    squares = jnp.zeros_like(mean)
    for part in parts:
        away = part[1:2] / jnp.maximum(part[0:1], 1.0) - mean
        squares = squares + (part[2:3] + part[0:1] * (away * away))
    return count, total, mean, squares


def stats_kernel(per, before, info_ref, video_ref, out_ref, tail_ref, ends_ref, sums, squares):
    frames = pl.num_programs(0)
    t = pl.program_id(0)
    rows, cols, chans = video_ref.shape[2:]
    size = float(rows * cols * per)
    lanes = 4
    split = (cols // (8 * lanes), lanes, 8, chans)

    def add(y, acc):
        return acc + jnp.sum(video_ref[0, 0, y].astype(F32).reshape(split), axis=0)

    start = jnp.zeros((lanes, 8, chans), F32)
    acc = jnp.sum(lax.fori_loop(0, rows, add, start, unroll=4), axis=0)
    total = group_sum(jnp.sum(acc, axis=0, keepdims=True), per)
    mean = total / size

    def deviate(y, acc):
        away = video_ref[0, 0, y].astype(F32).reshape(split) - mean
        return acc + jnp.sum(away * away, axis=0)

    acc = jnp.sum(lax.fori_loop(0, rows, deviate, start, unroll=4), axis=0)
    sums[t] = jnp.broadcast_to(total, (8, chans))
    squares[t] = jnp.broadcast_to(group_sum(jnp.sum(acc, axis=0, keepdims=True), per), (8, chans))
    ends_ref[0, t] = video_ref[0, 0, rows - 1]
    ends_ref[1, t] = video_ref[0, 0, 0]

    @pl.when(t >= frames - before)
    def _():
        tail_ref[0, t - (frames - before)] = video_ref[0, 0]

    @pl.when(t == frames - 1)
    def _():
        inside = info_ref[0]
        parts = []
        for f in range(sums.shape[0]):
            keep = (f < inside).astype(F32)
            parts.append(
                jnp.concatenate(
                    [jnp.full((1, chans), size, F32), sums[f, 0:1], squares[f, 0:1]], axis=0
                )
                * keep
            )
        count, total, _, deviations = merged(parts)
        out_ref[...] = jnp.concatenate(
            [count, total, deviations, jnp.zeros((5, chans), F32)], axis=0
        )


def merge_kernel(parts_n, ends_ref, early_ref, *refs):
    parts, (out_ref, low_ref, high_ref) = refs[:parts_n], refs[parts_n:]
    count, total, _, deviations = merged([ref[...] for ref in parts])
    out_ref[...] = jnp.concatenate(
        [count, total, deviations, jnp.zeros((5, count.shape[1]), F32)], axis=0
    )
    before = early_ref.shape[1]
    for side, ref in enumerate((low_ref, high_ref)):
        ref[0:before] = early_ref[side]
        ref[before:] = ends_ref[side]


def cotangent_kernel(info_ref, cot_ref, turned_ref, bias_ref, wide):
    t = pl.program_id(0)
    rows, cols, chans = cot_ref.shape[2:]
    step = cols // TILE
    keep = (t < info_ref[0]).astype(F32)

    @pl.when(t == 0)
    def _():
        bias_ref[...] = jnp.zeros_like(bias_ref)

    def row(y, acc):
        value = cot_ref[0, 0, y].astype(F32) * keep
        slot = wide.at[y % wide.shape[0]]
        slot[...] = value
        order = jnp.concatenate(
            [slot[pl.ds(r, TILE, stride=step), :] for r in range(step)], axis=0
        )
        turned_ref[0, y] = order.T.astype(BF16)
        return acc + jnp.sum(value.reshape(cols // 8, 8, chans), axis=0)

    acc = lax.fori_loop(0, rows, row, jnp.zeros((8, chans), F32), unroll=4)
    bias_ref[0:1, :] += jnp.sum(acc, axis=0, keepdims=True)


def activate_kernel(
    parts_n, info_ref, video_ref, early_ref, low_ref, high_ref, gain_ref, shift_ref, *refs
):
    parts, out_ref, wide = refs[:parts_n], refs[parts_n], refs[parts_n + 1]
    frames, rows, cols, chans = video_ref.shape[1:]
    before = early_ref.shape[1]
    step = cols // TILE
    inside, first, has_low, has_high = info_ref[0], info_ref[1], info_ref[2], info_ref[3]
    count, _, mean, squares = merged([ref[...] for ref in parts])
    scale = 0.5 * lax.rsqrt(squares / count + 1e-05) * gain_ref[...]
    offset = 0.5 * shift_ref[...] - mean * scale
    slots = wide.shape[0]
    wide[:, 0:8, :] = jnp.zeros((slots, 8, chans), F32)
    wide[:, 8 + cols : 16 + cols, :] = jnp.zeros((slots, 8, chans), F32)

    def row(values, keep, slot, f, y):
        half = values.astype(F32) * (scale * keep) + offset * keep
        wide[slot, 8 : 8 + cols, :] = half + half * jnp.tanh(half)
        for r in range(-1, step + 1):
            out_ref[f, y, r + 1] = wide[slot, pl.ds(8 + r, TILE, stride=step), :].astype(BF16)

    for f in range(frames + before):
        local = f - before
        ok = (local < inside) & (first + local >= 0)
        keep = ok.astype(F32)
        source = early_ref.at[0, f] if local < 0 else video_ref.at[0, local]

        def inner(y, carry, source=source, keep=keep, f=f):
            row(source[y], keep, y % slots, f, y + 1)
            return carry

        lax.fori_loop(0, rows, inner, 0, unroll=4)
        row(low_ref[f], keep * has_low.astype(F32), 0, f, 0)
        row(high_ref[f], keep * has_high.astype(F32), 1, f, rows + 1)


def packed(value):
    per = value.shape[0] - TILE
    total = value[per : per + 1] + value[per + 1 : per + 2] + value[per + 2 : per + 3]
    top = total.astype(BF16).astype(F32)
    mid = (total - top).astype(BF16).astype(F32)
    rest = total - top - mid
    tail = jnp.concatenate([top, mid, rest, jnp.zeros((TILE - 3, value.shape[1]), F32)], axis=0)
    return jnp.concatenate([value[:per].astype(BF16), tail.astype(BF16)], axis=0)


def weights_kernel(info_ref, turned_ref, act_ref, bias_ref, keep_ref, *refs):
    send_refs, acc = refs[:-2], refs[-2:]
    acc, shards = acc
    frames, rows = turned_ref.shape[:2]
    chans = turned_ref.shape[2]
    k = turned_ref.shape[3]
    step = act_ref.shape[2] - 2
    taps = [(kt, ky, kx) for kt in range(3) for ky in range(3) for kx in range(3)]
    pair = 2

    def frame(t, carry):
        left = jnp.concatenate([turned_ref[t, y] for y in range(rows)], axis=1)
        for j in range(0, len(taps), pair):
            chosen = taps[j : j + pair]
            right = jnp.concatenate(
                [
                    act_ref[t + kt, ky : ky + rows, kx : kx + step].reshape(rows * k, chans)
                    for kt, ky, kx in chosen
                ],
                axis=1,
            )
            product = jnp.dot(left, right, preferred_element_type=F32)
            where = slice(j * chans, (j + len(chosen)) * chans)
            acc[:, where] = jnp.where(t == 0, product, acc[:, where] + product)
        return carry

    lax.fori_loop(0, frames, frame, 0)
    tms, dps, per = shards.shape[:3]
    per -= TILE
    for tap in range(len(taps)):
        block = acc[:, tap * chans : (tap + 1) * chans].T
        done = 0
        while done < chans:
            shard, at = divmod(tap * chans + done, per)
            take = min(chans - done, per - at)
            shards[shard // dps, shard % dps, at : at + take, :] = block[done : done + take]
            done += take
    tail = jnp.concatenate([bias_ref[0:1], jnp.zeros((TILE - 1, chans), F32)], axis=0)
    for i in range(tms):
        for j in range(dps):
            shards[i, j, per : per + TILE, :] = tail
    me = info_ref[4]
    keep_ref[...] = shards[me]
    for r in range(1, tms):
        send_refs[r - 1][...] = shards[me ^ r]


def spread_kernel(count, info_ref, after_ref, keep_ref, *refs):
    incoming, own_ref, send_refs = refs[:count], refs[count], refs[count + 1 :]
    me = info_ref[5]
    for r in range(len(send_refs) + 1):
        value = keep_ref[me ^ r]
        for ref in incoming:
            value = value + ref[me ^ r]
        if r == 0:
            own_ref[...] = value
        else:
            send_refs[r - 1][...] = packed(value)


def add_kernel(after_ref, *refs):
    value = refs[0][...].astype(F32)
    for ref in refs[1:-1]:
        value = value + ref[...].astype(F32)
    refs[-1][...] = packed(value) if refs[-1].dtype == BF16 else value


def taps_kernel(after_ref, kernel_ref, out_ref):
    kts, kys, kxs, chans = kernel_ref.shape[:4]
    pair = out_ref.shape[1] // chans
    zero = jnp.zeros((kys * kxs * chans, chans), BF16)
    span = kys * kxs * chans
    for f in range(kts + pair - 1):
        for g in range(pair):
            if 0 <= f - g < kts:
                value = kernel_ref[f - g].reshape(span, chans)
            else:
                value = zero
            out_ref[f * span : (f + 1) * span, g * chans : (g + 1) * chans] = value


def conv_kernel(t0, y0, rows, info_ref, after_ref, act_ref, taps_ref, video_ref, bias_ref, *refs):
    out_ref, wide = refs
    cols, chans = out_ref.shape[2:]
    step = cols // TILE
    pair = taps_ref.shape[1] // chans
    used = [
        (f, ky, kx)
        for f in range(taps_ref.shape[0] // (9 * chans))
        for ky in range(3)
        for kx in range(3)
    ]
    left = jnp.concatenate(
        [
            act_ref[t0 + f, y0 + ky : y0 + ky + rows, kx : kx + step].reshape(rows * cols, chans)
            for f, ky, kx in used
        ],
        axis=1,
    )
    result = jnp.dot(left, taps_ref[...], preferred_element_type=F32)
    for f in range(pair):
        keep = (t0 + f < info_ref[0]).astype(F32)
        for y in range(rows):
            slot = f * rows + y
            for r in range(step):
                at = y * cols + r * TILE
                wide[slot, pl.ds(r, TILE, stride=step), :] = result[
                    at : at + TILE, f * chans : (f + 1) * chans
                ]
            value = video_ref[0, t0 + f, y0 + y].astype(F32) + wide[slot] + bias_ref[...]
            out_ref[f, y] = (value * keep).astype(BF16)


def step_of(video, lengths, norm_gain, norm_shift, kernel, conv_bias, cotangent):
    frames, rows, cols, chans = video.shape[1:]
    per = chans // GROUPS
    step = cols // TILE
    before = kernel.shape[0] - 1
    tms, dps, spaces = (lax.axis_size(axis) for axis in ("tm", "dp", "space"))
    tm, dp, space = (lax.axis_index(axis) for axis in ("tm", "dp", "space"))
    first = tm * frames
    inside = jnp.clip(lengths[0] - first, -before, frames)
    info = jnp.stack(
        [
            inside,
            first,
            (space > 0).astype(jnp.int32),
            (space < spaces - 1).astype(jnp.int32),
            tm,
            dp,
        ]
    ).astype(jnp.int32)

    frame_spec = pl.BlockSpec((1, 1, rows, cols, chans), lambda t: (0, t, 0, 0, 0))
    stats, tail, ends = pl.pallas_call(
        functools.partial(stats_kernel, per, before),
        grid=(frames,),
        in_specs=[SMEM, frame_spec],
        out_specs=[
            pl.BlockSpec((8, chans), lambda t: (0, 0)),
            pl.BlockSpec((1, before, rows, cols, chans), lambda t: (0, 0, 0, 0, 0)),
            pl.BlockSpec((2, frames, cols, chans), lambda t: (0, 0, 0, 0)),
        ],
        out_shape=[
            jax.ShapeDtypeStruct((8, chans), F32),
            jax.ShapeDtypeStruct((1, before, rows, cols, chans), BF16),
            jax.ShapeDtypeStruct((2, frames, cols, chans), BF16),
        ],
        scratch_shapes=[pltpu.VMEM((frames, 8, chans), F32), pltpu.VMEM((frames, 8, chans), F32)],
        compiler_params=params(8),
        name="stats",
    )(info, pltpu.with_memory_space_constraint(video, pltpu.HBM))
    gathered = [stats] + [swap(stats, "tm", r) for r in range(1, tms)]
    following = [(i, (i + 1) % tms) for i in range(tms)]
    early_ends = lax.ppermute(ends[:, frames - before :], "tm", following)
    early = lax.ppermute(tail, "tm", following)
    border = jax.ShapeDtypeStruct((before + frames, cols, chans), BF16)
    stats, edge_low, edge_high = pl.pallas_call(
        functools.partial(merge_kernel, tms),
        in_specs=[VMEM] * (2 + tms),
        out_specs=[VMEM] * 3,
        out_shape=[jax.ShapeDtypeStruct((8, chans), F32), border, border],
        compiler_params=params(2),
        name="merge",
    )(ends, early_ends, *gathered)
    parts = [stats] + [swap(stats, "space", r) for r in range(1, spaces)]
    low = shifted(edge_low, "space", 1)
    high = shifted(edge_high, "space", -1)
    pair = 2
    taps = pl.pallas_call(
        taps_kernel,
        in_specs=[ANY, VMEM],
        out_specs=VMEM,
        out_shape=jax.ShapeDtypeStruct(
            ((kernel.shape[0] + pair - 1) * 9 * chans, pair * chans), BF16
        ),
        compiler_params=params(2),
        name="taps",
    )(ends, kernel)

    turned, bias = pl.pallas_call(
        cotangent_kernel,
        grid=(frames,),
        in_specs=[SMEM, frame_spec],
        out_specs=[
            pl.BlockSpec((1, rows, chans, cols), lambda t: (t, 0, 0, 0)),
            pl.BlockSpec((8, chans), lambda t: (0, 0)),
        ],
        out_shape=[
            jax.ShapeDtypeStruct((frames, rows, chans, cols), BF16),
            jax.ShapeDtypeStruct((8, chans), F32),
        ],
        scratch_shapes=[pltpu.VMEM((4, cols, chans), F32)],
        compiler_params=params(8),
        name="cotangent",
    )(info, pltpu.with_memory_space_constraint(cotangent, pltpu.HBM))

    act = pl.pallas_call(
        functools.partial(activate_kernel, spaces),
        in_specs=[SMEM] + [VMEM] * (6 + spaces),
        out_specs=VMEM,
        out_shape=jax.ShapeDtypeStruct(
            (frames + before, rows + 2, step + 2, TILE, chans), BF16
        ),
        scratch_shapes=[pltpu.VMEM((4, cols + 16, chans), F32)],
        compiler_params=params(8),
        name="activate",
    )(
        info,
        video,
        early,
        low,
        high,
        norm_gain.reshape(1, chans),
        norm_shift.reshape(1, chans),
        *parts,
    )

    count = kernel.shape[0] * kernel.shape[1] * kernel.shape[2] * chans
    shards_n = tms * dps
    assert count % shards_n == 0
    shard = count // shards_n
    full = shard + TILE
    keep, *sends = pl.pallas_call(
        weights_kernel,
        in_specs=[SMEM, VMEM, VMEM, VMEM],
        out_specs=[VMEM] * tms,
        out_shape=[jax.ShapeDtypeStruct((dps, full, chans), F32)] * tms,
        scratch_shapes=[
            pltpu.VMEM((chans, count), F32),
            pltpu.VMEM((tms, dps, full, chans), F32),
        ],
        compiler_params=params(16),
        name="weights",
    )(info, turned, act, bias)

    block = 4
    pieces = [(t0, y0) for t0 in range(0, frames, pair) for y0 in range(0, rows, block)]
    done = []

    def cover(after, number):
        for _ in range(min(number, len(pieces) - len(done))):
            t0, y0 = pieces[len(done)]
            after = pl.pallas_call(
                functools.partial(conv_kernel, t0, y0, block),
                in_specs=[SMEM, ANY, VMEM, VMEM, VMEM, VMEM],
                out_specs=VMEM,
                out_shape=jax.ShapeDtypeStruct((pair, block, cols, chans), BF16),
                scratch_shapes=[pltpu.VMEM((pair * block, cols, chans), F32)],
                compiler_params=params(6),
                name="conv",
            )(info, after, act, taps, video, conv_bias.reshape(1, chans))
            done.append(after)
        return after

    incoming = [swap(send, "tm", r + 1) for r, send in enumerate(sends)]
    token = cover(keep, 2)
    own, *sends = pl.pallas_call(
        functools.partial(spread_kernel, len(incoming)),
        in_specs=[SMEM, ANY] + [VMEM] * (1 + len(incoming)),
        out_specs=[VMEM] * dps,
        out_shape=[jax.ShapeDtypeStruct((full, chans), F32)]
        + [jax.ShapeDtypeStruct((full, chans), BF16)] * (dps - 1),
        compiler_params=params(4),
        name="spread",
    )(info, token, keep, *incoming)

    def added(dtype, after, *arrays):
        return pl.pallas_call(
            add_kernel,
            in_specs=[ANY] + [VMEM] * len(arrays),
            out_specs=VMEM,
            out_shape=jax.ShapeDtypeStruct((full, chans), dtype),
            compiler_params=params(2),
            name="added",
        )(after, *arrays)

    incoming = [swap(send, "dp", r + 1) for r, send in enumerate(sends)]
    token = cover(own, 1)
    total = added(F32 if spaces > 2 else BF16, token, own, *incoming)
    by = 1
    while by < spaces:
        other = swap(total, "space", by)
        token = cover(total, 2)
        by *= 2
        total = added(F32 if 2 * by < spaces else BF16, token, total, other)
    mine = [total] + [swap(total, "dp", r) for r in range(1, dps)]
    cover(total, len(pieces))
    shards = {(0, r): array for r, array in enumerate(mine)}
    for q in range(1, tms):
        for r, array in enumerate(mine):
            shards[q, r] = swap(array, "tm", q)
    order = list(shards)

    def collect(info_ref, *refs):
        shard_refs, piece_refs = refs[: len(order)], refs[len(order) : len(order) + len(done)]
        out_ref, sum_ref, output_ref, sems = refs[-4:]
        copies = []
        for n, (t0, y0) in enumerate(pieces):
            target = output_ref.at[0, t0 : t0 + pair, y0 : y0 + block]
            copies.append(pltpu.make_async_copy(piece_refs[n], target, sems.at[n]))
            copies[-1].start()
        for (q, r), ref in zip(order, shard_refs):
            at = (info_ref[4] ^ q) * dps + (info_ref[5] ^ r)
            out_ref[at] = ref[0:shard, :].astype(F32)
        tail = shard_refs[0][shard : shard + TILE, :].astype(F32)
        sum_ref[...] = tail[0:1] + tail[1:2] + tail[2:3]
        for copy in copies:
            copy.wait()

    grad_kernel, grad_bias, output = pl.pallas_call(
        collect,
        in_specs=[SMEM] + [VMEM] * (len(order) + len(done)),
        out_specs=[VMEM, VMEM, ANY],
        out_shape=[
            jax.ShapeDtypeStruct((shards_n, shard, chans), F32),
            jax.ShapeDtypeStruct((1, chans), F32),
            jax.ShapeDtypeStruct(video.shape, BF16),
        ],
        scratch_shapes=[pltpu.SemaphoreType.DMA((len(pieces),))],
        compiler_params=params(4),
        name="collect",
    )(info, *[shards[key] for key in order], *done)

    return output, grad_kernel.reshape(kernel.shape), grad_bias.reshape(chans)


def solution(mesh):
    return jax.shard_map(
        step_of,
        mesh=mesh,
        in_specs=(
            P("dp", "tm", "space", None, None),
            P("dp"),
            P(),
            P(),
            P(),
            P(),
            P("dp", "tm", "space", None, None),
        ),
        out_specs=(P("dp", "tm", "space", None, None), P(), P()),
        check_vma=False,
    )
```

```python
import functools

import jax
import jax.numpy as jnp
from jax import lax
from jax.experimental import pallas as pl
from jax.experimental.pallas import tpu as pltpu
from jax.sharding import PartitionSpec as P


GROUPS = 32
TILE = 16
F32 = jnp.float32
BF16 = jnp.bfloat16
VMEM = pl.BlockSpec(memory_space=pltpu.VMEM)
ANY = pl.BlockSpec(memory_space=pl.ANY)
SMEM = pl.BlockSpec(memory_space=pltpu.SMEM)


def params(mib):
    return pltpu.CompilerParams(vmem_limit_bytes=mib * 1024 * 1024)


def swap(array, axis, by):
    length = lax.axis_size(axis)
    assert length & (length - 1) == 0
    return lax.ppermute(array, axis, [(i, i ^ by) for i in range(length)])


def shifted(array, axis, by):
    length = lax.axis_size(axis)
    return lax.ppermute(array, axis, [(i, i + by) for i in range(length) if 0 <= i + by < length])


def group_sum(row, per):
    value = jnp.broadcast_to(row, (8, row.shape[1]))
    lane = lax.broadcasted_iota(jnp.int32, value.shape, 1)
    size = value.shape[1]
    step = 1
    while step < per:
        up = pltpu.roll(value, size - step, 1)
        down = pltpu.roll(value, step, 1)
        value = value + jnp.where((lane & step) == 0, up, down)
        step *= 2
    return value[0:1]


def merged(parts):
    count = sum(part[0:1] for part in parts)
    total = sum(part[1:2] for part in parts)
    mean = total / jnp.maximum(count, 1.0)
    squares = jnp.zeros_like(mean)
    for part in parts:
        away = part[1:2] / jnp.maximum(part[0:1], 1.0) - mean
        squares = squares + (part[2:3] + part[0:1] * (away * away))
    return count, total, mean, squares


def stats_kernel(per, before, info_ref, video_hbm, cot_hbm, *refs):
    out_ref, video_ref, cot_ref, tail_ref, ends_ref, early_ref, sems = refs
    frames, rows, cols, chans = video_ref.shape[1:]
    parts_n = 2 * frames
    some = rows // 2
    first = frames - before
    copies = []
    for n in range(parts_n):
        at = (0, n // 2, pl.ds(n % 2 * some, some))
        copies.append((video_hbm.at[at], video_ref.at[at]))
    copies.append((video_hbm.at[:, first:], tail_ref))
    for side, row in enumerate((rows - 1, 0)):
        copies.append((video_hbm.at[0, :, row], ends_ref.at[side]))
        copies.append((video_hbm.at[0, first:, row], early_ref.at[side]))
    copies.append((cot_hbm, cot_ref))
    copies = [
        pltpu.make_async_copy(source, target, sems.at[n])
        for n, (source, target) in enumerate(copies)
    ]
    for copy in copies:
        copy.start()
    size = float(some * cols * per)
    lanes = 4
    split = (cols // (8 * lanes), lanes, 8, chans)
    start = jnp.zeros((lanes, 8, chans), F32)
    parts = []
    for n in range(parts_n):
        copies[n].wait()
        f, y0 = n // 2, n % 2 * some

        def add(y, acc, f=f, y0=y0):
            return acc + jnp.sum(video_ref[0, f, y0 + y].astype(F32).reshape(split), axis=0)

        acc = jnp.sum(lax.fori_loop(0, some, add, start, unroll=4), axis=0)
        total = group_sum(jnp.sum(acc, axis=0, keepdims=True), per)
        mean = total / size

        def deviate(y, acc, f=f, y0=y0, mean=mean):
            away = video_ref[0, f, y0 + y].astype(F32).reshape(split) - mean
            return acc + jnp.sum(away * away, axis=0)

        acc = jnp.sum(lax.fori_loop(0, some, deviate, start, unroll=4), axis=0)
        squares = group_sum(jnp.sum(acc, axis=0, keepdims=True), per)
        keep = (f < info_ref[0]).astype(F32)
        parts.append(
            jnp.concatenate([jnp.full((1, chans), size, F32), total, squares], axis=0) * keep
        )
    count, total, _, deviations = merged(parts)
    out_ref[...] = jnp.concatenate(
        [count, total, deviations, jnp.zeros((5, chans), F32)], axis=0
    )
    for copy in copies[parts_n:]:
        copy.wait()


def merge_kernel(parts_n, ends_ref, early_ref, *refs):
    parts, (out_ref, low_ref, high_ref) = refs[:parts_n], refs[parts_n:]
    count, total, _, deviations = merged([ref[...] for ref in parts])
    out_ref[...] = jnp.concatenate(
        [count, total, deviations, jnp.zeros((5, count.shape[1]), F32)], axis=0
    )
    before = early_ref.shape[1]
    for side, ref in enumerate((low_ref, high_ref)):
        ref[0:before] = early_ref[side]
        ref[before:] = ends_ref[side]


def cotangent_kernel(info_ref, cot_ref, turned_ref, bias_ref, wide):
    frames, rows, cols, chans = cot_ref.shape[1:]
    step = cols // TILE
    lanes = 4
    bias = jnp.zeros((lanes, 8, chans), F32)
    for t in range(frames):
        keep = (t < info_ref[0]).astype(F32)

        def row(y, acc, t=t, keep=keep):
            value = cot_ref[0, t, y].astype(F32) * keep
            slot = wide.at[y % wide.shape[0]]
            slot[...] = value
            order = jnp.concatenate(
                [slot[pl.ds(r, TILE, stride=step), :] for r in range(step)], axis=0
            )
            turned_ref[t, y] = order.astype(BF16).T
            return acc + jnp.sum(value.reshape(cols // (8 * lanes), lanes, 8, chans), axis=0)

        bias = lax.fori_loop(0, rows, row, bias, unroll=8)
    total = jnp.sum(jnp.sum(bias, axis=0), axis=0, keepdims=True)
    bias_ref[...] = jnp.broadcast_to(total, bias_ref.shape)


def activate_kernel(
    parts_n, info_ref, video_ref, early_ref, low_ref, high_ref, gain_ref, shift_ref, *refs
):
    parts, out_ref, wide = refs[:parts_n], refs[parts_n], refs[parts_n + 1]
    frames, rows, cols, chans = video_ref.shape[1:]
    before = early_ref.shape[1]
    step = cols // TILE
    inside, first, has_low, has_high = info_ref[0], info_ref[1], info_ref[2], info_ref[3]
    count, _, mean, squares = merged([ref[...] for ref in parts])
    scale = 0.5 * lax.rsqrt(squares / count + 1e-05) * gain_ref[...]
    offset = 0.5 * shift_ref[...] - mean * scale
    slots = wide.shape[0]
    wide[:, 0:8, :] = jnp.zeros((slots, 8, chans), F32)
    wide[:, 8 + cols : 16 + cols, :] = jnp.zeros((slots, 8, chans), F32)

    def row(values, keep, slot, f, y):
        half = values.astype(F32) * (scale * keep) + offset * keep
        wide[slot, 8 : 8 + cols, :] = half + half * jnp.tanh(half)
        for r in range(-1, step + 1):
            out_ref[f, y, r + 1] = wide[slot, pl.ds(8 + r, TILE, stride=step), :].astype(BF16)

    for f in range(frames + before):
        local = f - before
        ok = (local < inside) & (first + local >= 0)
        keep = ok.astype(F32)
        source = early_ref.at[0, f] if local < 0 else video_ref.at[0, local]

        def inner(y, carry, source=source, keep=keep, f=f):
            row(source[y], keep, y % slots, f, y + 1)
            return carry

        lax.fori_loop(0, rows, inner, 0, unroll=4)
        row(low_ref[f], keep * has_low.astype(F32), 0, f, 0)
        row(high_ref[f], keep * has_high.astype(F32), 1, f, rows + 1)


def packed(value):
    per = value.shape[0] - TILE
    total = value[per : per + 1] + value[per + 1 : per + 2] + value[per + 2 : per + 3]
    top = total.astype(BF16).astype(F32)
    mid = (total - top).astype(BF16).astype(F32)
    rest = total - top - mid
    tail = jnp.concatenate([top, mid, rest, jnp.zeros((TILE - 3, value.shape[1]), F32)], axis=0)
    return jnp.concatenate([value[:per].astype(BF16), tail.astype(BF16)], axis=0)


def weights_kernel(info_ref, turned_ref, act_ref, bias_ref, keep_ref, *refs):
    send_refs, acc = refs[:-2], refs[-2:]
    acc, shards = acc
    frames, rows = turned_ref.shape[:2]
    chans = turned_ref.shape[2]
    k = turned_ref.shape[3]
    step = act_ref.shape[2] - 2
    taps = [(kt, ky, kx) for kt in range(3) for ky in range(3) for kx in range(3)]
    pair = 2

    def frame(t, carry):
        left = jnp.concatenate([turned_ref[t, y] for y in range(rows)], axis=1)
        for j in range(0, len(taps), pair):
            chosen = taps[j : j + pair]
            right = jnp.concatenate(
                [
                    act_ref[t + kt, ky : ky + rows, kx : kx + step].reshape(rows * k, chans)
                    for kt, ky, kx in chosen
                ],
                axis=1,
            )
            product = jnp.dot(left, right, preferred_element_type=F32)
            where = slice(j * chans, (j + len(chosen)) * chans)
            acc[:, where] = jnp.where(t == 0, product, acc[:, where] + product)
        return carry

    lax.fori_loop(0, frames, frame, 0)
    tms, dps, per = shards.shape[:3]
    per -= TILE
    for tap in range(len(taps)):
        block = acc[:, tap * chans : (tap + 1) * chans].T
        done = 0
        while done < chans:
            shard, at = divmod(tap * chans + done, per)
            take = min(chans - done, per - at)
            shards[shard // dps, shard % dps, at : at + take, :] = block[done : done + take]
            done += take
    tail = jnp.concatenate([bias_ref[0:1], jnp.zeros((TILE - 1, chans), F32)], axis=0)
    for i in range(tms):
        for j in range(dps):
            shards[i, j, per : per + TILE, :] = tail
    me = info_ref[4]
    keep_ref[...] = shards[me]
    for r in range(1, tms):
        send_refs[r - 1][...] = shards[me ^ r]


def spread_kernel(count, info_ref, after_ref, keep_ref, *refs):
    incoming, own_ref, send_refs = refs[:count], refs[count], refs[count + 1 :]
    me = info_ref[5]
    for r in range(len(send_refs) + 1):
        value = keep_ref[me ^ r]
        for ref in incoming:
            value = value + ref[me ^ r]
        if r == 0:
            own_ref[...] = value
        else:
            send_refs[r - 1][...] = packed(value)


def add_kernel(after_ref, *refs):
    values = [ref[...].astype(F32) for ref in refs[:-1]]
    while len(values) > 1:
        values = [sum(values[n : n + 2]) for n in range(0, len(values), 2)]
    refs[-1][...] = packed(values[0])


def taps_kernel(after_ref, kernel_ref, out_ref):
    kts, kys, kxs, chans = kernel_ref.shape[:4]
    pair = out_ref.shape[1] // chans
    zero = jnp.zeros((kys * kxs * chans, chans), BF16)
    span = kys * kxs * chans
    for f in range(kts + pair - 1):
        for g in range(pair):
            if 0 <= f - g < kts:
                value = kernel_ref[f - g].reshape(span, chans)
            else:
                value = zero
            out_ref[f * span : (f + 1) * span, g * chans : (g + 1) * chans] = value


def conv_kernel(
    piece, last, info_ref, after_ref, act_ref, taps_ref, video_ref, bias_ref, *refs
):
    out_ref, whole_ref, wide, sem = refs[-4:]
    t0, y0 = piece
    rows = out_ref.shape[1]
    if last is not None:
        out = pltpu.make_async_copy(refs[0], whole_ref.at[last], sem)
        out.start()
    cols, chans = out_ref.shape[2:]
    step = cols // TILE
    pair = taps_ref.shape[1] // chans
    used = [
        (f, ky, kx)
        for f in range(taps_ref.shape[0] // (9 * chans))
        for ky in range(3)
        for kx in range(3)
    ]
    left = jnp.concatenate(
        [
            act_ref[t0 + f, y0 + ky : y0 + ky + rows, kx : kx + step].reshape(rows * cols, chans)
            for f, ky, kx in used
        ],
        axis=1,
    )
    result = jnp.dot(left, taps_ref[...], preferred_element_type=F32)
    for f in range(pair):
        keep = (t0 + f < info_ref[0]).astype(F32)
        for y in range(rows):
            slot = f * rows + y
            for r in range(step):
                at = y * cols + r * TILE
                wide[slot, pl.ds(r, TILE, stride=step), :] = result[
                    at : at + TILE, f * chans : (f + 1) * chans
                ]
            value = video_ref[0, t0 + f, y0 + y].astype(F32) + wide[slot] + bias_ref[...]
            out_ref[f, y] = (value * keep).astype(BF16)
    if last is not None:
        out.wait()


def step_of(video, lengths, norm_gain, norm_shift, kernel, conv_bias, cotangent):
    frames, rows, cols, chans = video.shape[1:]
    per = chans // GROUPS
    step = cols // TILE
    before = kernel.shape[0] - 1
    tms, dps, spaces = (lax.axis_size(axis) for axis in ("tm", "dp", "space"))
    tm, dp, space = (lax.axis_index(axis) for axis in ("tm", "dp", "space"))
    first = tm * frames
    inside = jnp.clip(lengths[0] - first, -before, frames)
    info = jnp.stack(
        [
            inside,
            first,
            (space > 0).astype(jnp.int32),
            (space < spaces - 1).astype(jnp.int32),
            tm,
            dp,
        ]
    ).astype(jnp.int32)

    both = 2 * frames + 6
    stats, local, masked_in, tail, ends, ends_tail = pl.pallas_call(
        functools.partial(stats_kernel, per, before),
        in_specs=[SMEM, ANY, ANY],
        out_specs=[VMEM] * 6,
        out_shape=[
            jax.ShapeDtypeStruct((8, chans), F32),
            jax.ShapeDtypeStruct(video.shape, BF16),
            jax.ShapeDtypeStruct(cotangent.shape, BF16),
            jax.ShapeDtypeStruct((1, before, rows, cols, chans), BF16),
            jax.ShapeDtypeStruct((2, frames, cols, chans), BF16),
            jax.ShapeDtypeStruct((2, before, cols, chans), BF16),
        ],
        scratch_shapes=[pltpu.SemaphoreType.DMA((both,))],
        compiler_params=params(2),
        name="stats",
    )(
        info,
        pltpu.with_memory_space_constraint(video, pltpu.HBM),
        pltpu.with_memory_space_constraint(cotangent, pltpu.HBM),
    )
    gathered = [stats] + [swap(stats, "tm", r) for r in range(1, tms)]
    following = [(i, (i + 1) % tms) for i in range(tms)]
    early_ends = lax.ppermute(ends_tail, "tm", following)
    early = lax.ppermute(tail, "tm", following)
    border = jax.ShapeDtypeStruct((before + frames, cols, chans), BF16)
    stats, edge_low, edge_high = pl.pallas_call(
        functools.partial(merge_kernel, tms),
        in_specs=[VMEM] * (2 + tms),
        out_specs=[VMEM] * 3,
        out_shape=[jax.ShapeDtypeStruct((8, chans), F32), border, border],
        compiler_params=params(2),
        name="merge",
    )(ends, early_ends, *gathered)
    parts = [stats] + [swap(stats, "space", r) for r in range(1, spaces)]
    low = shifted(edge_low, "space", 1)
    high = shifted(edge_high, "space", -1)
    pair = 2
    taps = pl.pallas_call(
        taps_kernel,
        in_specs=[ANY, VMEM],
        out_specs=VMEM,
        out_shape=jax.ShapeDtypeStruct(
            ((kernel.shape[0] + pair - 1) * 9 * chans, pair * chans), BF16
        ),
        compiler_params=params(2),
        name="taps",
    )(ends, kernel)

    turned, bias = pl.pallas_call(
        cotangent_kernel,
        in_specs=[SMEM, VMEM],
        out_specs=[VMEM, VMEM],
        out_shape=[
            jax.ShapeDtypeStruct((frames, rows, chans, cols), BF16),
            jax.ShapeDtypeStruct((8, chans), F32),
        ],
        scratch_shapes=[pltpu.VMEM((8, cols, chans), F32)],
        compiler_params=params(4),
        name="cotangent",
    )(info, masked_in)

    act = pl.pallas_call(
        functools.partial(activate_kernel, spaces),
        in_specs=[SMEM] + [VMEM] * (6 + spaces),
        out_specs=VMEM,
        out_shape=jax.ShapeDtypeStruct(
            (frames + before, rows + 2, step + 2, TILE, chans), BF16
        ),
        scratch_shapes=[pltpu.VMEM((4, cols + 16, chans), F32)],
        compiler_params=params(8),
        name="activate",
    )(
        info,
        local,
        early,
        low,
        high,
        norm_gain.reshape(1, chans),
        norm_shift.reshape(1, chans),
        *parts,
    )

    count = kernel.shape[0] * kernel.shape[1] * kernel.shape[2] * chans
    shards_n = tms * dps
    assert count % shards_n == 0
    shard = count // shards_n
    full = shard + TILE
    keep, *sends = pl.pallas_call(
        weights_kernel,
        in_specs=[SMEM, VMEM, VMEM, VMEM],
        out_specs=[VMEM] * tms,
        out_shape=[jax.ShapeDtypeStruct((dps, full, chans), F32)] * tms,
        scratch_shapes=[
            pltpu.VMEM((chans, count), F32),
            pltpu.VMEM((tms, dps, full, chans), F32),
        ],
        compiler_params=params(16),
        name="weights",
    )(info, turned, act, bias)

    block = 4
    pieces = [(t0, y0) for t0 in range(0, frames, pair) for y0 in range(0, rows, block)]
    done = []

    whole = jax.ShapeDtypeStruct(video.shape, BF16)

    def where(n):
        t0, y0 = pieces[n]
        return 0, pl.ds(t0, pair), pl.ds(y0, block)

    def cover(after, number):
        for _ in range(min(number, len(pieces) - len(done))):
            n = len(done)
            made = list(done[-1]) if done else []
            piece, output = pl.pallas_call(
                functools.partial(conv_kernel, pieces[n], where(n - 1) if made else None),
                in_specs=[SMEM, ANY, VMEM, VMEM, VMEM, VMEM] + [VMEM, ANY][: len(made)],
                out_specs=[VMEM, ANY],
                out_shape=[jax.ShapeDtypeStruct((pair, block, cols, chans), BF16), whole],
                scratch_shapes=[
                    pltpu.VMEM((pair * block, cols, chans), F32),
                    pltpu.SemaphoreType.DMA,
                ],
                input_output_aliases={7: 1} if made else {},
                compiler_params=params(6),
                name="conv",
            )(info, after, act, taps, local, conv_bias.reshape(1, chans), *made)
            done.append((piece, output))
            after = piece
        return after

    incoming = [swap(send, "tm", r + 1) for r, send in enumerate(sends)]
    token = cover(keep, 1)
    own, *sends = pl.pallas_call(
        functools.partial(spread_kernel, len(incoming)),
        in_specs=[SMEM, ANY] + [VMEM] * (1 + len(incoming)),
        out_specs=[VMEM] * dps,
        out_shape=[jax.ShapeDtypeStruct((full, chans), F32)]
        + [jax.ShapeDtypeStruct((full, chans), BF16)] * (dps - 1),
        compiler_params=params(4),
        name="spread",
    )(info, token, keep, *incoming)

    def added(dtype, after, *arrays):
        return pl.pallas_call(
            add_kernel,
            in_specs=[ANY] + [VMEM] * len(arrays),
            out_specs=VMEM,
            out_shape=jax.ShapeDtypeStruct((full, chans), dtype),
            compiler_params=params(2),
            name="added",
        )(after, *arrays)

    incoming = [swap(send, "dp", r + 1) for r, send in enumerate(sends)]
    token = cover(own, 3)
    total = added(BF16, token, own, *incoming)
    others = [swap(total, "space", r) for r in range(1, spaces)]
    token = cover(total, 3)
    total = added(BF16, token, total, *others)
    mine = [total] + [swap(total, "dp", r) for r in range(1, dps)]
    cover(total, len(pieces))
    shards = {(0, r): array for r, array in enumerate(mine)}
    for q in range(1, tms):
        for r, array in enumerate(mine):
            shards[q, r] = swap(array, "tm", q)
    order = list(shards)

    def collect(info_ref, *refs):
        shard_refs, piece_ref = refs[: len(order)], refs[len(order)]
        out_ref, sum_ref, whole_ref, sem = refs[-4:]
        copy = pltpu.make_async_copy(piece_ref, whole_ref.at[where(len(pieces) - 1)], sem)
        copy.start()
        for (q, r), ref in zip(order, shard_refs):
            at = (info_ref[4] ^ q) * dps + (info_ref[5] ^ r)
            out_ref[at] = ref[0:shard, :].astype(F32)
        tail = shard_refs[0][shard : shard + TILE, :].astype(F32)
        sum_ref[...] = tail[0:1] + tail[1:2] + tail[2:3]
        copy.wait()

    grad_kernel, grad_bias, output = pl.pallas_call(
        collect,
        in_specs=[SMEM] + [VMEM] * (len(order) + 1) + [ANY],
        out_specs=[VMEM, VMEM, ANY],
        out_shape=[
            jax.ShapeDtypeStruct((shards_n, shard, chans), F32),
            jax.ShapeDtypeStruct((1, chans), F32),
            whole,
        ],
        scratch_shapes=[pltpu.SemaphoreType.DMA],
        input_output_aliases={len(order) + 2: 2},
        compiler_params=params(4),
        name="collect",
    )(info, *[shards[key] for key in order], *done[-1])

    return output, grad_kernel.reshape(kernel.shape), grad_bias.reshape(chans)


def solution(mesh):
    return jax.shard_map(
        step_of,
        mesh=mesh,
        in_specs=(
            P("dp", "tm", "space", None, None),
            P("dp"),
            P(),
            P(),
            P(),
            P(),
            P("dp", "tm", "space", None, None),
        ),
        out_specs=(P("dp", "tm", "space", None, None), P(), P()),
        check_vma=False,
    )
```

```python
import functools

import jax
import jax.numpy as jnp
from jax import lax
from jax.experimental import pallas as pl
from jax.experimental.pallas import tpu as pltpu
from jax.sharding import PartitionSpec as P


GROUPS = 32
TILE = 16
F32 = jnp.float32
BF16 = jnp.bfloat16
VMEM = pl.BlockSpec(memory_space=pltpu.VMEM)
ANY = pl.BlockSpec(memory_space=pl.ANY)
SMEM = pl.BlockSpec(memory_space=pltpu.SMEM)


def params(mib):
    return pltpu.CompilerParams(vmem_limit_bytes=mib * 1024 * 1024)


def swap(array, axis, by):
    length = lax.axis_size(axis)
    assert length & (length - 1) == 0
    return lax.ppermute(array, axis, [(i, i ^ by) for i in range(length)])


def shifted(array, axis, by):
    length = lax.axis_size(axis)
    return lax.ppermute(array, axis, [(i, i + by) for i in range(length) if 0 <= i + by < length])


def group_sum(row, per):
    value = jnp.broadcast_to(row, (8, row.shape[1]))
    lane = lax.broadcasted_iota(jnp.int32, value.shape, 1)
    size = value.shape[1]
    step = 1
    while step < per:
        up = pltpu.roll(value, size - step, 1)
        down = pltpu.roll(value, step, 1)
        value = value + jnp.where((lane & step) == 0, up, down)
        step *= 2
    return value[0:1]


def merged(parts):
    count = sum(part[0:1] for part in parts)
    total = sum(part[1:2] for part in parts)
    mean = total / jnp.maximum(count, 1.0)
    squares = jnp.zeros_like(mean)
    for part in parts:
        away = part[1:2] / jnp.maximum(part[0:1], 1.0) - mean
        squares = squares + (part[2:3] + part[0:1] * (away * away))
    return count, total, mean, squares


def ends_kernel(video_hbm, low_ref, high_ref, sems):
    rows = video_hbm.shape[2]
    copies = [
        pltpu.make_async_copy(video_hbm.at[0, :, row], ref, sems.at[n])
        for n, (row, ref) in enumerate(((rows - 1, low_ref), (0, high_ref)))
    ]
    for copy in copies:
        copy.start()
    for copy in copies:
        copy.wait()


def stats_kernel(per, before, info_ref, video_hbm, cot_hbm, *refs):
    out_ref, video_ref, cot_ref, tail_ref, sems = refs
    frames, rows, cols, chans = video_ref.shape[1:]
    parts_n = 2 * frames
    some = rows // 2
    first = frames - before
    copies = []
    for n in range(parts_n):
        at = (0, n // 2, pl.ds(n % 2 * some, some))
        copies.append(pltpu.make_async_copy(video_hbm.at[at], video_ref.at[at], sems.at[n]))
        copies[-1].start()
    later = [pltpu.make_async_copy(cot_hbm, cot_ref, sems.at[parts_n])]
    later[0].start()
    size = float(some * cols * per)
    lanes = 4
    split = (cols // (8 * lanes), lanes, 8, chans)
    start = jnp.zeros((lanes, 8, chans), F32)
    parts = []
    for n in range(parts_n):
        copies[n].wait()
        f, y0 = n // 2, n % 2 * some
        if n % 2 and f >= first:
            sem = sems.at[parts_n + 1 + f - first]
            later.append(pltpu.make_async_copy(video_ref.at[0, f], tail_ref.at[0, f - first], sem))
            later[-1].start()

        def add(y, acc, f=f, y0=y0):
            return acc + jnp.sum(video_ref[0, f, y0 + y].astype(F32).reshape(split), axis=0)

        acc = jnp.sum(lax.fori_loop(0, some, add, start, unroll=4), axis=0)
        total = group_sum(jnp.sum(acc, axis=0, keepdims=True), per)
        mean = total / size

        def deviate(y, acc, f=f, y0=y0, mean=mean):
            away = video_ref[0, f, y0 + y].astype(F32).reshape(split) - mean
            return acc + jnp.sum(away * away, axis=0)

        acc = jnp.sum(lax.fori_loop(0, some, deviate, start, unroll=4), axis=0)
        squares = group_sum(jnp.sum(acc, axis=0, keepdims=True), per)
        keep = (f < info_ref[0]).astype(F32)
        parts.append(
            jnp.concatenate([jnp.full((1, chans), size, F32), total, squares], axis=0) * keep
        )
    count, total, _, deviations = merged(parts)
    out_ref[...] = jnp.concatenate(
        [count, total, deviations, jnp.zeros((5, chans), F32)], axis=0
    )
    for copy in later:
        copy.wait()


def merge_kernel(*refs):
    count, total, _, deviations = merged([ref[...] for ref in refs[:-1]])
    refs[-1][...] = jnp.concatenate(
        [count, total, deviations, jnp.zeros((5, count.shape[1]), F32)], axis=0
    )


def cotangent_kernel(info_ref, cot_ref, turned_ref, bias_ref, wide):
    frames, rows, cols, chans = cot_ref.shape[1:]
    step = cols // TILE
    lanes = 4
    bias = jnp.zeros((lanes, 8, chans), F32)
    for t in range(frames):
        keep = (t < info_ref[0]).astype(F32)

        def row(y, acc, t=t, keep=keep):
            value = cot_ref[0, t, y].astype(F32) * keep
            slot = wide.at[y % wide.shape[0]]
            slot[...] = value
            order = jnp.concatenate(
                [slot[pl.ds(r, TILE, stride=step), :] for r in range(step)], axis=0
            )
            turned_ref[t, y] = order.astype(BF16).T
            return acc + jnp.sum(value.reshape(cols // (8 * lanes), lanes, 8, chans), axis=0)

        bias = lax.fori_loop(0, rows, row, bias, unroll=8)
    total = jnp.sum(jnp.sum(bias, axis=0), axis=0, keepdims=True)
    bias_ref[...] = jnp.broadcast_to(total, bias_ref.shape)


def activate_kernel(
    parts_n, info_ref, video_ref, early_ref, low_ref, high_ref, low_early_ref, high_early_ref, *refs
):
    gain_ref, shift_ref, *refs = refs
    parts, out_ref, wide = refs[:parts_n], refs[parts_n], refs[parts_n + 1]
    frames, rows, cols, chans = video_ref.shape[1:]
    before = early_ref.shape[1]
    step = cols // TILE
    inside, first, has_low, has_high = info_ref[0], info_ref[1], info_ref[2], info_ref[3]
    count, _, mean, squares = merged([ref[...] for ref in parts])
    scale = 0.5 * lax.rsqrt(squares / count + 1e-05) * gain_ref[...]
    offset = 0.5 * shift_ref[...] - mean * scale
    slots = wide.shape[0]
    wide[:, 0:8, :] = jnp.zeros((slots, 8, chans), F32)
    wide[:, 8 + cols : 16 + cols, :] = jnp.zeros((slots, 8, chans), F32)

    def row(values, keep, slot, f, y):
        half = values.astype(F32) * (scale * keep) + offset * keep
        wide[slot, 8 : 8 + cols, :] = half + half * jnp.tanh(half)
        for r in range(-1, step + 1):
            out_ref[f, y, r + 1] = wide[slot, pl.ds(8 + r, TILE, stride=step), :].astype(BF16)

    for f in range(frames + before):
        local = f - before
        ok = (local < inside) & (first + local >= 0)
        keep = ok.astype(F32)
        source = early_ref.at[0, f] if local < 0 else video_ref.at[0, local]

        def inner(y, carry, source=source, keep=keep, f=f):
            row(source[y], keep, y % slots, f, y + 1)
            return carry

        lax.fori_loop(0, rows, inner, 0, unroll=4)
        low = low_early_ref[frames + local] if local < 0 else low_ref[local]
        high = high_early_ref[frames + local] if local < 0 else high_ref[local]
        row(low, keep * has_low.astype(F32), 0, f, 0)
        row(high, keep * has_high.astype(F32), 1, f, rows + 1)


def packed(value):
    per = value.shape[0] - TILE
    total = value[per : per + 1] + value[per + 1 : per + 2] + value[per + 2 : per + 3]
    top = total.astype(BF16).astype(F32)
    mid = (total - top).astype(BF16).astype(F32)
    rest = total - top - mid
    tail = jnp.concatenate([top, mid, rest, jnp.zeros((TILE - 3, value.shape[1]), F32)], axis=0)
    return jnp.concatenate([value[:per].astype(BF16), tail.astype(BF16)], axis=0)


def weights_kernel(info_ref, turned_ref, act_ref, bias_ref, keep_ref, *refs):
    send_refs, acc = refs[:-2], refs[-2:]
    acc, shards = acc
    frames, rows = turned_ref.shape[:2]
    chans = turned_ref.shape[2]
    k = turned_ref.shape[3]
    step = act_ref.shape[2] - 2
    taps = [(kt, ky, kx) for kt in range(3) for ky in range(3) for kx in range(3)]
    pair = 2

    def frame(t, carry):
        left = jnp.concatenate([turned_ref[t, y] for y in range(rows)], axis=1)
        for j in range(0, len(taps), pair):
            chosen = taps[j : j + pair]
            right = jnp.concatenate(
                [
                    act_ref[t + kt, ky : ky + rows, kx : kx + step].reshape(rows * k, chans)
                    for kt, ky, kx in chosen
                ],
                axis=1,
            )
            product = jnp.dot(left, right, preferred_element_type=F32)
            where = slice(j * chans, (j + len(chosen)) * chans)
            acc[:, where] = jnp.where(t == 0, product, acc[:, where] + product)
        return carry

    lax.fori_loop(0, frames, frame, 0)
    tms, dps, per = shards.shape[:3]
    per -= TILE
    for tap in range(len(taps)):
        block = acc[:, tap * chans : (tap + 1) * chans].T
        done = 0
        while done < chans:
            shard, at = divmod(tap * chans + done, per)
            take = min(chans - done, per - at)
            shards[shard // dps, shard % dps, at : at + take, :] = block[done : done + take]
            done += take
    tail = jnp.concatenate([bias_ref[0:1], jnp.zeros((TILE - 1, chans), F32)], axis=0)
    for i in range(tms):
        for j in range(dps):
            shards[i, j, per : per + TILE, :] = tail
    me = info_ref[4]
    keep_ref[...] = shards[me]
    for r in range(1, tms):
        send_refs[r - 1][...] = shards[me ^ r]


def spread_kernel(count, info_ref, after_ref, keep_ref, *refs):
    incoming, own_ref, send_refs = refs[:count], refs[count], refs[count + 1 :]
    me = info_ref[5]
    for r in range(len(send_refs) + 1):
        value = keep_ref[me ^ r]
        for ref in incoming:
            value = value + ref[me ^ r]
        if r == 0:
            own_ref[...] = value
        else:
            send_refs[r - 1][...] = packed(value)


def add_kernel(after_ref, *refs):
    values = [ref[...].astype(F32) for ref in refs[:-1]]
    while len(values) > 1:
        values = [sum(values[n : n + 2]) for n in range(0, len(values), 2)]
    refs[-1][...] = packed(values[0])


def taps_kernel(after_ref, kernel_ref, out_ref):
    kts, kys, kxs, chans = kernel_ref.shape[:4]
    pair = out_ref.shape[1] // chans
    zero = jnp.zeros((kys * kxs * chans, chans), BF16)
    span = kys * kxs * chans
    for f in range(kts + pair - 1):
        for g in range(pair):
            if 0 <= f - g < kts:
                value = kernel_ref[f - g].reshape(span, chans)
            else:
                value = zero
            out_ref[f * span : (f + 1) * span, g * chans : (g + 1) * chans] = value


def conv_kernel(
    piece, last, info_ref, after_ref, act_ref, taps_ref, video_ref, bias_ref, *refs
):
    out_ref, whole_ref, wide, sem = refs[-4:]
    t0, y0 = piece
    rows = out_ref.shape[1]
    if last is not None:
        out = pltpu.make_async_copy(refs[0], whole_ref.at[last], sem)
        out.start()
    cols, chans = out_ref.shape[2:]
    step = cols // TILE
    pair = taps_ref.shape[1] // chans
    used = [
        (f, ky, kx)
        for f in range(taps_ref.shape[0] // (9 * chans))
        for ky in range(3)
        for kx in range(3)
    ]
    left = jnp.concatenate(
        [
            act_ref[t0 + f, y0 + ky : y0 + ky + rows, kx : kx + step].reshape(rows * cols, chans)
            for f, ky, kx in used
        ],
        axis=1,
    )
    result = jnp.dot(left, taps_ref[...], preferred_element_type=F32)
    for f in range(pair):
        keep = (t0 + f < info_ref[0]).astype(F32)
        for y in range(rows):
            slot = f * rows + y
            for r in range(step):
                at = y * cols + r * TILE
                wide[slot, pl.ds(r, TILE, stride=step), :] = result[
                    at : at + TILE, f * chans : (f + 1) * chans
                ]
            value = video_ref[0, t0 + f, y0 + y].astype(F32) + wide[slot] + bias_ref[...]
            out_ref[f, y] = (value * keep).astype(BF16)
    if last is not None:
        out.wait()


def step_of(video, lengths, norm_gain, norm_shift, kernel, conv_bias, cotangent):
    frames, rows, cols, chans = video.shape[1:]
    per = chans // GROUPS
    step = cols // TILE
    before = kernel.shape[0] - 1
    tms, dps, spaces = (lax.axis_size(axis) for axis in ("tm", "dp", "space"))
    tm, dp, space = (lax.axis_index(axis) for axis in ("tm", "dp", "space"))
    first = tm * frames
    inside = jnp.clip(lengths[0] - first, -before, frames)
    info = jnp.stack(
        [
            inside,
            first,
            (space > 0).astype(jnp.int32),
            (space < spaces - 1).astype(jnp.int32),
            tm,
            dp,
        ]
    ).astype(jnp.int32)

    source = pltpu.with_memory_space_constraint(video, pltpu.HBM)
    border = jax.ShapeDtypeStruct((frames, cols, chans), BF16)
    edge_low, edge_high = pl.pallas_call(
        ends_kernel,
        in_specs=[ANY],
        out_specs=[VMEM, VMEM],
        out_shape=[border, border],
        scratch_shapes=[pltpu.SemaphoreType.DMA((2,))],
        compiler_params=params(1),
        name="ends",
    )(source)
    low = shifted(edge_low, "space", 1)
    high = shifted(edge_high, "space", -1)
    stats, local, masked_in, tail = pl.pallas_call(
        functools.partial(stats_kernel, per, before),
        in_specs=[SMEM, ANY, ANY],
        out_specs=[VMEM] * 4,
        out_shape=[
            jax.ShapeDtypeStruct((8, chans), F32),
            jax.ShapeDtypeStruct(video.shape, BF16),
            jax.ShapeDtypeStruct(cotangent.shape, BF16),
            jax.ShapeDtypeStruct((1, before, rows, cols, chans), BF16),
        ],
        scratch_shapes=[pltpu.SemaphoreType.DMA((2 * frames + 1 + before,))],
        compiler_params=params(2),
        name="stats",
    )(info, source, pltpu.with_memory_space_constraint(cotangent, pltpu.HBM))
    following = [(i, (i + 1) % tms) for i in range(tms)]
    gathered = [stats] + [swap(stats, "tm", r) for r in range(1, tms)]
    early = lax.ppermute(tail, "tm", following)
    stats = pl.pallas_call(
        merge_kernel,
        in_specs=[VMEM] * tms,
        out_specs=VMEM,
        out_shape=jax.ShapeDtypeStruct((8, chans), F32),
        compiler_params=params(1),
        name="merge",
    )(*gathered)
    parts = [stats] + [swap(stats, "space", r) for r in range(1, spaces)]
    low_early = lax.ppermute(low, "tm", following)
    high_early = lax.ppermute(high, "tm", following)
    pair = 2
    taps = pl.pallas_call(
        taps_kernel,
        in_specs=[ANY, VMEM],
        out_specs=VMEM,
        out_shape=jax.ShapeDtypeStruct(
            ((kernel.shape[0] + pair - 1) * 9 * chans, pair * chans), BF16
        ),
        compiler_params=params(2),
        name="taps",
    )(stats, kernel)

    turned, bias = pl.pallas_call(
        cotangent_kernel,
        in_specs=[SMEM, VMEM],
        out_specs=[VMEM, VMEM],
        out_shape=[
            jax.ShapeDtypeStruct((frames, rows, chans, cols), BF16),
            jax.ShapeDtypeStruct((8, chans), F32),
        ],
        scratch_shapes=[pltpu.VMEM((8, cols, chans), F32)],
        compiler_params=params(4),
        name="cotangent",
    )(info, masked_in)

    act = pl.pallas_call(
        functools.partial(activate_kernel, spaces),
        in_specs=[SMEM] + [VMEM] * (8 + spaces),
        out_specs=VMEM,
        out_shape=jax.ShapeDtypeStruct(
            (frames + before, rows + 2, step + 2, TILE, chans), BF16
        ),
        scratch_shapes=[pltpu.VMEM((4, cols + 16, chans), F32)],
        compiler_params=params(8),
        name="activate",
    )(
        info,
        local,
        early,
        low,
        high,
        low_early,
        high_early,
        norm_gain.reshape(1, chans),
        norm_shift.reshape(1, chans),
        *parts,
    )

    count = kernel.shape[0] * kernel.shape[1] * kernel.shape[2] * chans
    shards_n = tms * dps
    assert count % shards_n == 0
    shard = count // shards_n
    full = shard + TILE
    keep, *sends = pl.pallas_call(
        weights_kernel,
        in_specs=[SMEM, VMEM, VMEM, VMEM],
        out_specs=[VMEM] * tms,
        out_shape=[jax.ShapeDtypeStruct((dps, full, chans), F32)] * tms,
        scratch_shapes=[
            pltpu.VMEM((chans, count), F32),
            pltpu.VMEM((tms, dps, full, chans), F32),
        ],
        compiler_params=params(16),
        name="weights",
    )(info, turned, act, bias)

    block = 4
    pieces = [(t0, y0) for t0 in range(0, frames, pair) for y0 in range(0, rows, block)]
    done = []

    whole = jax.ShapeDtypeStruct(video.shape, BF16)

    def where(n):
        t0, y0 = pieces[n]
        return 0, pl.ds(t0, pair), pl.ds(y0, block)

    def cover(after, number):
        for _ in range(min(number, len(pieces) - len(done))):
            n = len(done)
            made = list(done[-1]) if done else []
            piece, output = pl.pallas_call(
                functools.partial(conv_kernel, pieces[n], where(n - 1) if made else None),
                in_specs=[SMEM, ANY, VMEM, VMEM, VMEM, VMEM] + [VMEM, ANY][: len(made)],
                out_specs=[VMEM, ANY],
                out_shape=[jax.ShapeDtypeStruct((pair, block, cols, chans), BF16), whole],
                scratch_shapes=[
                    pltpu.VMEM((pair * block, cols, chans), F32),
                    pltpu.SemaphoreType.DMA,
                ],
                input_output_aliases={7: 1} if made else {},
                compiler_params=params(6),
                name="conv",
            )(info, after, act, taps, local, conv_bias.reshape(1, chans), *made)
            done.append((piece, output))
            after = piece
        return after

    incoming = [swap(send, "tm", r + 1) for r, send in enumerate(sends)]
    token = cover(keep, 1)
    own, *sends = pl.pallas_call(
        functools.partial(spread_kernel, len(incoming)),
        in_specs=[SMEM, ANY] + [VMEM] * (1 + len(incoming)),
        out_specs=[VMEM] * dps,
        out_shape=[jax.ShapeDtypeStruct((full, chans), F32)]
        + [jax.ShapeDtypeStruct((full, chans), BF16)] * (dps - 1),
        compiler_params=params(4),
        name="spread",
    )(info, token, keep, *incoming)

    def added(dtype, after, *arrays):
        return pl.pallas_call(
            add_kernel,
            in_specs=[ANY] + [VMEM] * len(arrays),
            out_specs=VMEM,
            out_shape=jax.ShapeDtypeStruct((full, chans), dtype),
            compiler_params=params(2),
            name="added",
        )(after, *arrays)

    incoming = [swap(send, "dp", r + 1) for r, send in enumerate(sends)]
    token = cover(own, 3)
    total = added(BF16, token, own, *incoming)
    others = [swap(total, "space", r) for r in range(1, spaces)]
    token = cover(total, 3)
    total = added(BF16, token, total, *others)
    mine = [total] + [swap(total, "dp", r) for r in range(1, dps)]
    cover(total, len(pieces))
    shards = {(0, r): array for r, array in enumerate(mine)}
    for q in range(1, tms):
        for r, array in enumerate(mine):
            shards[q, r] = swap(array, "tm", q)
    order = list(shards)

    def collect(info_ref, *refs):
        shard_refs, piece_ref = refs[: len(order)], refs[len(order)]
        out_ref, sum_ref, whole_ref, sem = refs[-4:]
        copy = pltpu.make_async_copy(piece_ref, whole_ref.at[where(len(pieces) - 1)], sem)
        copy.start()
        for (q, r), ref in zip(order, shard_refs):
            at = (info_ref[4] ^ q) * dps + (info_ref[5] ^ r)
            out_ref[at] = ref[0:shard, :].astype(F32)
        tail = shard_refs[0][shard : shard + TILE, :].astype(F32)
        sum_ref[...] = tail[0:1] + tail[1:2] + tail[2:3]
        copy.wait()

    grad_kernel, grad_bias, output = pl.pallas_call(
        collect,
        in_specs=[SMEM] + [VMEM] * (len(order) + 1) + [ANY],
        out_specs=[VMEM, VMEM, ANY],
        out_shape=[
            jax.ShapeDtypeStruct((shards_n, shard, chans), F32),
            jax.ShapeDtypeStruct((1, chans), F32),
            whole,
        ],
        scratch_shapes=[pltpu.SemaphoreType.DMA],
        input_output_aliases={len(order) + 2: 2},
        compiler_params=params(4),
        name="collect",
    )(info, *[shards[key] for key in order], *done[-1])

    return output, grad_kernel.reshape(kernel.shape), grad_bias.reshape(chans)


def solution(mesh):
    return jax.shard_map(
        step_of,
        mesh=mesh,
        in_specs=(
            P("dp", "tm", "space", None, None),
            P("dp"),
            P(),
            P(),
            P(),
            P(),
            P("dp", "tm", "space", None, None),
        ),
        out_specs=(P("dp", "tm", "space", None, None), P(), P()),
        check_vma=False,
    )
```

```python
import functools

import jax
import jax.numpy as jnp
from jax import lax
from jax.experimental import pallas as pl
from jax.experimental.pallas import tpu as pltpu
from jax.sharding import PartitionSpec as P


GROUPS = 32
TILE = 16
F32 = jnp.float32
BF16 = jnp.bfloat16
VMEM = pl.BlockSpec(memory_space=pltpu.VMEM)
ANY = pl.BlockSpec(memory_space=pl.ANY)
SMEM = pl.BlockSpec(memory_space=pltpu.SMEM)


def params(mib):
    return pltpu.CompilerParams(vmem_limit_bytes=mib * 1024 * 1024)


def swap(array, axis, by):
    length = lax.axis_size(axis)
    assert length & (length - 1) == 0
    return lax.ppermute(array, axis, [(i, i ^ by) for i in range(length)])


def group_sum(row, per):
    value = jnp.broadcast_to(row, (8, row.shape[1]))
    lane = lax.broadcasted_iota(jnp.int32, value.shape, 1)
    size = value.shape[1]
    step = 1
    while step < per:
        up = pltpu.roll(value, size - step, 1)
        down = pltpu.roll(value, step, 1)
        value = value + jnp.where((lane & step) == 0, up, down)
        step *= 2
    return value[0:1]


def merged(parts):
    count = sum(part[0] for part in parts)
    total = sum(part[1] for part in parts)
    mean = total / jnp.maximum(count, 1.0)
    squares = jnp.zeros_like(mean)
    for part in parts:
        away = part[1] / jnp.maximum(part[0], 1.0) - mean
        squares = squares + (part[2] + part[0] * (away * away))
    return count, total, squares


def ends_kernel(info_ref, video_hbm, near_ref, far_ref, sems):
    rows = video_hbm.shape[2]
    odd = info_ref[6]
    copies = [
        pltpu.make_async_copy(video_hbm.at[0, :, row], ref, sems.at[n])
        for n, (row, ref) in enumerate(
            (((1 - odd) * (rows - 1), near_ref), (odd * (rows - 1), far_ref))
        )
    ]
    for copy in copies:
        copy.start()
    for copy in copies:
        copy.wait()


def stats_kernel(before, info_ref, video_hbm, cot_hbm, *refs):
    out_ref, video_ref, cot_ref, tail_ref, sems = refs
    frames, rows, cols, chans = video_ref.shape[1:]
    parts_n = 2 * frames
    some = rows // 2
    first = frames - before
    copies = []
    for n in range(parts_n):
        at = (0, n // 2, pl.ds(n % 2 * some, some))
        copies.append(pltpu.make_async_copy(video_hbm.at[at], video_ref.at[at], sems.at[n]))
        copies[-1].start()
    later = [pltpu.make_async_copy(cot_hbm, cot_ref, sems.at[parts_n])]
    later[0].start()
    size = float(some * cols // 8)
    lanes = 4
    split = (cols // (8 * lanes), lanes, 8, chans)
    start = jnp.zeros((lanes, 8, chans), F32)
    parts = []
    for n in range(parts_n):
        copies[n].wait()
        f, y0 = n // 2, n % 2 * some
        if n % 2 and f >= first:
            sem = sems.at[parts_n + 1 + f - first]
            later.append(pltpu.make_async_copy(video_ref.at[0, f], tail_ref.at[0, f - first], sem))
            later[-1].start()

        def add(y, acc, f=f, y0=y0):
            return acc + jnp.sum(video_ref[0, f, y0 + y].astype(F32).reshape(split), axis=0)

        total = jnp.sum(lax.fori_loop(0, some, add, start, unroll=8), axis=0)
        mean = total / size

        def deviate(y, acc, f=f, y0=y0, mean=mean):
            away = video_ref[0, f, y0 + y].astype(F32).reshape(split) - mean
            return acc + jnp.sum(away * away, axis=0)

        squares = jnp.sum(lax.fori_loop(0, some, deviate, start, unroll=8), axis=0)
        keep = (f < info_ref[0]).astype(F32)
        parts.append((jnp.full((8, chans), size, F32) * keep, total * keep, squares * keep))
    for n, value in enumerate(merged(parts)):
        out_ref[n] = value
    for copy in later:
        copy.wait()


def merge_kernel(*refs):
    for n, value in enumerate(merged([ref[...] for ref in refs[:-1]])):
        refs[-1][n] = value


def cotangent_kernel(info_ref, cot_ref, turned_ref, bias_ref, wide):
    frames, rows, cols, chans = cot_ref.shape[1:]
    step = cols // TILE
    lanes = 4
    bias = jnp.zeros((lanes, 8, chans), F32)
    for t in range(frames):
        keep = (t < info_ref[0]).astype(F32)

        def row(y, acc, t=t, keep=keep):
            value = cot_ref[0, t, y].astype(F32) * keep
            slot = wide.at[y % wide.shape[0]]
            slot[...] = value
            order = jnp.concatenate(
                [slot[pl.ds(r, TILE, stride=step), :] for r in range(step)], axis=0
            )
            turned_ref[t, y] = order.astype(BF16).T
            return acc + jnp.sum(value.reshape(cols // (8 * lanes), lanes, 8, chans), axis=0)

        bias = lax.fori_loop(0, rows, row, bias, unroll=8)
    total = jnp.sum(jnp.sum(bias, axis=0), axis=0, keepdims=True)
    bias_ref[...] = jnp.broadcast_to(total, bias_ref.shape)


def activate_kernel(
    parts_n, per, info_ref, video_ref, early_ref, near_ref, far_ref, near_early_ref, *refs
):
    far_early_ref, gain_ref, shift_ref, *refs = refs
    parts, out_ref, wide = refs[:parts_n], refs[parts_n], refs[parts_n + 1]
    frames, rows, cols, chans = video_ref.shape[1:]
    before = early_ref.shape[1]
    step = cols // TILE
    inside, first, has_low, has_high = info_ref[0], info_ref[1], info_ref[2], info_ref[3]
    count, total, squares = merged([ref[...] for ref in parts])
    every = jnp.sum(count, axis=0, keepdims=True) * per
    mean = group_sum(jnp.sum(total, axis=0, keepdims=True), per) / every
    away = total / jnp.maximum(count, 1.0) - mean
    squares = jnp.sum(squares + count * (away * away), axis=0, keepdims=True)
    squares = group_sum(squares, per)
    odd = info_ref[6] == 1
    scale = 0.5 * lax.rsqrt(squares / every + 1e-05) * gain_ref[...]
    offset = 0.5 * shift_ref[...] - mean * scale
    slots = wide.shape[0]
    wide[:, 0:8, :] = jnp.zeros((slots, 8, chans), F32)
    wide[:, 8 + cols : 16 + cols, :] = jnp.zeros((slots, 8, chans), F32)

    def row(values, keep, slot, f, y):
        half = values.astype(F32) * (scale * keep) + offset * keep
        wide[slot, 8 : 8 + cols, :] = half + half * jnp.tanh(half)
        for r in range(-1, step + 1):
            out_ref[f, y, r + 1] = wide[slot, pl.ds(8 + r, TILE, stride=step), :].astype(BF16)

    for f in range(frames + before):
        local = f - before
        ok = (local < inside) & (first + local >= 0)
        keep = ok.astype(F32)
        source = early_ref.at[0, f] if local < 0 else video_ref.at[0, local]

        def inner(y, carry, source=source, keep=keep, f=f):
            row(source[y], keep, y % slots, f, y + 1)
            return carry

        lax.fori_loop(0, rows, inner, 0, unroll=4)
        near = near_early_ref[frames + local] if local < 0 else near_ref[local]
        far = far_early_ref[frames + local] if local < 0 else far_ref[local]
        near, far = near.astype(F32), far.astype(F32)
        low, high = jnp.where(odd, near, far), jnp.where(odd, far, near)
        row(low, keep * has_low.astype(F32), 0, f, 0)
        row(high, keep * has_high.astype(F32), 1, f, rows + 1)


def packed(value):
    per = value.shape[0] - TILE
    total = value[per : per + 1] + value[per + 1 : per + 2] + value[per + 2 : per + 3]
    top = total.astype(BF16).astype(F32)
    mid = (total - top).astype(BF16).astype(F32)
    rest = total - top - mid
    tail = jnp.concatenate([top, mid, rest, jnp.zeros((TILE - 3, value.shape[1]), F32)], axis=0)
    return jnp.concatenate([value[:per].astype(BF16), tail.astype(BF16)], axis=0)


def weights_kernel(info_ref, turned_ref, act_ref, bias_ref, keep_ref, *refs):
    send_refs, acc = refs[:-2], refs[-2:]
    acc, shards = acc
    frames, rows = turned_ref.shape[:2]
    chans = turned_ref.shape[2]
    k = turned_ref.shape[3]
    step = act_ref.shape[2] - 2
    taps = [(kt, ky, kx) for kt in range(3) for ky in range(3) for kx in range(3)]
    pair = 2

    def frame(t, carry):
        left = jnp.concatenate([turned_ref[t, y] for y in range(rows)], axis=1)
        for j in range(0, len(taps), pair):
            chosen = taps[j : j + pair]
            right = jnp.concatenate(
                [
                    act_ref[t + kt, ky : ky + rows, kx : kx + step].reshape(rows * k, chans)
                    for kt, ky, kx in chosen
                ],
                axis=1,
            )
            product = jnp.dot(left, right, preferred_element_type=F32)
            where = slice(j * chans, (j + len(chosen)) * chans)
            acc[:, where] = jnp.where(t == 0, product, acc[:, where] + product)
        return carry

    lax.fori_loop(0, frames, frame, 0)
    tms, dps, per = shards.shape[:3]
    per -= TILE
    for tap in range(len(taps)):
        block = acc[:, tap * chans : (tap + 1) * chans].T
        done = 0
        while done < chans:
            shard, at = divmod(tap * chans + done, per)
            take = min(chans - done, per - at)
            shards[shard // dps, shard % dps, at : at + take, :] = block[done : done + take]
            done += take
    tail = jnp.concatenate([bias_ref[0:1], jnp.zeros((TILE - 1, chans), F32)], axis=0)
    for i in range(tms):
        for j in range(dps):
            shards[i, j, per : per + TILE, :] = tail
    me = info_ref[4]
    keep_ref[...] = shards[me]
    for r in range(1, tms):
        send_refs[r - 1][...] = shards[me ^ r]


def spread_kernel(count, info_ref, after_ref, keep_ref, *refs):
    incoming, own_ref, send_refs = refs[:count], refs[count], refs[count + 1 :]
    me = info_ref[5]
    for r in range(len(send_refs) + 1):
        value = keep_ref[me ^ r]
        for ref in incoming:
            value = value + ref[me ^ r]
        if r == 0:
            own_ref[...] = value
        else:
            send_refs[r - 1][...] = packed(value)


def add_kernel(after_ref, *refs):
    values = [ref[...].astype(F32) for ref in refs[:-1]]
    while len(values) > 1:
        values = [sum(values[n : n + 2]) for n in range(0, len(values), 2)]
    refs[-1][...] = packed(values[0])


def taps_kernel(after_ref, kernel_ref, out_ref):
    kts, kys, kxs, chans = kernel_ref.shape[:4]
    pair = out_ref.shape[1] // chans
    zero = jnp.zeros((kys * kxs * chans, chans), BF16)
    span = kys * kxs * chans
    for f in range(kts + pair - 1):
        for g in range(pair):
            if 0 <= f - g < kts:
                value = kernel_ref[f - g].reshape(span, chans)
            else:
                value = zero
            out_ref[f * span : (f + 1) * span, g * chans : (g + 1) * chans] = value


def conv_kernel(
    piece, last, info_ref, after_ref, act_ref, taps_ref, video_ref, bias_ref, *refs
):
    out_ref, whole_ref, wide, sem = refs[-4:]
    t0, y0 = piece
    rows = out_ref.shape[1]
    if last is not None:
        out = pltpu.make_async_copy(refs[0], whole_ref.at[last], sem)
        out.start()
    cols, chans = out_ref.shape[2:]
    step = cols // TILE
    pair = taps_ref.shape[1] // chans
    used = [
        (f, ky, kx)
        for f in range(taps_ref.shape[0] // (9 * chans))
        for ky in range(3)
        for kx in range(3)
    ]
    left = jnp.concatenate(
        [
            act_ref[t0 + f, y0 + ky : y0 + ky + rows, kx : kx + step].reshape(rows * cols, chans)
            for f, ky, kx in used
        ],
        axis=1,
    )
    result = jnp.dot(left, taps_ref[...], preferred_element_type=F32)
    for f in range(pair):
        keep = (t0 + f < info_ref[0]).astype(F32)
        for y in range(rows):
            slot = f * rows + y
            for r in range(step):
                at = y * cols + r * TILE
                wide[slot, pl.ds(r, TILE, stride=step), :] = result[
                    at : at + TILE, f * chans : (f + 1) * chans
                ]
            value = video_ref[0, t0 + f, y0 + y].astype(F32) + wide[slot] + bias_ref[...]
            out_ref[f, y] = (value * keep).astype(BF16)
    if last is not None:
        out.wait()


def step_of(video, lengths, norm_gain, norm_shift, kernel, conv_bias, cotangent):
    frames, rows, cols, chans = video.shape[1:]
    per = chans // GROUPS
    step = cols // TILE
    before = kernel.shape[0] - 1
    tms, dps, spaces = (lax.axis_size(axis) for axis in ("tm", "dp", "space"))
    tm, dp, space = (lax.axis_index(axis) for axis in ("tm", "dp", "space"))
    first = tm * frames
    inside = jnp.clip(lengths[0] - first, -before, frames)
    info = jnp.stack(
        [
            inside,
            first,
            (space > 0).astype(jnp.int32),
            (space < spaces - 1).astype(jnp.int32),
            tm,
            dp,
            space % 2,
        ]
    ).astype(jnp.int32)

    source = pltpu.with_memory_space_constraint(video, pltpu.HBM)
    border = jax.ShapeDtypeStruct((frames, cols, chans), BF16)
    near, far = pl.pallas_call(
        ends_kernel,
        in_specs=[SMEM, ANY],
        out_specs=[VMEM, VMEM],
        out_shape=[border, border],
        scratch_shapes=[pltpu.SemaphoreType.DMA((2,))],
        compiler_params=params(1),
        name="ends",
    )(info, source)
    near = swap(near, "space", 1)
    between = [(i, i + 1) for i in range(1, spaces - 1, 2)]
    far = lax.ppermute(far, "space", between + [(j, i) for i, j in between])
    stats, local, masked_in, tail = pl.pallas_call(
        functools.partial(stats_kernel, before),
        in_specs=[SMEM, ANY, ANY],
        out_specs=[VMEM] * 4,
        out_shape=[
            jax.ShapeDtypeStruct((3, 8, chans), F32),
            jax.ShapeDtypeStruct(video.shape, BF16),
            jax.ShapeDtypeStruct(cotangent.shape, BF16),
            jax.ShapeDtypeStruct((1, before, rows, cols, chans), BF16),
        ],
        scratch_shapes=[pltpu.SemaphoreType.DMA((2 * frames + 1 + before,))],
        compiler_params=params(2),
        name="stats",
    )(info, source, pltpu.with_memory_space_constraint(cotangent, pltpu.HBM))
    following = [(i, (i + 1) % tms) for i in range(tms)]
    gathered = [stats] + [swap(stats, "tm", r) for r in range(1, tms)]
    early = lax.ppermute(tail, "tm", following)
    stats = pl.pallas_call(
        merge_kernel,
        in_specs=[VMEM] * tms,
        out_specs=VMEM,
        out_shape=jax.ShapeDtypeStruct((3, 8, chans), F32),
        compiler_params=params(1),
        name="merge",
    )(*gathered)
    parts = [stats] + [swap(stats, "space", r) for r in range(1, spaces)]
    near_early = lax.ppermute(near, "tm", following)
    far_early = lax.ppermute(far, "tm", following)
    pair = 2
    taps = pl.pallas_call(
        taps_kernel,
        in_specs=[ANY, VMEM],
        out_specs=VMEM,
        out_shape=jax.ShapeDtypeStruct(
            ((kernel.shape[0] + pair - 1) * 9 * chans, pair * chans), BF16
        ),
        compiler_params=params(2),
        name="taps",
    )(stats, kernel)

    turned, bias = pl.pallas_call(
        cotangent_kernel,
        in_specs=[SMEM, VMEM],
        out_specs=[VMEM, VMEM],
        out_shape=[
            jax.ShapeDtypeStruct((frames, rows, chans, cols), BF16),
            jax.ShapeDtypeStruct((8, chans), F32),
        ],
        scratch_shapes=[pltpu.VMEM((8, cols, chans), F32)],
        compiler_params=params(4),
        name="cotangent",
    )(info, masked_in)

    act = pl.pallas_call(
        functools.partial(activate_kernel, spaces, per),
        in_specs=[SMEM] + [VMEM] * (8 + spaces),
        out_specs=VMEM,
        out_shape=jax.ShapeDtypeStruct(
            (frames + before, rows + 2, step + 2, TILE, chans), BF16
        ),
        scratch_shapes=[pltpu.VMEM((4, cols + 16, chans), F32)],
        compiler_params=params(8),
        name="activate",
    )(
        info,
        local,
        early,
        near,
        far,
        near_early,
        far_early,
        norm_gain.reshape(1, chans),
        norm_shift.reshape(1, chans),
        *parts,
    )

    count = kernel.shape[0] * kernel.shape[1] * kernel.shape[2] * chans
    shards_n = tms * dps
    assert count % shards_n == 0
    shard = count // shards_n
    full = shard + TILE
    keep, *sends = pl.pallas_call(
        weights_kernel,
        in_specs=[SMEM, VMEM, VMEM, VMEM],
        out_specs=[VMEM] * tms,
        out_shape=[jax.ShapeDtypeStruct((dps, full, chans), F32)] * tms,
        scratch_shapes=[
            pltpu.VMEM((chans, count), F32),
            pltpu.VMEM((tms, dps, full, chans), F32),
        ],
        compiler_params=params(16),
        name="weights",
    )(info, turned, act, bias)

    block = 4
    pieces = [(t0, y0) for t0 in range(0, frames, pair) for y0 in range(0, rows, block)]
    done = []

    whole = jax.ShapeDtypeStruct(video.shape, BF16)

    def where(n):
        t0, y0 = pieces[n]
        return 0, pl.ds(t0, pair), pl.ds(y0, block)

    def cover(after, number):
        for _ in range(min(number, len(pieces) - len(done))):
            n = len(done)
            made = list(done[-1]) if done else []
            piece, output = pl.pallas_call(
                functools.partial(conv_kernel, pieces[n], where(n - 1) if made else None),
                in_specs=[SMEM, ANY, VMEM, VMEM, VMEM, VMEM] + [VMEM, ANY][: len(made)],
                out_specs=[VMEM, ANY],
                out_shape=[jax.ShapeDtypeStruct((pair, block, cols, chans), BF16), whole],
                scratch_shapes=[
                    pltpu.VMEM((pair * block, cols, chans), F32),
                    pltpu.SemaphoreType.DMA,
                ],
                input_output_aliases={7: 1} if made else {},
                compiler_params=params(6),
                name="conv",
            )(info, after, act, taps, local, conv_bias.reshape(1, chans), *made)
            done.append((piece, output))
            after = piece
        return after

    incoming = [swap(send, "tm", r + 1) for r, send in enumerate(sends)]
    token = cover(keep, 1)
    own, *sends = pl.pallas_call(
        functools.partial(spread_kernel, len(incoming)),
        in_specs=[SMEM, ANY] + [VMEM] * (1 + len(incoming)),
        out_specs=[VMEM] * dps,
        out_shape=[jax.ShapeDtypeStruct((full, chans), F32)]
        + [jax.ShapeDtypeStruct((full, chans), BF16)] * (dps - 1),
        compiler_params=params(4),
        name="spread",
    )(info, token, keep, *incoming)

    def added(dtype, after, *arrays):
        return pl.pallas_call(
            add_kernel,
            in_specs=[ANY] + [VMEM] * len(arrays),
            out_specs=VMEM,
            out_shape=jax.ShapeDtypeStruct((full, chans), dtype),
            compiler_params=params(2),
            name="added",
        )(after, *arrays)

    incoming = [swap(send, "dp", r + 1) for r, send in enumerate(sends)]
    token = cover(own, 3)
    total = added(BF16, token, own, *incoming)
    others = [swap(total, "space", r) for r in range(1, spaces)]
    token = cover(total, 3)
    total = added(BF16, token, total, *others)
    mine = [total] + [swap(total, "dp", r) for r in range(1, dps)]
    cover(total, len(pieces))
    shards = {(0, r): array for r, array in enumerate(mine)}
    for q in range(1, tms):
        for r, array in enumerate(mine):
            shards[q, r] = swap(array, "tm", q)
    order = list(shards)

    def collect(info_ref, *refs):
        shard_refs, piece_ref = refs[: len(order)], refs[len(order)]
        out_ref, sum_ref, whole_ref, sem = refs[-4:]
        copy = pltpu.make_async_copy(piece_ref, whole_ref.at[where(len(pieces) - 1)], sem)
        copy.start()
        for (q, r), ref in zip(order, shard_refs):
            at = (info_ref[4] ^ q) * dps + (info_ref[5] ^ r)
            out_ref[at] = ref[0:shard, :].astype(F32)
        tail = shard_refs[0][shard : shard + TILE, :].astype(F32)
        sum_ref[...] = tail[0:1] + tail[1:2] + tail[2:3]
        copy.wait()

    grad_kernel, grad_bias, output = pl.pallas_call(
        collect,
        in_specs=[SMEM] + [VMEM] * (len(order) + 1) + [ANY],
        out_specs=[VMEM, VMEM, ANY],
        out_shape=[
            jax.ShapeDtypeStruct((shards_n, shard, chans), F32),
            jax.ShapeDtypeStruct((1, chans), F32),
            whole,
        ],
        scratch_shapes=[pltpu.SemaphoreType.DMA],
        input_output_aliases={len(order) + 2: 2},
        compiler_params=params(4),
        name="collect",
    )(info, *[shards[key] for key in order], *done[-1])

    return output, grad_kernel.reshape(kernel.shape), grad_bias.reshape(chans)


def solution(mesh):
    return jax.shard_map(
        step_of,
        mesh=mesh,
        in_specs=(
            P("dp", "tm", "space", None, None),
            P("dp"),
            P(),
            P(),
            P(),
            P(),
            P("dp", "tm", "space", None, None),
        ),
        out_specs=(P("dp", "tm", "space", None, None), P(), P()),
        check_vma=False,
    )
```

```python
import functools

import jax
import jax.numpy as jnp
from jax import lax
from jax.experimental import pallas as pl
from jax.experimental.pallas import tpu as pltpu
from jax.sharding import PartitionSpec as P


GROUPS = 32
TILE = 16
F32 = jnp.float32
BF16 = jnp.bfloat16
VMEM = pl.BlockSpec(memory_space=pltpu.VMEM)
ANY = pl.BlockSpec(memory_space=pl.ANY)
SMEM = pl.BlockSpec(memory_space=pltpu.SMEM)


def params(mib):
    return pltpu.CompilerParams(vmem_limit_bytes=mib * 1024 * 1024)


def swap(array, axis, by):
    length = lax.axis_size(axis)
    assert length & (length - 1) == 0
    return lax.ppermute(array, axis, [(i, i ^ by) for i in range(length)])


def group_sum(row, per):
    value = jnp.broadcast_to(row, (8, row.shape[1]))
    lane = lax.broadcasted_iota(jnp.int32, value.shape, 1)
    size = value.shape[1]
    step = 1
    while step < per:
        up = pltpu.roll(value, size - step, 1)
        down = pltpu.roll(value, step, 1)
        value = value + jnp.where((lane & step) == 0, up, down)
        step *= 2
    return value[0:1]


def merged(parts):
    count = sum(part[0] for part in parts)
    total = sum(part[1] for part in parts)
    mean = total / jnp.maximum(count, 1.0)
    squares = jnp.zeros_like(mean)
    for part in parts:
        away = part[1] / jnp.maximum(part[0], 1.0) - mean
        squares = squares + (part[2] + part[0] * (away * away))
    return count, total, squares


def ends_kernel(info_ref, video_hbm, near_ref, far_ref, sems):
    rows = video_hbm.shape[2]
    odd = info_ref[6]
    copies = [
        pltpu.make_async_copy(video_hbm.at[0, :, row], ref, sems.at[n])
        for n, (row, ref) in enumerate(
            (((1 - odd) * (rows - 1), near_ref), (odd * (rows - 1), far_ref))
        )
    ]
    for copy in copies:
        copy.start()
    for copy in copies:
        copy.wait()


def stats_kernel(before, info_ref, video_hbm, cot_hbm, *refs):
    out_ref, video_ref, cot_ref, tail_ref, sems = refs
    frames, rows, cols, chans = video_ref.shape[1:]
    parts_n = 2 * frames
    some = rows // 2
    first = frames - before
    copies = []
    for n in range(parts_n):
        at = (0, n // 2, pl.ds(n % 2 * some, some))
        copies.append(pltpu.make_async_copy(video_hbm.at[at], video_ref.at[at], sems.at[n]))
        copies[-1].start()
    later = [pltpu.make_async_copy(cot_hbm, cot_ref, sems.at[parts_n])]
    later[0].start()
    size = float(some * cols // 8)
    lanes = 4
    split = (cols // (8 * lanes), lanes, 8, chans)
    start = jnp.zeros((lanes, 8, chans), F32)
    parts = []
    for n in range(parts_n):
        copies[n].wait()
        f, y0 = n // 2, n % 2 * some
        if n % 2 and f >= first:
            sem = sems.at[parts_n + 1 + f - first]
            later.append(pltpu.make_async_copy(video_ref.at[0, f], tail_ref.at[0, f - first], sem))
            later[-1].start()

        def add(y, acc, f=f, y0=y0):
            return acc + jnp.sum(video_ref[0, f, y0 + y].astype(F32).reshape(split), axis=0)

        total = jnp.sum(lax.fori_loop(0, some, add, start, unroll=8), axis=0)
        mean = total / size

        def deviate(y, acc, f=f, y0=y0, mean=mean):
            away = video_ref[0, f, y0 + y].astype(F32).reshape(split) - mean
            return acc + jnp.sum(away * away, axis=0)

        squares = jnp.sum(lax.fori_loop(0, some, deviate, start, unroll=8), axis=0)
        keep = (f < info_ref[0]).astype(F32)
        parts.append((jnp.full((8, chans), size, F32) * keep, total * keep, squares * keep))
    for n, value in enumerate(merged(parts)):
        out_ref[n] = value
    for copy in later:
        copy.wait()


def merge_kernel(*refs):
    for n, value in enumerate(merged([ref[...] for ref in refs[:-1]])):
        refs[-1][n] = value


def cotangent_kernel(info_ref, cot_ref, turned_ref, bias_ref, wide):
    frames, rows, cols, chans = cot_ref.shape[1:]
    step = cols // TILE
    lanes = 4
    bias = jnp.zeros((lanes, 8, chans), F32)
    for t in range(frames):
        keep = (t < info_ref[0]).astype(F32)

        def row(y, acc, t=t, keep=keep):
            value = cot_ref[0, t, y].astype(F32) * keep
            slot = wide.at[y % wide.shape[0]]
            slot[...] = value
            order = jnp.concatenate(
                [slot[pl.ds(r, TILE, stride=step), :] for r in range(step)], axis=0
            )
            turned_ref[t, y] = order.astype(BF16).T
            return acc + jnp.sum(value.reshape(cols // (8 * lanes), lanes, 8, chans), axis=0)

        bias = lax.fori_loop(0, rows, row, bias, unroll=8)
    total = jnp.sum(jnp.sum(bias, axis=0), axis=0, keepdims=True)
    bias_ref[...] = jnp.broadcast_to(total, bias_ref.shape)


def packed(value):
    per = value.shape[0] - TILE
    total = value[per : per + 1] + value[per + 1 : per + 2] + value[per + 2 : per + 3]
    top = total.astype(BF16).astype(F32)
    mid = (total - top).astype(BF16).astype(F32)
    rest = total - top - mid
    tail = jnp.concatenate([top, mid, rest, jnp.zeros((TILE - 3, value.shape[1]), F32)], axis=0)
    return jnp.concatenate([value[:per].astype(BF16), tail.astype(BF16)], axis=0)


def weights_kernel(
    parts_n, per, info_ref, turned_ref, bias_ref, video_ref, early_ref, near_ref, far_ref, *refs
):
    near_early_ref, far_early_ref, gain_ref, shift_ref, *refs = refs
    parts, (act_ref, keep_ref, *send_refs) = refs[:parts_n], refs[parts_n:-3]
    wide, acc, shards = refs[-3:]
    frames, rows, cols, chans = video_ref.shape[1:]
    before = early_ref.shape[1]
    step = cols // TILE
    slots = wide.shape[0]
    inside, first, has_low, has_high = info_ref[0], info_ref[1], info_ref[2], info_ref[3]
    count, total, squares = merged([ref[...] for ref in parts])
    every = jnp.sum(count, axis=0, keepdims=True) * per
    mean = group_sum(jnp.sum(total, axis=0, keepdims=True), per) / every
    away = total / jnp.maximum(count, 1.0) - mean
    squares = jnp.sum(squares + count * (away * away), axis=0, keepdims=True)
    squares = group_sum(squares, per)
    odd = info_ref[6] == 1
    scale = 0.5 * lax.rsqrt(squares / every + 1e-05) * gain_ref[...]
    offset = 0.5 * shift_ref[...] - mean * scale
    wide[:, 0:8, :] = jnp.zeros((slots, 8, chans), F32)
    wide[:, 8 + cols : 16 + cols, :] = jnp.zeros((slots, 8, chans), F32)

    def row(values, keep, slot, f, y):
        half = values.astype(F32) * (scale * keep) + offset * keep
        wide[slot, 8 : 8 + cols, :] = half + half * jnp.tanh(half)
        for r in range(-1, step + 1):
            act_ref[f, y, r + 1] = wide[slot, pl.ds(8 + r, TILE, stride=step), :].astype(BF16)

    def kept(f):
        local = f - before
        return ((local < inside) & (first + local >= 0)).astype(F32)

    def inner(f, y, slot):
        local = f - before
        source = early_ref.at[0, f] if local < 0 else video_ref.at[0, local]
        row(source[y], kept(f), slot, f, y + 1)

    def border(f, side, slot):
        local = f - before
        near = near_early_ref[frames + local] if local < 0 else near_ref[local]
        far = far_early_ref[frames + local] if local < 0 else far_ref[local]
        near, far = near.astype(F32), far.astype(F32)
        if side:
            value, has = jnp.where(odd, far, near), has_high
        else:
            value, has = jnp.where(odd, near, far), has_low
        row(value, kept(f) * has.astype(F32), slot, f, side * (rows + 1))

    for f in range(before + 1):

        def many(y, carry, f=f):
            inner(f, y, y % slots)
            return carry

        lax.fori_loop(0, rows, many, 0, unroll=4)
        border(f, 0, 0)
        border(f, 1, 1)

    taps = [(kt, ky, kx) for kt in range(3) for ky in range(3) for kx in range(3)]
    pair = 2
    k = turned_ref.shape[3]
    tms, dps, full = shards.shape[:3]
    size = full - TILE

    def place(tap):
        block = acc[:, tap * chans : (tap + 1) * chans].T
        done = 0
        while done < chans:
            shard, at = divmod(tap * chans + done, size)
            take = min(chans - done, size - at)
            shards[shard // dps, shard % dps, at : at + take, :] = block[done : done + take]
            done += take

    groups = [taps[j : j + pair] for j in range(0, len(taps), pair)]
    for t in range(frames):
        f = t + before + 1
        work = []
        if f < frames + before:
            work = [functools.partial(border, f, side, side) for side in range(2)]
            work += [functools.partial(inner, f, y, y % slots) for y in range(rows)]
        left = jnp.concatenate([turned_ref[t, y] for y in range(rows)], axis=1)
        for j, chosen in enumerate(groups):
            right = jnp.concatenate(
                [
                    act_ref[t + kt, ky : ky + rows, kx : kx + step].reshape(rows * k, chans)
                    for kt, ky, kx in chosen
                ],
                axis=1,
            )
            product = jnp.dot(left, right, preferred_element_type=F32)
            where = slice(j * pair * chans, (j * pair + len(chosen)) * chans)
            acc[:, where] = product if t == 0 else acc[:, where] + product
            for task in work[j * len(work) // len(groups) : (j + 1) * len(work) // len(groups)]:
                task()
            if t == frames - 1:
                for n in range(len(chosen)):
                    place(j * pair + n)
    tail = jnp.concatenate([bias_ref[0:1], jnp.zeros((TILE - 1, chans), F32)], axis=0)
    for i in range(tms):
        for j in range(dps):
            shards[i, j, size:full, :] = tail
    me = info_ref[4]
    keep_ref[...] = shards[me]
    for r in range(1, tms):
        send_refs[r - 1][...] = shards[me ^ r]


def spread_kernel(count, info_ref, after_ref, keep_ref, *refs):
    incoming, own_ref, send_refs = refs[:count], refs[count], refs[count + 1 :]
    me = info_ref[5]
    for r in range(len(send_refs) + 1):
        value = keep_ref[me ^ r]
        for ref in incoming:
            value = value + ref[me ^ r]
        if r == 0:
            own_ref[...] = value
        else:
            send_refs[r - 1][...] = packed(value)


def add_kernel(after_ref, *refs):
    values = [ref[...].astype(F32) for ref in refs[:-1]]
    while len(values) > 1:
        values = [sum(values[n : n + 2]) for n in range(0, len(values), 2)]
    refs[-1][...] = packed(values[0])


def taps_kernel(after_ref, kernel_ref, out_ref):
    kts, kys, kxs, chans = kernel_ref.shape[:4]
    pair = out_ref.shape[1] // chans
    zero = jnp.zeros((kys * kxs * chans, chans), BF16)
    span = kys * kxs * chans
    for f in range(kts + pair - 1):
        for g in range(pair):
            if 0 <= f - g < kts:
                value = kernel_ref[f - g].reshape(span, chans)
            else:
                value = zero
            out_ref[f * span : (f + 1) * span, g * chans : (g + 1) * chans] = value


def conv_kernel(
    piece, last, info_ref, after_ref, act_ref, taps_ref, video_ref, bias_ref, *refs
):
    out_ref, whole_ref, wide, sem = refs[-4:]
    t0, y0 = piece
    rows = out_ref.shape[1]
    if last is not None:
        out = pltpu.make_async_copy(refs[0], whole_ref.at[last], sem)
        out.start()
    cols, chans = out_ref.shape[2:]
    step = cols // TILE
    pair = taps_ref.shape[1] // chans
    used = [
        (f, ky, kx)
        for f in range(taps_ref.shape[0] // (9 * chans))
        for ky in range(3)
        for kx in range(3)
    ]
    left = jnp.concatenate(
        [
            act_ref[t0 + f, y0 + ky : y0 + ky + rows, kx : kx + step].reshape(rows * cols, chans)
            for f, ky, kx in used
        ],
        axis=1,
    )
    result = jnp.dot(left, taps_ref[...], preferred_element_type=F32)
    for f in range(pair):
        keep = (t0 + f < info_ref[0]).astype(F32)
        for y in range(rows):
            slot = f * rows + y
            for r in range(step):
                at = y * cols + r * TILE
                wide[slot, pl.ds(r, TILE, stride=step), :] = result[
                    at : at + TILE, f * chans : (f + 1) * chans
                ]
            value = video_ref[0, t0 + f, y0 + y].astype(F32) + wide[slot] + bias_ref[...]
            out_ref[f, y] = (value * keep).astype(BF16)
    if last is not None:
        out.wait()


def step_of(video, lengths, norm_gain, norm_shift, kernel, conv_bias, cotangent):
    frames, rows, cols, chans = video.shape[1:]
    per = chans // GROUPS
    step = cols // TILE
    before = kernel.shape[0] - 1
    tms, dps, spaces = (lax.axis_size(axis) for axis in ("tm", "dp", "space"))
    tm, dp, space = (lax.axis_index(axis) for axis in ("tm", "dp", "space"))
    first = tm * frames
    inside = jnp.clip(lengths[0] - first, -before, frames)
    info = jnp.stack(
        [
            inside,
            first,
            (space > 0).astype(jnp.int32),
            (space < spaces - 1).astype(jnp.int32),
            tm,
            dp,
            space % 2,
        ]
    ).astype(jnp.int32)

    source = pltpu.with_memory_space_constraint(video, pltpu.HBM)
    border = jax.ShapeDtypeStruct((frames, cols, chans), BF16)
    near, far = pl.pallas_call(
        ends_kernel,
        in_specs=[SMEM, ANY],
        out_specs=[VMEM, VMEM],
        out_shape=[border, border],
        scratch_shapes=[pltpu.SemaphoreType.DMA((2,))],
        compiler_params=params(1),
        name="ends",
    )(info, source)
    near = swap(near, "space", 1)
    between = [(i, i + 1) for i in range(1, spaces - 1, 2)]
    far = lax.ppermute(far, "space", between + [(j, i) for i, j in between])
    stats, local, masked_in, tail = pl.pallas_call(
        functools.partial(stats_kernel, before),
        in_specs=[SMEM, ANY, ANY],
        out_specs=[VMEM] * 4,
        out_shape=[
            jax.ShapeDtypeStruct((3, 8, chans), F32),
            jax.ShapeDtypeStruct(video.shape, BF16),
            jax.ShapeDtypeStruct(cotangent.shape, BF16),
            jax.ShapeDtypeStruct((1, before, rows, cols, chans), BF16),
        ],
        scratch_shapes=[pltpu.SemaphoreType.DMA((2 * frames + 1 + before,))],
        compiler_params=params(2),
        name="stats",
    )(info, source, pltpu.with_memory_space_constraint(cotangent, pltpu.HBM))
    following = [(i, (i + 1) % tms) for i in range(tms)]
    gathered = [stats] + [swap(stats, "tm", r) for r in range(1, tms)]
    early = lax.ppermute(tail, "tm", following)
    stats = pl.pallas_call(
        merge_kernel,
        in_specs=[VMEM] * tms,
        out_specs=VMEM,
        out_shape=jax.ShapeDtypeStruct((3, 8, chans), F32),
        compiler_params=params(1),
        name="merge",
    )(*gathered)
    parts = [stats] + [swap(stats, "space", r) for r in range(1, spaces)]
    near_early = lax.ppermute(near, "tm", following)
    far_early = lax.ppermute(far, "tm", following)
    pair = 2
    taps = pl.pallas_call(
        taps_kernel,
        in_specs=[ANY, VMEM],
        out_specs=VMEM,
        out_shape=jax.ShapeDtypeStruct(
            ((kernel.shape[0] + pair - 1) * 9 * chans, pair * chans), BF16
        ),
        compiler_params=params(2),
        name="taps",
    )(stats, kernel)

    turned, bias = pl.pallas_call(
        cotangent_kernel,
        in_specs=[SMEM, VMEM],
        out_specs=[VMEM, VMEM],
        out_shape=[
            jax.ShapeDtypeStruct((frames, rows, chans, cols), BF16),
            jax.ShapeDtypeStruct((8, chans), F32),
        ],
        scratch_shapes=[pltpu.VMEM((8, cols, chans), F32)],
        compiler_params=params(4),
        name="cotangent",
    )(info, masked_in)

    count = kernel.shape[0] * kernel.shape[1] * kernel.shape[2] * chans
    shards_n = tms * dps
    assert count % shards_n == 0
    shard = count // shards_n
    full = shard + TILE
    act, keep, *sends = pl.pallas_call(
        functools.partial(weights_kernel, spaces, per),
        in_specs=[SMEM] + [VMEM] * (10 + spaces),
        out_specs=[VMEM] * (1 + tms),
        out_shape=[
            jax.ShapeDtypeStruct((frames + before, rows + 2, step + 2, TILE, chans), BF16)
        ]
        + [jax.ShapeDtypeStruct((dps, full, chans), F32)] * tms,
        scratch_shapes=[
            pltpu.VMEM((8, cols + 16, chans), F32),
            pltpu.VMEM((chans, count), F32),
            pltpu.VMEM((tms, dps, full, chans), F32),
        ],
        compiler_params=params(16),
        name="weights",
    )(
        info,
        turned,
        bias,
        local,
        early,
        near,
        far,
        near_early,
        far_early,
        norm_gain.reshape(1, chans),
        norm_shift.reshape(1, chans),
        *parts,
    )

    block = 4
    pieces = [(t0, y0) for t0 in range(0, frames, pair) for y0 in range(0, rows, block)]
    done = []

    whole = jax.ShapeDtypeStruct(video.shape, BF16)

    def where(n):
        t0, y0 = pieces[n]
        return 0, pl.ds(t0, pair), pl.ds(y0, block)

    def cover(after, number):
        for _ in range(min(number, len(pieces) - len(done))):
            n = len(done)
            made = list(done[-1]) if done else []
            piece, output = pl.pallas_call(
                functools.partial(conv_kernel, pieces[n], where(n - 1) if made else None),
                in_specs=[SMEM, ANY, VMEM, VMEM, VMEM, VMEM] + [VMEM, ANY][: len(made)],
                out_specs=[VMEM, ANY],
                out_shape=[jax.ShapeDtypeStruct((pair, block, cols, chans), BF16), whole],
                scratch_shapes=[
                    pltpu.VMEM((pair * block, cols, chans), F32),
                    pltpu.SemaphoreType.DMA,
                ],
                input_output_aliases={7: 1} if made else {},
                compiler_params=params(6),
                name="conv",
            )(info, after, act, taps, local, conv_bias.reshape(1, chans), *made)
            done.append((piece, output))
            after = piece
        return after

    incoming = [swap(send, "tm", r + 1) for r, send in enumerate(sends)]
    token = cover(keep, 1)
    own, *sends = pl.pallas_call(
        functools.partial(spread_kernel, len(incoming)),
        in_specs=[SMEM, ANY] + [VMEM] * (1 + len(incoming)),
        out_specs=[VMEM] * dps,
        out_shape=[jax.ShapeDtypeStruct((full, chans), F32)]
        + [jax.ShapeDtypeStruct((full, chans), BF16)] * (dps - 1),
        compiler_params=params(4),
        name="spread",
    )(info, token, keep, *incoming)

    def added(dtype, after, *arrays):
        return pl.pallas_call(
            add_kernel,
            in_specs=[ANY] + [VMEM] * len(arrays),
            out_specs=VMEM,
            out_shape=jax.ShapeDtypeStruct((full, chans), dtype),
            compiler_params=params(2),
            name="added",
        )(after, *arrays)

    incoming = [swap(send, "dp", r + 1) for r, send in enumerate(sends)]
    token = cover(own, 2)
    total = added(BF16, token, own, *incoming)
    others = [swap(total, "space", r) for r in range(1, spaces)]
    token = cover(total, 4)
    total = added(BF16, token, total, *others)
    mine = [total] + [swap(total, "dp", r) for r in range(1, dps)]
    cover(total, len(pieces))
    shards = {(0, r): array for r, array in enumerate(mine)}
    for q in range(1, tms):
        for r, array in enumerate(mine):
            shards[q, r] = swap(array, "tm", q)
    order = list(shards)

    def collect(info_ref, *refs):
        shard_refs, piece_ref = refs[: len(order)], refs[len(order)]
        out_ref, sum_ref, whole_ref, sem = refs[-4:]
        copy = pltpu.make_async_copy(piece_ref, whole_ref.at[where(len(pieces) - 1)], sem)
        copy.start()
        for (q, r), ref in zip(order, shard_refs):
            at = (info_ref[4] ^ q) * dps + (info_ref[5] ^ r)
            out_ref[at] = ref[0:shard, :].astype(F32)
        tail = shard_refs[0][shard : shard + TILE, :].astype(F32)
        sum_ref[...] = tail[0:1] + tail[1:2] + tail[2:3]
        copy.wait()

    grad_kernel, grad_bias, output = pl.pallas_call(
        collect,
        in_specs=[SMEM] + [VMEM] * (len(order) + 1) + [ANY],
        out_specs=[VMEM, VMEM, ANY],
        out_shape=[
            jax.ShapeDtypeStruct((shards_n, shard, chans), F32),
            jax.ShapeDtypeStruct((1, chans), F32),
            whole,
        ],
        scratch_shapes=[pltpu.SemaphoreType.DMA],
        input_output_aliases={len(order) + 2: 2},
        compiler_params=params(4),
        name="collect",
    )(info, *[shards[key] for key in order], *done[-1])

    return output, grad_kernel.reshape(kernel.shape), grad_bias.reshape(chans)


def solution(mesh):
    return jax.shard_map(
        step_of,
        mesh=mesh,
        in_specs=(
            P("dp", "tm", "space", None, None),
            P("dp"),
            P(),
            P(),
            P(),
            P(),
            P("dp", "tm", "space", None, None),
        ),
        out_specs=(P("dp", "tm", "space", None, None), P(), P()),
        check_vma=False,
    )
```

```python
import functools

import jax
import jax.numpy as jnp
from jax import lax
from jax.experimental import pallas as pl
from jax.experimental.pallas import tpu as pltpu
from jax.sharding import PartitionSpec as P


GROUPS = 32
TILE = 16
F32 = jnp.float32
BF16 = jnp.bfloat16
VMEM = pl.BlockSpec(memory_space=pltpu.VMEM)
ANY = pl.BlockSpec(memory_space=pl.ANY)
SMEM = pl.BlockSpec(memory_space=pltpu.SMEM)


def params(mib):
    return pltpu.CompilerParams(vmem_limit_bytes=mib * 1024 * 1024)


def swap(array, axis, by):
    length = lax.axis_size(axis)
    assert length & (length - 1) == 0
    return lax.ppermute(array, axis, [(i, i ^ by) for i in range(length)])


def group_sum(row, per):
    value = jnp.broadcast_to(row, (8, row.shape[1]))
    lane = lax.broadcasted_iota(jnp.int32, value.shape, 1)
    size = value.shape[1]
    step = 1
    while step < per:
        up = pltpu.roll(value, size - step, 1)
        down = pltpu.roll(value, step, 1)
        value = value + jnp.where((lane & step) == 0, up, down)
        step *= 2
    return value[0:1]


def merged(parts):
    count = sum(part[0] for part in parts)
    total = sum(part[1] for part in parts)
    mean = total / jnp.maximum(count, 1.0)
    squares = jnp.zeros_like(mean)
    for part in parts:
        away = part[1] / jnp.maximum(part[0], 1.0) - mean
        squares = squares + (part[2] + part[0] * (away * away))
    return count, total, squares


def ends_kernel(info_ref, video_hbm, near_ref, far_ref, sems):
    rows = video_hbm.shape[2]
    odd = info_ref[6]
    copies = [
        pltpu.make_async_copy(video_hbm.at[0, :, row], ref, sems.at[n])
        for n, (row, ref) in enumerate(
            (((1 - odd) * (rows - 1), near_ref), (odd * (rows - 1), far_ref))
        )
    ]
    for copy in copies:
        copy.start()
    for copy in copies:
        copy.wait()


def stats_kernel(before, info_ref, video_hbm, cot_hbm, *refs):
    out_ref, video_ref, cot_ref, tail_ref, sems = refs
    frames, rows, cols, chans = video_ref.shape[1:]
    parts_n = 2 * frames
    some = rows // 2
    first = frames - before
    copies = []
    for n in range(parts_n):
        at = (0, n // 2, pl.ds(n % 2 * some, some))
        copies.append(pltpu.make_async_copy(video_hbm.at[at], video_ref.at[at], sems.at[n]))
        copies[-1].start()
    later = [pltpu.make_async_copy(cot_hbm, cot_ref, sems.at[parts_n])]
    later[0].start()
    size = float(some * cols // 8)
    lanes = 4
    split = (cols // (8 * lanes), lanes, 8, chans)
    start = jnp.zeros((lanes, 8, chans), F32)
    parts = []
    for n in range(parts_n):
        copies[n].wait()
        f, y0 = n // 2, n % 2 * some
        if n % 2 and f >= first:
            sem = sems.at[parts_n + 1 + f - first]
            later.append(pltpu.make_async_copy(video_ref.at[0, f], tail_ref.at[0, f - first], sem))
            later[-1].start()

        def add(y, acc, f=f, y0=y0):
            return acc + jnp.sum(video_ref[0, f, y0 + y].astype(F32).reshape(split), axis=0)

        total = jnp.sum(lax.fori_loop(0, some, add, start, unroll=8), axis=0)
        mean = total / size

        def deviate(y, acc, f=f, y0=y0, mean=mean):
            away = video_ref[0, f, y0 + y].astype(F32).reshape(split) - mean
            return acc + jnp.sum(away * away, axis=0)

        squares = jnp.sum(lax.fori_loop(0, some, deviate, start, unroll=8), axis=0)
        keep = (f < info_ref[0]).astype(F32)
        parts.append((jnp.full((8, chans), size, F32) * keep, total * keep, squares * keep))
    for n, value in enumerate(merged(parts)):
        out_ref[n] = value
    for copy in later:
        copy.wait()


def merge_kernel(*refs):
    for n, value in enumerate(merged([ref[...] for ref in refs[:-1]])):
        refs[-1][n] = value


def cotangent_kernel(info_ref, cot_ref, turned_ref, bias_ref, wide):
    rows, cols, chans = cot_ref.shape[2:]
    step = cols // TILE
    lanes = 4
    bias = jnp.zeros((lanes, 8, chans), F32)
    for t in range(turned_ref.shape[0]):
        keep = (t < info_ref[0]).astype(F32)

        def row(y, acc, t=t, keep=keep):
            value = cot_ref[0, t, y].astype(F32) * keep
            slot = wide.at[y % wide.shape[0]]
            slot[...] = value
            order = jnp.concatenate(
                [slot[pl.ds(r, TILE, stride=step), :] for r in range(step)], axis=0
            )
            turned_ref[t, y] = order.astype(BF16).T
            return acc + jnp.sum(value.reshape(cols // (8 * lanes), lanes, 8, chans), axis=0)

        bias = lax.fori_loop(0, rows, row, bias, unroll=8)
    bias_ref[...] = jnp.sum(bias, axis=0)


def packed(value):
    per = value.shape[0] - TILE
    total = value[per : per + 1] + value[per + 1 : per + 2] + value[per + 2 : per + 3]
    top = total.astype(BF16).astype(F32)
    mid = (total - top).astype(BF16).astype(F32)
    rest = total - top - mid
    tail = jnp.concatenate([top, mid, rest, jnp.zeros((TILE - 3, value.shape[1]), F32)], axis=0)
    return jnp.concatenate([value[:per].astype(BF16), tail.astype(BF16)], axis=0)


def weights_kernel(
    parts_n, per, info_ref, turned_ref, bias_ref, cot_ref, video_ref, early_ref, near_ref, *refs
):
    far_ref, near_early_ref, far_early_ref, gain_ref, shift_ref, *refs = refs
    parts, (act_ref, keep_ref, *send_refs) = refs[:parts_n], refs[parts_n:-6]
    wide, acc, shards, late, plain, bias_acc = refs[-6:]
    ahead = turned_ref.shape[0]
    bias_acc[...] = bias_ref[...]
    frames, rows, cols, chans = video_ref.shape[1:]
    before = early_ref.shape[1]
    step = cols // TILE
    slots = wide.shape[0]
    inside, first, has_low, has_high = info_ref[0], info_ref[1], info_ref[2], info_ref[3]
    count, total, squares = merged([ref[...] for ref in parts])
    every = jnp.sum(count, axis=0, keepdims=True) * per
    mean = group_sum(jnp.sum(total, axis=0, keepdims=True), per) / every
    away = total / jnp.maximum(count, 1.0) - mean
    squares = jnp.sum(squares + count * (away * away), axis=0, keepdims=True)
    squares = group_sum(squares, per)
    odd = info_ref[6] == 1
    scale = 0.5 * lax.rsqrt(squares / every + 1e-05) * gain_ref[...]
    offset = 0.5 * shift_ref[...] - mean * scale
    wide[:, 0:8, :] = jnp.zeros((slots, 8, chans), F32)
    wide[:, 8 + cols : 16 + cols, :] = jnp.zeros((slots, 8, chans), F32)

    def row(values, keep, slot, f, y):
        half = values.astype(F32) * (scale * keep) + offset * keep
        wide[slot, 8 : 8 + cols, :] = half + half * jnp.tanh(half)
        for r in range(-1, step + 1):
            act_ref[f, y, r + 1] = wide[slot, pl.ds(8 + r, TILE, stride=step), :].astype(BF16)

    def kept(f):
        local = f - before
        return ((local < inside) & (first + local >= 0)).astype(F32)

    def inner(f, y, slot):
        local = f - before
        source = early_ref.at[0, f] if local < 0 else video_ref.at[0, local]
        row(source[y], kept(f), slot, f, y + 1)

    def border(f, side, slot):
        local = f - before
        near = near_early_ref[frames + local] if local < 0 else near_ref[local]
        far = far_early_ref[frames + local] if local < 0 else far_ref[local]
        near, far = near.astype(F32), far.astype(F32)
        if side:
            value, has = jnp.where(odd, far, near), has_high
        else:
            value, has = jnp.where(odd, near, far), has_low
        row(value, kept(f) * has.astype(F32), slot, f, side * (rows + 1))

    def turn(t, y, slot):
        value = cot_ref[0, t, y].astype(F32) * (t < inside).astype(F32)
        plain[slot] = value
        order = jnp.concatenate(
            [plain[slot, pl.ds(r, TILE, stride=step), :] for r in range(step)], axis=0
        )
        late[t - ahead, y] = order.astype(BF16).T
        bias_acc[...] += jnp.sum(value.reshape(cols // 8, 8, chans), axis=0)

    def all_rows(f):
        work = [functools.partial(border, f, side, side) for side in range(2)]
        return work + [functools.partial(inner, f, y, y % slots) for y in range(rows)]

    def many(y, carry):
        inner(0, y, y % slots)
        return carry

    lax.fori_loop(0, rows, many, 0, unroll=4)
    border(0, 0, 0)
    border(0, 1, 1)

    taps = [(kt, ky, kx) for kt in range(3) for ky in range(3) for kx in range(3)]
    pair = 2
    k = turned_ref.shape[3]
    tms, dps, full = shards.shape[:3]
    size = full - TILE

    def place(tap):
        block = acc[:, tap * chans : (tap + 1) * chans].T
        done = 0
        while done < chans:
            shard, at = divmod(tap * chans + done, size)
            take = min(chans - done, size - at)
            shards[shard // dps, shard % dps, at : at + take, :] = block[done : done + take]
            done += take

    groups = [taps[j : j + pair] for j in range(0, len(taps), pair)]
    for t in range(frames):
        work = []
        if t == 0:
            for f in range(1, before + 1):
                work.append((f * 9 // pair, all_rows(f)))
        if t + before + 1 < frames + before:
            tasks = all_rows(t + before + 1)
            if ahead <= t + 1 < frames:
                tasks += [
                    functools.partial(turn, t + 1, y, y % plain.shape[0]) for y in range(rows)
                ]
            work.append((len(groups), tasks))
        slots_of = [[] for _ in groups]
        begin = 0
        for end, tasks in work:
            for n, task in enumerate(tasks):
                slots_of[begin + n * (end - begin) // len(tasks)].append(task)
            begin = end
        source = turned_ref.at[t] if t < ahead else late.at[t - ahead]
        left = jnp.concatenate([source[y] for y in range(rows)], axis=1)
        for j, chosen in enumerate(groups):
            right = jnp.concatenate(
                [
                    act_ref[t + kt, ky : ky + rows, kx : kx + step].reshape(rows * k, chans)
                    for kt, ky, kx in chosen
                ],
                axis=1,
            )
            product = jnp.dot(left, right, preferred_element_type=F32)
            where = slice(j * pair * chans, (j * pair + len(chosen)) * chans)
            acc[:, where] = product if t == 0 else acc[:, where] + product
            for task in slots_of[j]:
                task()
            if t == frames - 1:
                for n in range(len(chosen)):
                    place(j * pair + n)
    bias = jnp.sum(bias_acc[...], axis=0, keepdims=True)
    tail = jnp.concatenate([bias, jnp.zeros((TILE - 1, chans), F32)], axis=0)
    for i in range(tms):
        for j in range(dps):
            shards[i, j, size:full, :] = tail
    me = info_ref[4]
    keep_ref[...] = shards[me]
    for r in range(1, tms):
        send_refs[r - 1][...] = shards[me ^ r]


def spread_kernel(count, info_ref, after_ref, keep_ref, *refs):
    incoming, own_ref, send_refs = refs[:count], refs[count], refs[count + 1 :]
    me = info_ref[5]
    for r in range(len(send_refs) + 1):
        value = keep_ref[me ^ r]
        for ref in incoming:
            value = value + ref[me ^ r]
        if r == 0:
            own_ref[...] = value
        else:
            send_refs[r - 1][...] = packed(value)


def add_kernel(after_ref, *refs):
    values = [ref[...].astype(F32) for ref in refs[:-1]]
    while len(values) > 1:
        values = [sum(values[n : n + 2]) for n in range(0, len(values), 2)]
    refs[-1][...] = packed(values[0])


def taps_kernel(after_ref, kernel_ref, out_ref):
    kts, kys, kxs, chans = kernel_ref.shape[:4]
    pair = out_ref.shape[1] // chans
    zero = jnp.zeros((kys * kxs * chans, chans), BF16)
    span = kys * kxs * chans
    for f in range(kts + pair - 1):
        for g in range(pair):
            if 0 <= f - g < kts:
                value = kernel_ref[f - g].reshape(span, chans)
            else:
                value = zero
            out_ref[f * span : (f + 1) * span, g * chans : (g + 1) * chans] = value


def conv_kernel(
    piece, last, info_ref, after_ref, act_ref, taps_ref, video_ref, bias_ref, *refs
):
    out_ref, whole_ref, wide, sem = refs[-4:]
    t0, y0 = piece
    rows = out_ref.shape[1]
    if last is not None:
        out = pltpu.make_async_copy(refs[0], whole_ref.at[last], sem)
        out.start()
    cols, chans = out_ref.shape[2:]
    step = cols // TILE
    pair = taps_ref.shape[1] // chans
    used = [
        (f, ky, kx)
        for f in range(taps_ref.shape[0] // (9 * chans))
        for ky in range(3)
        for kx in range(3)
    ]
    left = jnp.concatenate(
        [
            act_ref[t0 + f, y0 + ky : y0 + ky + rows, kx : kx + step].reshape(rows * cols, chans)
            for f, ky, kx in used
        ],
        axis=1,
    )
    result = jnp.dot(left, taps_ref[...], preferred_element_type=F32)
    for f in range(pair):
        keep = (t0 + f < info_ref[0]).astype(F32)
        for y in range(rows):
            slot = f * rows + y
            for r in range(step):
                at = y * cols + r * TILE
                wide[slot, pl.ds(r, TILE, stride=step), :] = result[
                    at : at + TILE, f * chans : (f + 1) * chans
                ]
            value = video_ref[0, t0 + f, y0 + y].astype(F32) + wide[slot] + bias_ref[...]
            out_ref[f, y] = (value * keep).astype(BF16)
    if last is not None:
        out.wait()


def step_of(video, lengths, norm_gain, norm_shift, kernel, conv_bias, cotangent):
    frames, rows, cols, chans = video.shape[1:]
    per = chans // GROUPS
    step = cols // TILE
    before = kernel.shape[0] - 1
    tms, dps, spaces = (lax.axis_size(axis) for axis in ("tm", "dp", "space"))
    tm, dp, space = (lax.axis_index(axis) for axis in ("tm", "dp", "space"))
    first = tm * frames
    inside = jnp.clip(lengths[0] - first, -before, frames)
    info = jnp.stack(
        [
            inside,
            first,
            (space > 0).astype(jnp.int32),
            (space < spaces - 1).astype(jnp.int32),
            tm,
            dp,
            space % 2,
        ]
    ).astype(jnp.int32)

    source = pltpu.with_memory_space_constraint(video, pltpu.HBM)
    border = jax.ShapeDtypeStruct((frames, cols, chans), BF16)
    near, far = pl.pallas_call(
        ends_kernel,
        in_specs=[SMEM, ANY],
        out_specs=[VMEM, VMEM],
        out_shape=[border, border],
        scratch_shapes=[pltpu.SemaphoreType.DMA((2,))],
        compiler_params=params(1),
        name="ends",
    )(info, source)
    near = swap(near, "space", 1)
    between = [(i, i + 1) for i in range(1, spaces - 1, 2)]
    far = lax.ppermute(far, "space", between + [(j, i) for i, j in between])
    stats, local, masked_in, tail = pl.pallas_call(
        functools.partial(stats_kernel, before),
        in_specs=[SMEM, ANY, ANY],
        out_specs=[VMEM] * 4,
        out_shape=[
            jax.ShapeDtypeStruct((3, 8, chans), F32),
            jax.ShapeDtypeStruct(video.shape, BF16),
            jax.ShapeDtypeStruct(cotangent.shape, BF16),
            jax.ShapeDtypeStruct((1, before, rows, cols, chans), BF16),
        ],
        scratch_shapes=[pltpu.SemaphoreType.DMA((2 * frames + 1 + before,))],
        compiler_params=params(2),
        name="stats",
    )(info, source, pltpu.with_memory_space_constraint(cotangent, pltpu.HBM))
    following = [(i, (i + 1) % tms) for i in range(tms)]
    gathered = [stats] + [swap(stats, "tm", r) for r in range(1, tms)]
    early = lax.ppermute(tail, "tm", following)
    stats = pl.pallas_call(
        merge_kernel,
        in_specs=[VMEM] * tms,
        out_specs=VMEM,
        out_shape=jax.ShapeDtypeStruct((3, 8, chans), F32),
        compiler_params=params(1),
        name="merge",
    )(*gathered)
    parts = [stats] + [swap(stats, "space", r) for r in range(1, spaces)]
    near_early = lax.ppermute(near, "tm", following)
    far_early = lax.ppermute(far, "tm", following)
    pair = 2
    taps = pl.pallas_call(
        taps_kernel,
        in_specs=[ANY, VMEM],
        out_specs=VMEM,
        out_shape=jax.ShapeDtypeStruct(
            ((kernel.shape[0] + pair - 1) * 9 * chans, pair * chans), BF16
        ),
        compiler_params=params(2),
        name="taps",
    )(stats, kernel)

    ahead = frames // 2
    turned, bias = pl.pallas_call(
        cotangent_kernel,
        in_specs=[SMEM, VMEM],
        out_specs=[VMEM, VMEM],
        out_shape=[
            jax.ShapeDtypeStruct((ahead, rows, chans, cols), BF16),
            jax.ShapeDtypeStruct((8, chans), F32),
        ],
        scratch_shapes=[pltpu.VMEM((8, cols, chans), F32)],
        compiler_params=params(4),
        name="cotangent",
    )(info, masked_in)

    count = kernel.shape[0] * kernel.shape[1] * kernel.shape[2] * chans
    shards_n = tms * dps
    assert count % shards_n == 0
    shard = count // shards_n
    full = shard + TILE
    act, keep, *sends = pl.pallas_call(
        functools.partial(weights_kernel, spaces, per),
        in_specs=[SMEM] + [VMEM] * (11 + spaces),
        out_specs=[VMEM] * (1 + tms),
        out_shape=[
            jax.ShapeDtypeStruct((frames + before, rows + 2, step + 2, TILE, chans), BF16)
        ]
        + [jax.ShapeDtypeStruct((dps, full, chans), F32)] * tms,
        scratch_shapes=[
            pltpu.VMEM((8, cols + 16, chans), F32),
            pltpu.VMEM((chans, count), F32),
            pltpu.VMEM((tms, dps, full, chans), F32),
            pltpu.VMEM((frames - ahead, rows, chans, cols), BF16),
            pltpu.VMEM((8, cols, chans), F32),
            pltpu.VMEM((8, chans), F32),
        ],
        compiler_params=params(16),
        name="weights",
    )(
        info,
        turned,
        bias,
        masked_in,
        local,
        early,
        near,
        far,
        near_early,
        far_early,
        norm_gain.reshape(1, chans),
        norm_shift.reshape(1, chans),
        *parts,
    )

    block = 4
    pieces = [(t0, y0) for t0 in range(0, frames, pair) for y0 in range(0, rows, block)]
    done = []

    whole = jax.ShapeDtypeStruct(video.shape, BF16)

    def where(n):
        t0, y0 = pieces[n]
        return 0, pl.ds(t0, pair), pl.ds(y0, block)

    def cover(after, number):
        for _ in range(min(number, len(pieces) - len(done))):
            n = len(done)
            made = list(done[-1]) if done else []
            piece, output = pl.pallas_call(
                functools.partial(conv_kernel, pieces[n], where(n - 1) if made else None),
                in_specs=[SMEM, ANY, VMEM, VMEM, VMEM, VMEM] + [VMEM, ANY][: len(made)],
                out_specs=[VMEM, ANY],
                out_shape=[jax.ShapeDtypeStruct((pair, block, cols, chans), BF16), whole],
                scratch_shapes=[
                    pltpu.VMEM((pair * block, cols, chans), F32),
                    pltpu.SemaphoreType.DMA,
                ],
                input_output_aliases={7: 1} if made else {},
                compiler_params=params(6),
                name="conv",
            )(info, after, act, taps, local, conv_bias.reshape(1, chans), *made)
            done.append((piece, output))
            after = piece
        return after

    def exchanged(arrays, axis):
        result = []
        for n, array in enumerate(arrays):
            result.append(swap(array, axis, n + 1))
        return result

    incoming = [swap(send, "tm", r + 1) for r, send in enumerate(sends)]
    token = cover(keep, 1)
    own, *sends = pl.pallas_call(
        functools.partial(spread_kernel, len(incoming)),
        in_specs=[SMEM, ANY] + [VMEM] * (1 + len(incoming)),
        out_specs=[VMEM] * dps,
        out_shape=[jax.ShapeDtypeStruct((full, chans), F32)]
        + [jax.ShapeDtypeStruct((full, chans), BF16)] * (dps - 1),
        compiler_params=params(4),
        name="spread",
    )(info, token, keep, *incoming)

    def added(dtype, after, *arrays):
        return pl.pallas_call(
            add_kernel,
            in_specs=[ANY] + [VMEM] * len(arrays),
            out_specs=VMEM,
            out_shape=jax.ShapeDtypeStruct((full, chans), dtype),
            compiler_params=params(2),
            name="added",
        )(after, *arrays)

    incoming = exchanged(sends, "dp")
    token = cover(own, 2)
    total = added(BF16, token, own, *incoming)
    others = exchanged([total] * (spaces - 1), "space")
    token = cover(total, 4)
    total = added(BF16, token, total, *others)
    mine = [total] + exchanged([total] * (dps - 1), "dp")
    cover(total, len(pieces))
    shards = {(0, r): array for r, array in enumerate(mine)}
    for q in range(1, tms):
        for r, array in enumerate(mine):
            shards[q, r] = swap(array, "tm", q)
    final = 1 % dps
    late = [key for key in shards if key[1] == final]
    order = [key for key in shards if key[1] != final]

    def collect(keys, info_ref, *refs):
        shard_refs, out_ref = refs[: len(keys)], refs[-3]
        wide, sems = refs[-2:]
        copies = []
        if keys is order:
            target = refs[-4].at[where(len(pieces) - 1)]
            copies.append(pltpu.make_async_copy(refs[len(keys)], target, sems.at[len(keys)]))
            copies[-1].start()
            tail = shard_refs[0][shard : shard + TILE, :].astype(F32)
            refs[-5][...] = tail[0:1] + tail[1:2] + tail[2:3]
        for n, ((q, r), ref) in enumerate(zip(keys, shard_refs)):
            at = (info_ref[4] ^ q) * dps + (info_ref[5] ^ r)
            wide[n] = ref[0:shard, :].astype(F32)
            copies.append(pltpu.make_async_copy(wide.at[n], out_ref.at[at], sems.at[n]))
            copies[-1].start()
        for copy in copies:
            copy.wait()

    gradient = jax.ShapeDtypeStruct((shards_n, shard, chans), F32)
    grad_bias, output, grad_kernel = pl.pallas_call(
        functools.partial(collect, order),
        in_specs=[SMEM] + [VMEM] * (len(order) + 1) + [ANY],
        out_specs=[VMEM, ANY, ANY],
        out_shape=[jax.ShapeDtypeStruct((1, chans), F32), whole, gradient],
        scratch_shapes=[
            pltpu.VMEM((len(order), shard, chans), F32),
            pltpu.SemaphoreType.DMA((len(order) + 1,)),
        ],
        input_output_aliases={len(order) + 2: 1},
        compiler_params=params(8),
        name="collect_most",
    )(info, *[shards[key] for key in order], *done[-1])
    grad_kernel = pl.pallas_call(
        functools.partial(collect, late),
        in_specs=[SMEM] + [VMEM] * len(late) + [ANY],
        out_specs=ANY,
        out_shape=gradient,
        scratch_shapes=[
            pltpu.VMEM((len(late), shard, chans), F32),
            pltpu.SemaphoreType.DMA((len(late),)),
        ],
        input_output_aliases={len(late) + 1: 0},
        compiler_params=params(8),
        name="collect_rest",
    )(info, *[shards[key] for key in late], grad_kernel)

    return output, grad_kernel.reshape(kernel.shape), grad_bias.reshape(chans)


def solution(mesh):
    return jax.shard_map(
        step_of,
        mesh=mesh,
        in_specs=(
            P("dp", "tm", "space", None, None),
            P("dp"),
            P(),
            P(),
            P(),
            P(),
            P("dp", "tm", "space", None, None),
        ),
        out_specs=(P("dp", "tm", "space", None, None), P(), P()),
        check_vma=False,
    )
```

```python
import functools

import jax
import jax.numpy as jnp
from jax import lax
from jax.experimental import pallas as pl
from jax.experimental.pallas import tpu as pltpu
from jax.sharding import PartitionSpec as P


GROUPS = 32
TILE = 16
F32 = jnp.float32
BF16 = jnp.bfloat16
VMEM = pl.BlockSpec(memory_space=pltpu.VMEM)
ANY = pl.BlockSpec(memory_space=pl.ANY)
SMEM = pl.BlockSpec(memory_space=pltpu.SMEM)


def params(mib):
    return pltpu.CompilerParams(vmem_limit_bytes=mib * 1024 * 1024)


def swap(array, axis, by):
    length = lax.axis_size(axis)
    assert length & (length - 1) == 0
    return lax.ppermute(array, axis, [(i, i ^ by) for i in range(length)])


def group_sum(row, per):
    value = jnp.broadcast_to(row, (8, row.shape[1]))
    lane = lax.broadcasted_iota(jnp.int32, value.shape, 1)
    size = value.shape[1]
    step = 1
    while step < per:
        up = pltpu.roll(value, size - step, 1)
        down = pltpu.roll(value, step, 1)
        value = value + jnp.where((lane & step) == 0, up, down)
        step *= 2
    return value[0:1]


def merged(parts):
    count = sum(part[0] for part in parts)
    total = sum(part[1] for part in parts)
    mean = total / jnp.maximum(count, 1.0)
    squares = jnp.zeros_like(mean)
    for part in parts:
        away = part[1] / jnp.maximum(part[0], 1.0) - mean
        squares = squares + (part[2] + part[0] * (away * away))
    return count, total, squares


def ends_kernel(info_ref, video_hbm, near_ref, far_ref, sems):
    rows = video_hbm.shape[2]
    odd = info_ref[6]
    copies = [
        pltpu.make_async_copy(video_hbm.at[0, :, row], ref, sems.at[n])
        for n, (row, ref) in enumerate(
            (((1 - odd) * (rows - 1), near_ref), (odd * (rows - 1), far_ref))
        )
    ]
    for copy in copies:
        copy.start()
    for copy in copies:
        copy.wait()


def stats_kernel(before, info_ref, video_hbm, cot_hbm, *refs):
    out_ref, video_ref, cot_ref, tail_ref, sems = refs
    frames, rows, cols, chans = video_ref.shape[1:]
    parts_n = 2 * frames
    some = rows // 2
    first = frames - before
    copies = []
    for n in range(parts_n):
        at = (0, n // 2, pl.ds(n % 2 * some, some))
        copies.append(pltpu.make_async_copy(video_hbm.at[at], video_ref.at[at], sems.at[n]))
        copies[-1].start()
    later = [pltpu.make_async_copy(cot_hbm, cot_ref, sems.at[parts_n])]
    later[0].start()
    size = float(some * cols // 8)
    lanes = 4
    split = (cols // (8 * lanes), lanes, 8, chans)
    start = jnp.zeros((lanes, 8, chans), F32)
    parts = []
    for n in range(parts_n):
        copies[n].wait()
        f, y0 = n // 2, n % 2 * some
        if n % 2 and f >= first:
            sem = sems.at[parts_n + 1 + f - first]
            later.append(pltpu.make_async_copy(video_ref.at[0, f], tail_ref.at[0, f - first], sem))
            later[-1].start()

        def add(y, acc, f=f, y0=y0):
            return acc + jnp.sum(video_ref[0, f, y0 + y].astype(F32).reshape(split), axis=0)

        total = jnp.sum(lax.fori_loop(0, some, add, start, unroll=8), axis=0)
        mean = total / size

        def deviate(y, acc, f=f, y0=y0, mean=mean):
            away = video_ref[0, f, y0 + y].astype(F32).reshape(split) - mean
            return acc + jnp.sum(away * away, axis=0)

        squares = jnp.sum(lax.fori_loop(0, some, deviate, start, unroll=8), axis=0)
        keep = (f < info_ref[0]).astype(F32)
        parts.append((jnp.full((8, chans), size, F32) * keep, total * keep, squares * keep))
    for n, value in enumerate(merged(parts)):
        out_ref[n] = value
    for copy in later:
        copy.wait()


def merge_kernel(*refs):
    for n, value in enumerate(merged([ref[...] for ref in refs[:-1]])):
        refs[-1][n] = value


def cotangent_kernel(t0, info_ref, cot_ref, turned_ref, bias_ref, wide):
    rows, cols, chans = cot_ref.shape[2:]
    step = cols // TILE
    lanes = 4
    bias = jnp.zeros((lanes, 8, chans), F32)
    for t in range(turned_ref.shape[0]):
        keep = (t0 + t < info_ref[0]).astype(F32)

        def row(y, acc, t=t, keep=keep):
            value = cot_ref[0, t0 + t, y].astype(F32) * keep
            slot = wide.at[y % wide.shape[0]]
            slot[...] = value
            order = jnp.concatenate(
                [slot[pl.ds(r, TILE, stride=step), :] for r in range(step)], axis=0
            )
            turned_ref[t, y] = order.astype(BF16).T
            return acc + jnp.sum(value.reshape(cols // (8 * lanes), lanes, 8, chans), axis=0)

        bias = lax.fori_loop(0, rows, row, bias, unroll=8)
    bias_ref[...] = jnp.sum(bias, axis=0)


def packed(value):
    per = value.shape[0] - TILE
    total = value[per : per + 1] + value[per + 1 : per + 2] + value[per + 2 : per + 3]
    top = total.astype(BF16).astype(F32)
    mid = (total - top).astype(BF16).astype(F32)
    rest = total - top - mid
    tail = jnp.concatenate([top, mid, rest, jnp.zeros((TILE - 3, value.shape[1]), F32)], axis=0)
    return jnp.concatenate([value[:per].astype(BF16), tail.astype(BF16)], axis=0)


def weights_kernel(
    per, info_ref, turned_0, turned_1, bias_0, bias_1, video_ref, early_ref, near_ref, *refs
):
    far_ref, near_early_ref, far_early_ref, gain_ref, shift_ref, *refs = refs
    stats_ref, act_ref, keep_ref, *send_refs = refs[:-3]
    wide, acc, shards = refs[-3:]
    ahead = turned_0.shape[0]
    frames, rows, cols, chans = video_ref.shape[1:]
    before = early_ref.shape[1]
    step = cols // TILE
    slots = wide.shape[0]
    inside, first, has_low, has_high = info_ref[0], info_ref[1], info_ref[2], info_ref[3]
    count, total, squares = stats_ref[0], stats_ref[1], stats_ref[2]
    every = jnp.sum(count, axis=0, keepdims=True) * per
    mean = group_sum(jnp.sum(total, axis=0, keepdims=True), per) / every
    away = total / jnp.maximum(count, 1.0) - mean
    squares = jnp.sum(squares + count * (away * away), axis=0, keepdims=True)
    squares = group_sum(squares, per)
    odd = info_ref[6] == 1
    scale = 0.5 * lax.rsqrt(squares / every + 1e-05) * gain_ref[...]
    offset = 0.5 * shift_ref[...] - mean * scale
    wide[:, 0:8, :] = jnp.zeros((slots, 8, chans), F32)
    wide[:, 8 + cols : 16 + cols, :] = jnp.zeros((slots, 8, chans), F32)

    def row(values, keep, slot, f, y):
        half = values.astype(F32) * (scale * keep) + offset * keep
        wide[slot, 8 : 8 + cols, :] = half + half * jnp.tanh(half)
        for r in range(-1, step + 1):
            act_ref[f, y, r + 1] = wide[slot, pl.ds(8 + r, TILE, stride=step), :].astype(BF16)

    def kept(f):
        local = f - before
        return ((local < inside) & (first + local >= 0)).astype(F32)

    def inner(f, y, slot):
        local = f - before
        source = early_ref.at[0, f] if local < 0 else video_ref.at[0, local]
        row(source[y], kept(f), slot, f, y + 1)

    def border(f, side, slot):
        local = f - before
        near = near_early_ref[frames + local] if local < 0 else near_ref[local]
        far = far_early_ref[frames + local] if local < 0 else far_ref[local]
        near, far = near.astype(F32), far.astype(F32)
        if side:
            value, has = jnp.where(odd, far, near), has_high
        else:
            value, has = jnp.where(odd, near, far), has_low
        row(value, kept(f) * has.astype(F32), slot, f, side * (rows + 1))

    def all_rows(f):
        work = [functools.partial(border, f, side, side) for side in range(2)]
        return work + [functools.partial(inner, f, y, y % slots) for y in range(rows)]

    def many(y, carry):
        inner(0, y, y % slots)
        return carry

    lax.fori_loop(0, rows, many, 0, unroll=4)
    border(0, 0, 0)
    border(0, 1, 1)

    taps = [(kt, ky, kx) for kt in range(3) for ky in range(3) for kx in range(3)]
    pair = 2
    k = turned_0.shape[3]
    tms, dps, full = shards.shape[:3]
    size = full - TILE

    def place(tap):
        block = acc[:, tap * chans : (tap + 1) * chans].T
        done = 0
        while done < chans:
            shard, at = divmod(tap * chans + done, size)
            take = min(chans - done, size - at)
            shards[shard // dps, shard % dps, at : at + take, :] = block[done : done + take]
            done += take

    groups = [taps[j : j + pair] for j in range(0, len(taps), pair)]
    for t in range(frames):
        work = []
        if t == 0:
            for f in range(1, before + 1):
                work.append((f * 9 // pair, all_rows(f)))
        if t + before + 1 < frames + before:
            tasks = all_rows(t + before + 1)
            work.append((len(groups), tasks))
        slots_of = [[] for _ in groups]
        begin = 0
        for end, tasks in work:
            for n, task in enumerate(tasks):
                slots_of[begin + n * (end - begin) // len(tasks)].append(task)
            begin = end
        source = (turned_0 if t < ahead else turned_1).at[t % ahead]
        left = jnp.concatenate([source[y] for y in range(rows)], axis=1)
        for j, chosen in enumerate(groups):
            right = jnp.concatenate(
                [
                    act_ref[t + kt, ky : ky + rows, kx : kx + step].reshape(rows * k, chans)
                    for kt, ky, kx in chosen
                ],
                axis=1,
            )
            product = jnp.dot(left, right, preferred_element_type=F32)
            where = slice(j * pair * chans, (j * pair + len(chosen)) * chans)
            acc[:, where] = product if t == 0 else acc[:, where] + product
            for task in slots_of[j]:
                task()
            if t == frames - 1:
                for n in range(len(chosen)):
                    place(j * pair + n)
    bias = jnp.sum(bias_0[...] + bias_1[...], axis=0, keepdims=True)
    tail = jnp.concatenate([bias, jnp.zeros((TILE - 1, chans), F32)], axis=0)
    for i in range(tms):
        for j in range(dps):
            shards[i, j, size:full, :] = tail
    me = info_ref[4]
    keep_ref[...] = shards[me]
    for r in range(1, tms):
        send_refs[r - 1][...] = shards[me ^ r]


def spread_kernel(count, info_ref, after_ref, keep_ref, *refs):
    incoming, own_ref, send_refs = refs[:count], refs[count], refs[count + 1 :]
    me = info_ref[5]
    for r in range(len(send_refs) + 1):
        value = keep_ref[me ^ r]
        for ref in incoming:
            value = value + ref[me ^ r]
        if r == 0:
            own_ref[...] = value
        else:
            send_refs[r - 1][...] = packed(value)


def add_kernel(after_ref, *refs):
    values = [ref[...].astype(F32) for ref in refs[:-1]]
    while len(values) > 1:
        values = [sum(values[n : n + 2]) for n in range(0, len(values), 2)]
    refs[-1][...] = packed(values[0])


def taps_kernel(after_ref, kernel_ref, out_ref):
    kts, kys, kxs, chans = kernel_ref.shape[:4]
    pair = out_ref.shape[1] // chans
    zero = jnp.zeros((kys * kxs * chans, chans), BF16)
    span = kys * kxs * chans
    for f in range(kts + pair - 1):
        for g in range(pair):
            if 0 <= f - g < kts:
                value = kernel_ref[f - g].reshape(span, chans)
            else:
                value = zero
            out_ref[f * span : (f + 1) * span, g * chans : (g + 1) * chans] = value


def conv_kernel(
    piece, last, info_ref, after_ref, act_ref, taps_ref, video_ref, bias_ref, *refs
):
    out_ref, whole_ref, wide, sem = refs[-4:]
    t0, y0 = piece
    rows = out_ref.shape[1]
    if last is not None:
        out = pltpu.make_async_copy(refs[0], whole_ref.at[last], sem)
        out.start()
    cols, chans = out_ref.shape[2:]
    step = cols // TILE
    pair = taps_ref.shape[1] // chans
    used = [
        (f, ky, kx)
        for f in range(taps_ref.shape[0] // (9 * chans))
        for ky in range(3)
        for kx in range(3)
    ]
    left = jnp.concatenate(
        [
            act_ref[t0 + f, y0 + ky : y0 + ky + rows, kx : kx + step].reshape(rows * cols, chans)
            for f, ky, kx in used
        ],
        axis=1,
    )
    result = jnp.dot(left, taps_ref[...], preferred_element_type=F32)
    for f in range(pair):
        keep = (t0 + f < info_ref[0]).astype(F32)
        for y in range(rows):
            slot = f * rows + y
            for r in range(step):
                at = y * cols + r * TILE
                wide[slot, pl.ds(r, TILE, stride=step), :] = result[
                    at : at + TILE, f * chans : (f + 1) * chans
                ]
            value = video_ref[0, t0 + f, y0 + y].astype(F32) + wide[slot] + bias_ref[...]
            out_ref[f, y] = (value * keep).astype(BF16)
    if last is not None:
        out.wait()


def step_of(video, lengths, norm_gain, norm_shift, kernel, conv_bias, cotangent):
    frames, rows, cols, chans = video.shape[1:]
    per = chans // GROUPS
    step = cols // TILE
    before = kernel.shape[0] - 1
    tms, dps, spaces = (lax.axis_size(axis) for axis in ("tm", "dp", "space"))
    tm, dp, space = (lax.axis_index(axis) for axis in ("tm", "dp", "space"))
    first = tm * frames
    inside = jnp.clip(lengths[0] - first, -before, frames)
    info = jnp.stack(
        [
            inside,
            first,
            (space > 0).astype(jnp.int32),
            (space < spaces - 1).astype(jnp.int32),
            tm,
            dp,
            space % 2,
        ]
    ).astype(jnp.int32)

    source = pltpu.with_memory_space_constraint(video, pltpu.HBM)
    border = jax.ShapeDtypeStruct((frames, cols, chans), BF16)
    near, far = pl.pallas_call(
        ends_kernel,
        in_specs=[SMEM, ANY],
        out_specs=[VMEM, VMEM],
        out_shape=[border, border],
        scratch_shapes=[pltpu.SemaphoreType.DMA((2,))],
        compiler_params=params(1),
        name="ends",
    )(info, source)
    near = swap(near, "space", 1)
    between = [(i, i + 1) for i in range(1, spaces - 1, 2)]
    far = lax.ppermute(far, "space", between + [(j, i) for i, j in between])
    stats, local, masked_in, tail = pl.pallas_call(
        functools.partial(stats_kernel, before),
        in_specs=[SMEM, ANY, ANY],
        out_specs=[VMEM] * 4,
        out_shape=[
            jax.ShapeDtypeStruct((3, 8, chans), F32),
            jax.ShapeDtypeStruct(video.shape, BF16),
            jax.ShapeDtypeStruct(cotangent.shape, BF16),
            jax.ShapeDtypeStruct((1, before, rows, cols, chans), BF16),
        ],
        scratch_shapes=[pltpu.SemaphoreType.DMA((2 * frames + 1 + before,))],
        compiler_params=params(2),
        name="stats",
    )(info, source, pltpu.with_memory_space_constraint(cotangent, pltpu.HBM))
    following = [(i, (i + 1) % tms) for i in range(tms)]
    gathered = [stats] + [swap(stats, "tm", r) for r in range(1, tms)]
    early = lax.ppermute(tail, "tm", following)

    def together(arrays):
        return pl.pallas_call(
            merge_kernel,
            in_specs=[VMEM] * len(arrays),
            out_specs=VMEM,
            out_shape=jax.ShapeDtypeStruct((3, 8, chans), F32),
            compiler_params=params(1),
            name="merge",
        )(*arrays)

    stats = core_stats = together(gathered)
    by = 1
    while by < spaces:
        other = swap(stats, "space", by)
        stats = together([stats, other])
        by *= 2
    near_early = lax.ppermute(near, "tm", following)
    far_early = lax.ppermute(far, "tm", following)
    pair = 2
    taps = pl.pallas_call(
        taps_kernel,
        in_specs=[ANY, VMEM],
        out_specs=VMEM,
        out_shape=jax.ShapeDtypeStruct(
            ((kernel.shape[0] + pair - 1) * 9 * chans, pair * chans), BF16
        ),
        compiler_params=params(2),
        name="taps",
    )(core_stats, kernel)

    ahead = frames // 2
    turned, bias = [], []
    for n in range(2):
        some, part = pl.pallas_call(
            functools.partial(cotangent_kernel, n * ahead),
            in_specs=[SMEM, VMEM],
            out_specs=[VMEM, VMEM],
            out_shape=[
                jax.ShapeDtypeStruct((ahead, rows, chans, cols), BF16),
                jax.ShapeDtypeStruct((8, chans), F32),
            ],
            scratch_shapes=[pltpu.VMEM((8, cols, chans), F32)],
            compiler_params=params(2),
            name="cotangent",
        )(info, masked_in)
        turned.append(some)
        bias.append(part)

    count = kernel.shape[0] * kernel.shape[1] * kernel.shape[2] * chans
    shards_n = tms * dps
    assert count % shards_n == 0
    shard = count // shards_n
    full = shard + TILE
    act, keep, *sends = pl.pallas_call(
        functools.partial(weights_kernel, per),
        in_specs=[SMEM] + [VMEM] * 13,
        out_specs=[VMEM] * (1 + tms),
        out_shape=[
            jax.ShapeDtypeStruct((frames + before, rows + 2, step + 2, TILE, chans), BF16)
        ]
        + [jax.ShapeDtypeStruct((dps, full, chans), F32)] * tms,
        scratch_shapes=[
            pltpu.VMEM((8, cols + 16, chans), F32),
            pltpu.VMEM((chans, count), F32),
            pltpu.VMEM((tms, dps, full, chans), F32),
        ],
        compiler_params=params(16),
        name="weights",
    )(
        info,
        *turned,
        *bias,
        local,
        early,
        near,
        far,
        near_early,
        far_early,
        norm_gain.reshape(1, chans),
        norm_shift.reshape(1, chans),
        stats,
    )

    block = 4
    pieces = [(t0, y0) for t0 in range(0, frames, pair) for y0 in range(0, rows, block)]
    done = []

    whole = jax.ShapeDtypeStruct(video.shape, BF16)

    def where(n):
        t0, y0 = pieces[n]
        return 0, pl.ds(t0, pair), pl.ds(y0, block)

    def cover(after, number):
        for _ in range(min(number, len(pieces) - len(done))):
            n = len(done)
            made = list(done[-1]) if done else []
            piece, output = pl.pallas_call(
                functools.partial(conv_kernel, pieces[n], where(n - 1) if made else None),
                in_specs=[SMEM, ANY, VMEM, VMEM, VMEM, VMEM] + [VMEM, ANY][: len(made)],
                out_specs=[VMEM, ANY],
                out_shape=[jax.ShapeDtypeStruct((pair, block, cols, chans), BF16), whole],
                scratch_shapes=[
                    pltpu.VMEM((pair * block, cols, chans), F32),
                    pltpu.SemaphoreType.DMA,
                ],
                input_output_aliases={7: 1} if made else {},
                compiler_params=params(6),
                name="conv",
            )(info, after, act, taps, local, conv_bias.reshape(1, chans), *made)
            done.append((piece, output))
            after = piece
        return after

    def exchanged(arrays, axis):
        result = []
        for n, array in enumerate(arrays):
            result.append(swap(array, axis, n + 1))
        return result

    incoming = [swap(send, "tm", r + 1) for r, send in enumerate(sends)]
    token = cover(keep, 1)
    own, *sends = pl.pallas_call(
        functools.partial(spread_kernel, len(incoming)),
        in_specs=[SMEM, ANY] + [VMEM] * (1 + len(incoming)),
        out_specs=[VMEM] * dps,
        out_shape=[jax.ShapeDtypeStruct((full, chans), F32)]
        + [jax.ShapeDtypeStruct((full, chans), BF16)] * (dps - 1),
        compiler_params=params(4),
        name="spread",
    )(info, token, keep, *incoming)

    def added(dtype, after, *arrays):
        return pl.pallas_call(
            add_kernel,
            in_specs=[ANY] + [VMEM] * len(arrays),
            out_specs=VMEM,
            out_shape=jax.ShapeDtypeStruct((full, chans), dtype),
            compiler_params=params(2),
            name="added",
        )(after, *arrays)

    incoming = exchanged(sends, "dp")
    token = cover(own, 2)
    total = added(BF16, token, own, *incoming)
    others = exchanged([total] * (spaces - 1), "space")
    token = cover(total, 4)
    total = added(BF16, token, total, *others)
    mine = [total] + exchanged([total] * (dps - 1), "dp")
    cover(total, len(pieces))
    shards = {(0, r): array for r, array in enumerate(mine)}
    for q in range(1, tms):
        for r, array in enumerate(mine):
            shards[q, r] = swap(array, "tm", q)
    final = 1 % dps
    order = sorted(shards, key=lambda key: key[1] == final)

    def collect(info_ref, *refs):
        shard_refs, piece_ref = refs[: len(order)], refs[len(order)]
        bias_ref, output_ref, out_ref, wide, sems = refs[-5:]
        copies = []
        for n, ((q, r), ref) in enumerate(zip(order, shard_refs)):
            at = (info_ref[4] ^ q) * dps + (info_ref[5] ^ r)
            wide[n] = ref[0:shard, :].astype(F32)
            copies.append(pltpu.make_async_copy(wide.at[n], out_ref.at[at], sems.at[n]))
            copies[-1].start()
        target = output_ref.at[where(len(pieces) - 1)]
        copies.append(pltpu.make_async_copy(piece_ref, target, sems.at[len(order)]))
        copies[-1].start()
        tail = shard_refs[0][shard : shard + TILE, :].astype(F32)
        bias_ref[...] = tail[0:1] + tail[1:2] + tail[2:3]
        for copy in copies:
            copy.wait()

    grad_bias, output, grad_kernel = pl.pallas_call(
        collect,
        in_specs=[SMEM] + [VMEM] * (len(order) + 1) + [ANY],
        out_specs=[VMEM, ANY, ANY],
        out_shape=[
            jax.ShapeDtypeStruct((1, chans), F32),
            whole,
            jax.ShapeDtypeStruct((shards_n, shard, chans), F32),
        ],
        scratch_shapes=[
            pltpu.VMEM((len(order), shard, chans), F32),
            pltpu.SemaphoreType.DMA((len(order) + 1,)),
        ],
        input_output_aliases={len(order) + 2: 1},
        compiler_params=params(4),
        name="collect",
    )(info, *[shards[key] for key in order], *done[-1])

    return output, grad_kernel.reshape(kernel.shape), grad_bias.reshape(chans)


def solution(mesh):
    return jax.shard_map(
        step_of,
        mesh=mesh,
        in_specs=(
            P("dp", "tm", "space", None, None),
            P("dp"),
            P(),
            P(),
            P(),
            P(),
            P("dp", "tm", "space", None, None),
        ),
        out_specs=(P("dp", "tm", "space", None, None), P(), P()),
        check_vma=False,
    )
```

```python
import functools

import jax
import jax.numpy as jnp
from jax import lax
from jax.experimental import pallas as pl
from jax.experimental.pallas import tpu as pltpu
from jax.sharding import PartitionSpec as P


GROUPS = 32
TILE = 16
F32 = jnp.float32
BF16 = jnp.bfloat16
VMEM = pl.BlockSpec(memory_space=pltpu.VMEM)
ANY = pl.BlockSpec(memory_space=pl.ANY)
SMEM = pl.BlockSpec(memory_space=pltpu.SMEM)


def params(mib):
    return pltpu.CompilerParams(vmem_limit_bytes=mib * 1024 * 1024)


def swap(array, axis, by):
    length = lax.axis_size(axis)
    assert length & (length - 1) == 0
    return lax.ppermute(array, axis, [(i, i ^ by) for i in range(length)])


def group_sum(row, per):
    value = jnp.broadcast_to(row, (8, row.shape[1]))
    lane = lax.broadcasted_iota(jnp.int32, value.shape, 1)
    size = value.shape[1]
    step = 1
    while step < per:
        up = pltpu.roll(value, size - step, 1)
        down = pltpu.roll(value, step, 1)
        value = value + jnp.where((lane & step) == 0, up, down)
        step *= 2
    return value[0:1]


def merged(parts):
    count = sum(part[0] for part in parts)
    total = sum(part[1] for part in parts)
    mean = total / jnp.maximum(count, 1.0)
    squares = jnp.zeros_like(mean)
    for part in parts:
        away = part[1] / jnp.maximum(part[0], 1.0) - mean
        squares = squares + (part[2] + part[0] * (away * away))
    return count, total, squares


def ends_kernel(info_ref, video_hbm, near_ref, far_ref, sems):
    rows = video_hbm.shape[2]
    odd = info_ref[6]
    copies = [
        pltpu.make_async_copy(video_hbm.at[0, :, row], ref, sems.at[n])
        for n, (row, ref) in enumerate(
            (((1 - odd) * (rows - 1), near_ref), (odd * (rows - 1), far_ref))
        )
    ]
    for copy in copies:
        copy.start()
    for copy in copies:
        copy.wait()


def stats_kernel(before, info_ref, video_hbm, cot_hbm, *refs):
    out_ref, video_ref, cot_ref, tail_ref, sems = refs
    frames, rows, cols, chans = video_ref.shape[1:]
    parts_n = 2 * frames
    some = rows // 2
    first = frames - before
    copies = []
    for n in range(parts_n):
        at = (0, n // 2, pl.ds(n % 2 * some, some))
        copies.append(pltpu.make_async_copy(video_hbm.at[at], video_ref.at[at], sems.at[n]))
        copies[-1].start()
    later = [pltpu.make_async_copy(cot_hbm, cot_ref, sems.at[parts_n])]
    later[0].start()
    size = float(some * cols // 8)
    lanes = 4
    split = (cols // (8 * lanes), lanes, 8, chans)
    start = jnp.zeros((lanes, 8, chans), F32)
    parts = []
    for n in range(parts_n):
        copies[n].wait()
        f, y0 = n // 2, n % 2 * some
        if n % 2 and f >= first:
            sem = sems.at[parts_n + 1 + f - first]
            later.append(pltpu.make_async_copy(video_ref.at[0, f], tail_ref.at[0, f - first], sem))
            later[-1].start()

        def add(y, acc, f=f, y0=y0):
            return acc + jnp.sum(video_ref[0, f, y0 + y].astype(F32).reshape(split), axis=0)

        total = jnp.sum(lax.fori_loop(0, some, add, start, unroll=8), axis=0)
        mean = total / size

        def deviate(y, acc, f=f, y0=y0, mean=mean):
            away = video_ref[0, f, y0 + y].astype(F32).reshape(split) - mean
            return acc + jnp.sum(away * away, axis=0)

        squares = jnp.sum(lax.fori_loop(0, some, deviate, start, unroll=8), axis=0)
        keep = (f < info_ref[0]).astype(F32)
        parts.append((jnp.full((8, chans), size, F32) * keep, total * keep, squares * keep))
    for n, value in enumerate(merged(parts)):
        out_ref[n] = value
    for copy in later:
        copy.wait()


def merge_kernel(*refs):
    for n, value in enumerate(merged([ref[...] for ref in refs[:-1]])):
        refs[-1][n] = value


def cotangent_kernel(t0, info_ref, cot_ref, turned_ref, bias_ref, wide):
    rows, cols, chans = cot_ref.shape[2:]
    step = cols // TILE
    lanes = 4
    bias = jnp.zeros((lanes, 8, chans), F32)
    for t in range(turned_ref.shape[0]):
        keep = (t0 + t < info_ref[0]).astype(F32)

        def row(y, acc, t=t, keep=keep):
            value = cot_ref[0, t0 + t, y].astype(F32) * keep
            slot = wide.at[y % wide.shape[0]]
            slot[...] = value
            order = jnp.concatenate(
                [slot[pl.ds(r, TILE, stride=step), :] for r in range(step)], axis=0
            )
            turned_ref[t, y] = order.astype(BF16).T
            return acc + jnp.sum(value.reshape(cols // (8 * lanes), lanes, 8, chans), axis=0)

        bias = lax.fori_loop(0, rows, row, bias, unroll=8)
    bias_ref[...] = jnp.sum(bias, axis=0)


def packed(value):
    per = value.shape[0] - TILE
    total = value[per : per + 1] + value[per + 1 : per + 2] + value[per + 2 : per + 3]
    top = total.astype(BF16).astype(F32)
    mid = (total - top).astype(BF16).astype(F32)
    rest = total - top - mid
    tail = jnp.concatenate([top, mid, rest, jnp.zeros((TILE - 3, value.shape[1]), F32)], axis=0)
    return jnp.concatenate([value[:per].astype(BF16), tail.astype(BF16)], axis=0)


def weights_kernel(
    parts_n, per, info_ref, turned_0, turned_1, bias_0, bias_1, video_ref, early_ref, near_ref, *refs
):
    far_ref, near_early_ref, far_early_ref, gain_ref, shift_ref, *refs = refs
    parts, (act_ref, keep_ref, *send_refs) = refs[:parts_n], refs[parts_n:-3]
    wide, acc, shards = refs[-3:]
    ahead = turned_0.shape[0]
    frames, rows, cols, chans = video_ref.shape[1:]
    before = early_ref.shape[1]
    step = cols // TILE
    slots = wide.shape[0]
    inside, first, has_low, has_high = info_ref[0], info_ref[1], info_ref[2], info_ref[3]
    count, total, squares = merged([ref[...] for ref in parts])
    every = jnp.sum(count, axis=0, keepdims=True) * per
    mean = group_sum(jnp.sum(total, axis=0, keepdims=True), per) / every
    away = total / jnp.maximum(count, 1.0) - mean
    squares = jnp.sum(squares + count * (away * away), axis=0, keepdims=True)
    squares = group_sum(squares, per)
    odd = info_ref[6] == 1
    scale = 0.5 * lax.rsqrt(squares / every + 1e-05) * gain_ref[...]
    offset = 0.5 * shift_ref[...] - mean * scale
    wide[:, 0:8, :] = jnp.zeros((slots, 8, chans), F32)
    wide[:, 8 + cols : 16 + cols, :] = jnp.zeros((slots, 8, chans), F32)

    def row(values, keep, slot, f, y):
        half = values.astype(F32) * (scale * keep) + offset * keep
        wide[slot, 8 : 8 + cols, :] = half + half * jnp.tanh(half)
        for r in range(-1, step + 1):
            act_ref[f, y, r + 1] = wide[slot, pl.ds(8 + r, TILE, stride=step), :].astype(BF16)

    def kept(f):
        local = f - before
        return ((local < inside) & (first + local >= 0)).astype(F32)

    def inner(f, y, slot):
        local = f - before
        source = early_ref.at[0, f] if local < 0 else video_ref.at[0, local]
        row(source[y], kept(f), slot, f, y + 1)

    def border(f, side, slot):
        local = f - before
        near = near_early_ref[frames + local] if local < 0 else near_ref[local]
        far = far_early_ref[frames + local] if local < 0 else far_ref[local]
        near, far = near.astype(F32), far.astype(F32)
        if side:
            value, has = jnp.where(odd, far, near), has_high
        else:
            value, has = jnp.where(odd, near, far), has_low
        row(value, kept(f) * has.astype(F32), slot, f, side * (rows + 1))

    def all_rows(f):
        work = [functools.partial(border, f, side, side) for side in range(2)]
        return work + [functools.partial(inner, f, y, y % slots) for y in range(rows)]

    def many(y, carry):
        inner(0, y, y % slots)
        return carry

    lax.fori_loop(0, rows, many, 0, unroll=4)
    border(0, 0, 0)
    border(0, 1, 1)

    taps = [(kt, ky, kx) for kt in range(3) for ky in range(3) for kx in range(3)]
    pair = 2
    k = turned_0.shape[3]
    tms, dps, full = shards.shape[:3]
    size = full - TILE

    def place(tap):
        block = acc[:, tap * chans : (tap + 1) * chans].T
        done = 0
        while done < chans:
            shard, at = divmod(tap * chans + done, size)
            take = min(chans - done, size - at)
            shards[shard // dps, shard % dps, at : at + take, :] = block[done : done + take]
            done += take

    groups = [taps[j : j + pair] for j in range(0, len(taps), pair)]
    for t in range(frames):
        work = []
        if t == 0:
            for f in range(1, before + 1):
                work.append((f * 9 // pair, all_rows(f)))
        if t + before + 1 < frames + before:
            tasks = all_rows(t + before + 1)
            work.append((len(groups), tasks))
        slots_of = [[] for _ in groups]
        begin = 0
        for end, tasks in work:
            for n, task in enumerate(tasks):
                slots_of[begin + n * (end - begin) // len(tasks)].append(task)
            begin = end
        source = (turned_0 if t < ahead else turned_1).at[t % ahead]
        left = jnp.concatenate([source[y] for y in range(rows)], axis=1)
        for j, chosen in enumerate(groups):
            right = jnp.concatenate(
                [
                    act_ref[t + kt, ky : ky + rows, kx : kx + step].reshape(rows * k, chans)
                    for kt, ky, kx in chosen
                ],
                axis=1,
            )
            product = jnp.dot(left, right, preferred_element_type=F32)
            where = slice(j * pair * chans, (j * pair + len(chosen)) * chans)
            acc[:, where] = product if t == 0 else acc[:, where] + product
            for task in slots_of[j]:
                task()
            if t == frames - 1:
                for n in range(len(chosen)):
                    place(j * pair + n)
    bias = jnp.sum(bias_0[...] + bias_1[...], axis=0, keepdims=True)
    tail = jnp.concatenate([bias, jnp.zeros((TILE - 1, chans), F32)], axis=0)
    for i in range(tms):
        for j in range(dps):
            shards[i, j, size:full, :] = tail
    me = info_ref[4]
    keep_ref[...] = shards[me]
    for r in range(1, tms):
        send_refs[r - 1][...] = shards[me ^ r]


def spread_kernel(count, info_ref, after_ref, keep_ref, *refs):
    incoming, own_ref, send_refs = refs[:count], refs[count], refs[count + 1 :]
    me = info_ref[5]
    for r in range(len(send_refs) + 1):
        value = keep_ref[me ^ r]
        for ref in incoming:
            value = value + ref[me ^ r]
        if r == 0:
            own_ref[...] = value
        else:
            send_refs[r - 1][...] = packed(value)


def add_kernel(after_ref, *refs):
    values = [ref[...].astype(F32) for ref in refs[:-1]]
    while len(values) > 1:
        values = [sum(values[n : n + 2]) for n in range(0, len(values), 2)]
    refs[-1][...] = packed(values[0])


def taps_kernel(after_ref, kernel_ref, out_ref):
    kts, kys, kxs, chans = kernel_ref.shape[:4]
    pair = out_ref.shape[1] // chans
    zero = jnp.zeros((kys * kxs * chans, chans), BF16)
    span = kys * kxs * chans
    for f in range(kts + pair - 1):
        for g in range(pair):
            if 0 <= f - g < kts:
                value = kernel_ref[f - g].reshape(span, chans)
            else:
                value = zero
            out_ref[f * span : (f + 1) * span, g * chans : (g + 1) * chans] = value


def conv_kernel(
    piece, last, info_ref, after_ref, act_ref, taps_ref, video_ref, bias_ref, *refs
):
    out_ref, whole_ref, wide, sem = refs[-4:]
    t0, y0 = piece
    rows = out_ref.shape[1]
    if last is not None:
        out = pltpu.make_async_copy(refs[0], whole_ref.at[last], sem)
        out.start()
    cols, chans = out_ref.shape[2:]
    step = cols // TILE
    pair = taps_ref.shape[1] // chans
    used = [
        (f, ky, kx)
        for f in range(taps_ref.shape[0] // (9 * chans))
        for ky in range(3)
        for kx in range(3)
    ]
    left = jnp.concatenate(
        [
            act_ref[t0 + f, y0 + ky : y0 + ky + rows, kx : kx + step].reshape(rows * cols, chans)
            for f, ky, kx in used
        ],
        axis=1,
    )
    result = jnp.dot(left, taps_ref[...], preferred_element_type=F32)
    for f in range(pair):
        keep = (t0 + f < info_ref[0]).astype(F32)
        for y in range(rows):
            slot = f * rows + y
            for r in range(step):
                at = y * cols + r * TILE
                wide[slot, pl.ds(r, TILE, stride=step), :] = result[
                    at : at + TILE, f * chans : (f + 1) * chans
                ]
            value = video_ref[0, t0 + f, y0 + y].astype(F32) + wide[slot] + bias_ref[...]
            out_ref[f, y] = (value * keep).astype(BF16)
    if last is not None:
        out.wait()


def step_of(video, lengths, norm_gain, norm_shift, kernel, conv_bias, cotangent):
    frames, rows, cols, chans = video.shape[1:]
    per = chans // GROUPS
    step = cols // TILE
    before = kernel.shape[0] - 1
    tms, dps, spaces = (lax.axis_size(axis) for axis in ("tm", "dp", "space"))
    tm, dp, space = (lax.axis_index(axis) for axis in ("tm", "dp", "space"))
    first = tm * frames
    inside = jnp.clip(lengths[0] - first, -before, frames)
    info = jnp.stack(
        [
            inside,
            first,
            (space > 0).astype(jnp.int32),
            (space < spaces - 1).astype(jnp.int32),
            tm,
            dp,
            space % 2,
        ]
    ).astype(jnp.int32)

    source = pltpu.with_memory_space_constraint(video, pltpu.HBM)
    border = jax.ShapeDtypeStruct((frames, cols, chans), BF16)
    near, far = pl.pallas_call(
        ends_kernel,
        in_specs=[SMEM, ANY],
        out_specs=[VMEM, VMEM],
        out_shape=[border, border],
        scratch_shapes=[pltpu.SemaphoreType.DMA((2,))],
        compiler_params=params(1),
        name="ends",
    )(info, source)
    near = swap(near, "space", 1)
    between = [(i, i + 1) for i in range(1, spaces - 1, 2)]
    far = lax.ppermute(far, "space", between + [(j, i) for i, j in between])
    stats, local, masked_in, tail = pl.pallas_call(
        functools.partial(stats_kernel, before),
        in_specs=[SMEM, ANY, ANY],
        out_specs=[VMEM] * 4,
        out_shape=[
            jax.ShapeDtypeStruct((3, 8, chans), F32),
            jax.ShapeDtypeStruct(video.shape, BF16),
            jax.ShapeDtypeStruct(cotangent.shape, BF16),
            jax.ShapeDtypeStruct((1, before, rows, cols, chans), BF16),
        ],
        scratch_shapes=[pltpu.SemaphoreType.DMA((2 * frames + 1 + before,))],
        compiler_params=params(2),
        name="stats",
    )(info, source, pltpu.with_memory_space_constraint(cotangent, pltpu.HBM))
    following = [(i, (i + 1) % tms) for i in range(tms)]
    gathered = [stats] + [swap(stats, "tm", r) for r in range(1, tms)]
    early = lax.ppermute(tail, "tm", following)

    def together(arrays):
        return pl.pallas_call(
            merge_kernel,
            in_specs=[VMEM] * len(arrays),
            out_specs=VMEM,
            out_shape=jax.ShapeDtypeStruct((3, 8, chans), F32),
            compiler_params=params(1),
            name="merge",
        )(*arrays)

    stats = together(gathered)
    parts = [stats] + [swap(stats, "space", r) for r in range(1, spaces)]
    near_early = lax.ppermute(near, "tm", following)
    far_early = lax.ppermute(far, "tm", following)
    pair = 2
    taps = pl.pallas_call(
        taps_kernel,
        in_specs=[ANY, VMEM],
        out_specs=VMEM,
        out_shape=jax.ShapeDtypeStruct(
            ((kernel.shape[0] + pair - 1) * 9 * chans, pair * chans), BF16
        ),
        compiler_params=params(2),
        name="taps",
    )(stats, kernel)

    ahead = frames // 2
    turned, bias = [], []
    for n in range(2):
        some, part = pl.pallas_call(
            functools.partial(cotangent_kernel, n * ahead),
            in_specs=[SMEM, VMEM],
            out_specs=[VMEM, VMEM],
            out_shape=[
                jax.ShapeDtypeStruct((ahead, rows, chans, cols), BF16),
                jax.ShapeDtypeStruct((8, chans), F32),
            ],
            scratch_shapes=[pltpu.VMEM((8, cols, chans), F32)],
            compiler_params=params(2),
            name="cotangent",
        )(info, masked_in)
        turned.append(some)
        bias.append(part)

    count = kernel.shape[0] * kernel.shape[1] * kernel.shape[2] * chans
    shards_n = tms * dps
    assert count % shards_n == 0
    shard = count // shards_n
    full = shard + TILE
    act, keep, *sends = pl.pallas_call(
        functools.partial(weights_kernel, spaces, per),
        in_specs=[SMEM] + [VMEM] * (12 + spaces),
        out_specs=[VMEM] * (1 + tms),
        out_shape=[
            jax.ShapeDtypeStruct((frames + before, rows + 2, step + 2, TILE, chans), BF16)
        ]
        + [jax.ShapeDtypeStruct((dps, full, chans), F32)] * tms,
        scratch_shapes=[
            pltpu.VMEM((8, cols + 16, chans), F32),
            pltpu.VMEM((chans, count), F32),
            pltpu.VMEM((tms, dps, full, chans), F32),
        ],
        compiler_params=params(16),
        name="weights",
    )(
        info,
        *turned,
        *bias,
        local,
        early,
        near,
        far,
        near_early,
        far_early,
        norm_gain.reshape(1, chans),
        norm_shift.reshape(1, chans),
        *parts,
    )

    block = 4
    pieces = [(t0, y0) for t0 in range(0, frames, pair) for y0 in range(0, rows, block)]
    done = []

    whole = jax.ShapeDtypeStruct(video.shape, BF16)

    def where(n):
        t0, y0 = pieces[n]
        return 0, pl.ds(t0, pair), pl.ds(y0, block)

    def cover(after, number):
        for _ in range(min(number, len(pieces) - len(done))):
            n = len(done)
            made = list(done[-1]) if done else []
            piece, output = pl.pallas_call(
                functools.partial(conv_kernel, pieces[n], where(n - 1) if made else None),
                in_specs=[SMEM, ANY, VMEM, VMEM, VMEM, VMEM] + [VMEM, ANY][: len(made)],
                out_specs=[VMEM, ANY],
                out_shape=[jax.ShapeDtypeStruct((pair, block, cols, chans), BF16), whole],
                scratch_shapes=[
                    pltpu.VMEM((pair * block, cols, chans), F32),
                    pltpu.SemaphoreType.DMA,
                ],
                input_output_aliases={7: 1} if made else {},
                compiler_params=params(6),
                name="conv",
            )(info, after, act, taps, local, conv_bias.reshape(1, chans), *made)
            done.append((piece, output))
            after = piece
        return after

    def exchanged(arrays, axis):
        result = []
        for n, array in enumerate(arrays):
            result.append(swap(array, axis, n + 1))
        return result

    incoming = [swap(send, "tm", r + 1) for r, send in enumerate(sends)]
    token = cover(keep, 1)
    own, *sends = pl.pallas_call(
        functools.partial(spread_kernel, len(incoming)),
        in_specs=[SMEM, ANY] + [VMEM] * (1 + len(incoming)),
        out_specs=[VMEM] * dps,
        out_shape=[jax.ShapeDtypeStruct((full, chans), F32)]
        + [jax.ShapeDtypeStruct((full, chans), BF16)] * (dps - 1),
        compiler_params=params(4),
        name="spread",
    )(info, token, keep, *incoming)

    def added(dtype, after, *arrays):
        return pl.pallas_call(
            add_kernel,
            in_specs=[ANY] + [VMEM] * len(arrays),
            out_specs=VMEM,
            out_shape=jax.ShapeDtypeStruct((full, chans), dtype),
            compiler_params=params(2),
            name="added",
        )(after, *arrays)

    incoming = exchanged(sends, "dp")
    token = cover(own, 2)
    total = added(BF16, token, own, *incoming)
    others = exchanged([total] * (spaces - 1), "space")
    token = cover(total, 4)
    total = added(BF16, token, total, *others)
    mine = [total] + exchanged([total] * (dps - 1), "dp")
    cover(total, len(pieces))
    shards = {(0, r): array for r, array in enumerate(mine)}
    for q in range(1, tms):
        for r, array in enumerate(mine):
            shards[q, r] = swap(array, "tm", q)
    final = 1 % dps
    order = sorted(shards, key=lambda key: key[1] == final)

    def collect(info_ref, *refs):
        shard_refs, piece_ref = refs[: len(order)], refs[len(order)]
        bias_ref, output_ref, out_ref, wide, sems = refs[-5:]
        copies = []
        for n, ((q, r), ref) in enumerate(zip(order, shard_refs)):
            at = (info_ref[4] ^ q) * dps + (info_ref[5] ^ r)
            wide[n] = ref[0:shard, :].astype(F32)
            copies.append(pltpu.make_async_copy(wide.at[n], out_ref.at[at], sems.at[n]))
            copies[-1].start()
        target = output_ref.at[where(len(pieces) - 1)]
        copies.append(pltpu.make_async_copy(piece_ref, target, sems.at[len(order)]))
        copies[-1].start()
        tail = shard_refs[0][shard : shard + TILE, :].astype(F32)
        bias_ref[...] = tail[0:1] + tail[1:2] + tail[2:3]
        for copy in copies:
            copy.wait()

    grad_bias, output, grad_kernel = pl.pallas_call(
        collect,
        in_specs=[SMEM] + [VMEM] * (len(order) + 1) + [ANY],
        out_specs=[VMEM, ANY, ANY],
        out_shape=[
            jax.ShapeDtypeStruct((1, chans), F32),
            whole,
            jax.ShapeDtypeStruct((shards_n, shard, chans), F32),
        ],
        scratch_shapes=[
            pltpu.VMEM((len(order), shard, chans), F32),
            pltpu.SemaphoreType.DMA((len(order) + 1,)),
        ],
        input_output_aliases={len(order) + 2: 1},
        compiler_params=params(4),
        name="collect",
    )(info, *[shards[key] for key in order], *done[-1])

    return output, grad_kernel.reshape(kernel.shape), grad_bias.reshape(chans)


def solution(mesh):
    return jax.shard_map(
        step_of,
        mesh=mesh,
        in_specs=(
            P("dp", "tm", "space", None, None),
            P("dp"),
            P(),
            P(),
            P(),
            P(),
            P("dp", "tm", "space", None, None),
        ),
        out_specs=(P("dp", "tm", "space", None, None), P(), P()),
        check_vma=False,
    )
```

```python
import functools

import jax
import jax.numpy as jnp
from jax import lax
from jax.experimental import pallas as pl
from jax.experimental.pallas import tpu as pltpu
from jax.sharding import PartitionSpec as P


GROUPS = 32
TILE = 16
F32 = jnp.float32
BF16 = jnp.bfloat16
VMEM = pl.BlockSpec(memory_space=pltpu.VMEM)
ANY = pl.BlockSpec(memory_space=pl.ANY)
SMEM = pl.BlockSpec(memory_space=pltpu.SMEM)


def params(mib):
    return pltpu.CompilerParams(vmem_limit_bytes=mib * 1024 * 1024)


def swap(array, axis, by):
    length = lax.axis_size(axis)
    assert length & (length - 1) == 0
    return lax.ppermute(array, axis, [(i, i ^ by) for i in range(length)])


def exchanged(arrays, axis):
    result = []
    for n, array in enumerate(arrays):
        result.append(swap(array, axis, n + 1))
    return result


def group_sum(row, per):
    value = jnp.broadcast_to(row, (8, row.shape[1]))
    lane = lax.broadcasted_iota(jnp.int32, value.shape, 1)
    size = value.shape[1]
    step = 1
    while step < per:
        up = pltpu.roll(value, size - step, 1)
        down = pltpu.roll(value, step, 1)
        value = value + jnp.where((lane & step) == 0, up, down)
        step *= 2
    return value[0:1]


def merged(parts):
    count = sum(part[0] for part in parts)
    total = sum(part[1] for part in parts)
    mean = total / jnp.maximum(count, 1.0)
    squares = jnp.zeros_like(mean)
    for part in parts:
        away = part[1] / jnp.maximum(part[0], 1.0) - mean
        squares = squares + (part[2] + part[0] * (away * away))
    return count, total, squares


def ends_kernel(video_hbm, near_ref, far_ref, sems):
    rows = video_hbm.shape[2]
    odd = lax.axis_index("space") % 2
    copies = [
        pltpu.make_async_copy(video_hbm.at[0, :, row], ref, sems.at[n])
        for n, (row, ref) in enumerate(
            (((1 - odd) * (rows - 1), near_ref), (odd * (rows - 1), far_ref))
        )
    ]
    for copy in copies:
        copy.start()
    for copy in copies:
        copy.wait()


def stats_kernel(before, info_ref, video_hbm, cot_hbm, *refs):
    out_ref, video_ref, cot_ref, tail_ref, sems = refs
    frames, rows, cols, chans = video_ref.shape[1:]
    parts_n = 2 * frames
    some = rows // 2
    first = frames - before
    copies = []
    for n in range(parts_n):
        at = (0, n // 2, pl.ds(n % 2 * some, some))
        copies.append(pltpu.make_async_copy(video_hbm.at[at], video_ref.at[at], sems.at[n]))
        copies[-1].start()
    later = [pltpu.make_async_copy(cot_hbm, cot_ref, sems.at[parts_n])]
    later[0].start()
    size = float(some * cols // 8)
    lanes = 4
    split = (cols // (8 * lanes), lanes, 8, chans)
    start = jnp.zeros((lanes, 8, chans), F32)
    parts = []
    for n in range(parts_n):
        copies[n].wait()
        f, y0 = n // 2, n % 2 * some
        if n % 2 and f >= first:
            sem = sems.at[parts_n + 1 + f - first]
            later.append(pltpu.make_async_copy(video_ref.at[0, f], tail_ref.at[0, f - first], sem))
            later[-1].start()

        def add(y, acc, f=f, y0=y0):
            return acc + jnp.sum(video_ref[0, f, y0 + y].astype(F32).reshape(split), axis=0)

        total = jnp.sum(lax.fori_loop(0, some, add, start, unroll=8), axis=0)
        mean = total / size

        def deviate(y, acc, f=f, y0=y0, mean=mean):
            away = video_ref[0, f, y0 + y].astype(F32).reshape(split) - mean
            return acc + jnp.sum(away * away, axis=0)

        squares = jnp.sum(lax.fori_loop(0, some, deviate, start, unroll=8), axis=0)
        keep = (f < info_ref[0]).astype(F32)
        parts.append((jnp.full((8, chans), size, F32) * keep, total * keep, squares * keep))
    for n, value in enumerate(merged(parts)):
        out_ref[n] = value
    for copy in later:
        copy.wait()


def merge_kernel(*refs):
    for n, value in enumerate(merged([ref[...] for ref in refs[:-1]])):
        refs[-1][n] = value


def cotangent_kernel(t0, info_ref, cot_ref, turned_ref, bias_ref, wide):
    rows, cols, chans = cot_ref.shape[2:]
    step = cols // TILE
    lanes = 4
    bias = jnp.zeros((lanes, 8, chans), F32)
    for t in range(turned_ref.shape[0]):
        keep = (t0 + t < info_ref[0]).astype(F32)

        def row(y, acc, t=t, keep=keep):
            value = cot_ref[0, t0 + t, y].astype(F32) * keep
            slot = wide.at[y % wide.shape[0]]
            slot[...] = value
            order = jnp.concatenate(
                [slot[pl.ds(r, TILE, stride=step), :] for r in range(step)], axis=0
            )
            turned_ref[t, y] = order.astype(BF16).T
            return acc + jnp.sum(value.reshape(cols // (8 * lanes), lanes, 8, chans), axis=0)

        bias = lax.fori_loop(0, rows, row, bias, unroll=8)
    bias_ref[...] = jnp.sum(bias, axis=0)


def packed(value):
    per = value.shape[0] - TILE
    total = value[per : per + 1] + value[per + 1 : per + 2] + value[per + 2 : per + 3]
    top = total.astype(BF16).astype(F32)
    mid = (total - top).astype(BF16).astype(F32)
    rest = total - top - mid
    tail = jnp.concatenate([top, mid, rest, jnp.zeros((TILE - 3, value.shape[1]), F32)], axis=0)
    return jnp.concatenate([value[:per].astype(BF16), tail.astype(BF16)], axis=0)


def weights_kernel(
    parts_n, per, info_ref, turned_0, turned_1, bias_0, bias_1, video_ref, early_ref, near_ref, *refs
):
    far_ref, near_early_ref, far_early_ref, gain_ref, shift_ref, *refs = refs
    parts, (act_ref, keep_ref, *send_refs) = refs[:parts_n], refs[parts_n:-3]
    wide, acc, shards = refs[-3:]
    ahead = turned_0.shape[0]
    frames, rows, cols, chans = video_ref.shape[1:]
    before = early_ref.shape[1]
    step = cols // TILE
    slots = wide.shape[0]
    inside, first, has_low, has_high = info_ref[0], info_ref[1], info_ref[2], info_ref[3]
    count, total, squares = merged([ref[...] for ref in parts])
    every = jnp.sum(count, axis=0, keepdims=True) * per
    mean = group_sum(jnp.sum(total, axis=0, keepdims=True), per) / every
    away = total / jnp.maximum(count, 1.0) - mean
    squares = jnp.sum(squares + count * (away * away), axis=0, keepdims=True)
    squares = group_sum(squares, per)
    odd = info_ref[6] == 1
    scale = 0.5 * lax.rsqrt(squares / every + 1e-05) * gain_ref[...]
    offset = 0.5 * shift_ref[...] - mean * scale
    wide[:, 0:8, :] = jnp.zeros((slots, 8, chans), F32)
    wide[:, 8 + cols : 16 + cols, :] = jnp.zeros((slots, 8, chans), F32)

    def row(values, keep, slot, f, y):
        half = values.astype(F32) * (scale * keep) + offset * keep
        wide[slot, 8 : 8 + cols, :] = half + half * jnp.tanh(half)
        for r in range(-1, step + 1):
            act_ref[f, y, r + 1] = wide[slot, pl.ds(8 + r, TILE, stride=step), :].astype(BF16)

    def kept(f):
        local = f - before
        return ((local < inside) & (first + local >= 0)).astype(F32)

    def inner(f, y, slot):
        local = f - before
        source = early_ref.at[0, f] if local < 0 else video_ref.at[0, local]
        row(source[y], kept(f), slot, f, y + 1)

    def border(f, side, slot):
        local = f - before
        near = near_early_ref[frames + local] if local < 0 else near_ref[local]
        far = far_early_ref[frames + local] if local < 0 else far_ref[local]
        near, far = near.astype(F32), far.astype(F32)
        if side:
            value, has = jnp.where(odd, far, near), has_high
        else:
            value, has = jnp.where(odd, near, far), has_low
        row(value, kept(f) * has.astype(F32), slot, f, side * (rows + 1))

    def all_rows(f):
        work = [functools.partial(border, f, side, side) for side in range(2)]
        return work + [functools.partial(inner, f, y, y % slots) for y in range(rows)]

    def many(y, carry):
        inner(0, y, y % slots)
        return carry

    lax.fori_loop(0, rows, many, 0, unroll=4)
    border(0, 0, 0)
    border(0, 1, 1)

    taps = [(kt, ky, kx) for kt in range(3) for ky in range(3) for kx in range(3)]
    pair = 2
    k = turned_0.shape[3]
    tms, dps, full = shards.shape[:3]
    size = full - TILE

    def place(tap):
        block = acc[:, tap * chans : (tap + 1) * chans].T
        done = 0
        while done < chans:
            shard, at = divmod(tap * chans + done, size)
            take = min(chans - done, size - at)
            shards[shard // dps, shard % dps, at : at + take, :] = block[done : done + take]
            done += take

    groups = [taps[j : j + pair] for j in range(0, len(taps), pair)]
    for t in range(frames):
        work = []
        if t == 0:
            for f in range(1, before + 1):
                work.append((f * 9 // pair, all_rows(f)))
        if t + before + 1 < frames + before:
            tasks = all_rows(t + before + 1)
            work.append((len(groups), tasks))
        slots_of = [[] for _ in groups]
        begin = 0
        for end, tasks in work:
            for n, task in enumerate(tasks):
                slots_of[begin + n * (end - begin) // len(tasks)].append(task)
            begin = end
        source = (turned_0 if t < ahead else turned_1).at[t % ahead]
        left = jnp.concatenate([source[y] for y in range(rows)], axis=1)
        for j, chosen in enumerate(groups):
            right = jnp.concatenate(
                [
                    act_ref[t + kt, ky : ky + rows, kx : kx + step].reshape(rows * k, chans)
                    for kt, ky, kx in chosen
                ],
                axis=1,
            )
            product = jnp.dot(left, right, preferred_element_type=F32)
            where = slice(j * pair * chans, (j * pair + len(chosen)) * chans)
            acc[:, where] = product if t == 0 else acc[:, where] + product
            for task in slots_of[j]:
                task()
            if t == frames - 1:
                for n in range(len(chosen)):
                    place(j * pair + n)
    bias = jnp.sum(bias_0[...] + bias_1[...], axis=0, keepdims=True)
    tail = jnp.concatenate([bias, jnp.zeros((TILE - 1, chans), F32)], axis=0)
    for i in range(tms):
        for j in range(dps):
            shards[i, j, size:full, :] = tail
    me = info_ref[4]
    keep_ref[...] = shards[me]
    for r in range(1, tms):
        send_refs[r - 1][...] = shards[me ^ r]


def spread_kernel(count, info_ref, after_ref, keep_ref, *refs):
    incoming, own_ref, send_refs = refs[:count], refs[count], refs[count + 1 :]
    me = info_ref[5]
    for r in range(len(send_refs) + 1):
        value = keep_ref[me ^ r]
        for ref in incoming:
            value = value + ref[me ^ r]
        if r == 0:
            own_ref[...] = value
        else:
            send_refs[r - 1][...] = packed(value)


def add_kernel(after_ref, *refs):
    values = [ref[...].astype(F32) for ref in refs[:-1]]
    while len(values) > 1:
        values = [sum(values[n : n + 2]) for n in range(0, len(values), 2)]
    refs[-1][...] = packed(values[0])


def taps_kernel(after_ref, kernel_ref, out_ref):
    kts, kys, kxs, chans = kernel_ref.shape[:4]
    pair = out_ref.shape[1] // chans
    zero = jnp.zeros((kys * kxs * chans, chans), BF16)
    span = kys * kxs * chans
    for f in range(kts + pair - 1):
        for g in range(pair):
            if 0 <= f - g < kts:
                value = kernel_ref[f - g].reshape(span, chans)
            else:
                value = zero
            out_ref[f * span : (f + 1) * span, g * chans : (g + 1) * chans] = value


def conv_kernel(
    piece, last, info_ref, after_ref, act_ref, taps_ref, video_ref, bias_ref, *refs
):
    out_ref, whole_ref, wide, sem = refs[-4:]
    t0, y0 = piece
    rows = out_ref.shape[1]
    if last is not None:
        out = pltpu.make_async_copy(refs[0], whole_ref.at[last], sem)
        out.start()
    cols, chans = out_ref.shape[2:]
    step = cols // TILE
    pair = taps_ref.shape[1] // chans
    used = [
        (f, ky, kx)
        for f in range(taps_ref.shape[0] // (9 * chans))
        for ky in range(3)
        for kx in range(3)
    ]
    left = jnp.concatenate(
        [
            act_ref[t0 + f, y0 + ky : y0 + ky + rows, kx : kx + step].reshape(rows * cols, chans)
            for f, ky, kx in used
        ],
        axis=1,
    )
    result = jnp.dot(left, taps_ref[...], preferred_element_type=F32)
    for f in range(pair):
        keep = (t0 + f < info_ref[0]).astype(F32)
        for y in range(rows):
            slot = f * rows + y
            for r in range(step):
                at = y * cols + r * TILE
                wide[slot, pl.ds(r, TILE, stride=step), :] = result[
                    at : at + TILE, f * chans : (f + 1) * chans
                ]
            value = video_ref[0, t0 + f, y0 + y].astype(F32) + wide[slot] + bias_ref[...]
            out_ref[f, y] = (value * keep).astype(BF16)
    if last is not None:
        out.wait()


def step_of(video, lengths, norm_gain, norm_shift, kernel, conv_bias, cotangent):
    frames, rows, cols, chans = video.shape[1:]
    per = chans // GROUPS
    step = cols // TILE
    before = kernel.shape[0] - 1
    tms, dps, spaces = (lax.axis_size(axis) for axis in ("tm", "dp", "space"))
    tm, dp, space = (lax.axis_index(axis) for axis in ("tm", "dp", "space"))
    first = tm * frames
    inside = jnp.clip(lengths[0] - first, -before, frames)
    info = jnp.stack(
        [
            inside,
            first,
            (space > 0).astype(jnp.int32),
            (space < spaces - 1).astype(jnp.int32),
            tm,
            dp,
            space % 2,
        ]
    ).astype(jnp.int32)

    source = pltpu.with_memory_space_constraint(video, pltpu.HBM)
    border = jax.ShapeDtypeStruct((frames, cols, chans), BF16)
    near, far = pl.pallas_call(
        ends_kernel,
        in_specs=[ANY],
        out_specs=[VMEM, VMEM],
        out_shape=[border, border],
        scratch_shapes=[pltpu.SemaphoreType.DMA((2,))],
        compiler_params=params(1),
        name="ends",
    )(source)
    near = swap(near, "space", 1)
    between = [(i, i + 1) for i in range(1, spaces - 1, 2)]
    far = lax.ppermute(far, "space", between + [(j, i) for i, j in between])
    stats, local, masked_in, tail = pl.pallas_call(
        functools.partial(stats_kernel, before),
        in_specs=[SMEM, ANY, ANY],
        out_specs=[VMEM] * 4,
        out_shape=[
            jax.ShapeDtypeStruct((3, 8, chans), F32),
            jax.ShapeDtypeStruct(video.shape, BF16),
            jax.ShapeDtypeStruct(cotangent.shape, BF16),
            jax.ShapeDtypeStruct((1, before, rows, cols, chans), BF16),
        ],
        scratch_shapes=[pltpu.SemaphoreType.DMA((2 * frames + 1 + before,))],
        compiler_params=params(2),
        name="stats",
    )(info, source, pltpu.with_memory_space_constraint(cotangent, pltpu.HBM))
    following = [(i, (i + 1) % tms) for i in range(tms)]
    gathered = [stats] + [swap(stats, "tm", r) for r in range(1, tms)]
    early = lax.ppermute(tail, "tm", following)

    def together(arrays):
        return pl.pallas_call(
            merge_kernel,
            in_specs=[VMEM] * len(arrays),
            out_specs=VMEM,
            out_shape=jax.ShapeDtypeStruct((3, 8, chans), F32),
            compiler_params=params(1),
            name="merge",
        )(*arrays)

    stats = together(gathered)
    parts = [stats] + exchanged([stats] * (spaces - 1), "space")
    near_early = lax.ppermute(near, "tm", following)
    far_early = lax.ppermute(far, "tm", following)
    pair = 2
    taps = pl.pallas_call(
        taps_kernel,
        in_specs=[ANY, VMEM],
        out_specs=VMEM,
        out_shape=jax.ShapeDtypeStruct(
            ((kernel.shape[0] + pair - 1) * 9 * chans, pair * chans), BF16
        ),
        compiler_params=params(2),
        name="taps",
    )(stats, kernel)

    ahead = frames // 2
    turned, bias = [], []
    for n in range(2):
        some, part = pl.pallas_call(
            functools.partial(cotangent_kernel, n * ahead),
            in_specs=[SMEM, VMEM],
            out_specs=[VMEM, VMEM],
            out_shape=[
                jax.ShapeDtypeStruct((ahead, rows, chans, cols), BF16),
                jax.ShapeDtypeStruct((8, chans), F32),
            ],
            scratch_shapes=[pltpu.VMEM((8, cols, chans), F32)],
            compiler_params=params(2),
            name="cotangent",
        )(info, masked_in)
        turned.append(some)
        bias.append(part)

    count = kernel.shape[0] * kernel.shape[1] * kernel.shape[2] * chans
    shards_n = tms * dps
    assert count % shards_n == 0
    shard = count // shards_n
    full = shard + TILE
    act, keep, *sends = pl.pallas_call(
        functools.partial(weights_kernel, spaces, per),
        in_specs=[SMEM] + [VMEM] * (12 + spaces),
        out_specs=[VMEM] * (1 + tms),
        out_shape=[
            jax.ShapeDtypeStruct((frames + before, rows + 2, step + 2, TILE, chans), BF16)
        ]
        + [jax.ShapeDtypeStruct((dps, full, chans), F32)] * tms,
        scratch_shapes=[
            pltpu.VMEM((8, cols + 16, chans), F32),
            pltpu.VMEM((chans, count), F32),
            pltpu.VMEM((tms, dps, full, chans), F32),
        ],
        compiler_params=params(16),
        name="weights",
    )(
        info,
        *turned,
        *bias,
        local,
        early,
        near,
        far,
        near_early,
        far_early,
        norm_gain.reshape(1, chans),
        norm_shift.reshape(1, chans),
        *parts,
    )

    block = 4
    pieces = [(t0, y0) for t0 in range(0, frames, pair) for y0 in range(0, rows, block)]
    done = []

    whole = jax.ShapeDtypeStruct(video.shape, BF16)

    def where(n):
        t0, y0 = pieces[n]
        return 0, pl.ds(t0, pair), pl.ds(y0, block)

    def cover(after, number):
        for _ in range(min(number, len(pieces) - len(done))):
            n = len(done)
            made = list(done[-1]) if done else []
            piece, output = pl.pallas_call(
                functools.partial(conv_kernel, pieces[n], where(n - 1) if made else None),
                in_specs=[SMEM, ANY, VMEM, VMEM, VMEM, VMEM] + [VMEM, ANY][: len(made)],
                out_specs=[VMEM, ANY],
                out_shape=[jax.ShapeDtypeStruct((pair, block, cols, chans), BF16), whole],
                scratch_shapes=[
                    pltpu.VMEM((pair * block, cols, chans), F32),
                    pltpu.SemaphoreType.DMA,
                ],
                input_output_aliases={7: 1} if made else {},
                compiler_params=params(6),
                name="conv",
            )(info, after, act, taps, local, conv_bias.reshape(1, chans), *made)
            done.append((piece, output))
            after = piece
        return after

    incoming = [swap(send, "tm", r + 1) for r, send in enumerate(sends)]
    token = cover(keep, 1)
    own, *sends = pl.pallas_call(
        functools.partial(spread_kernel, len(incoming)),
        in_specs=[SMEM, ANY] + [VMEM] * (1 + len(incoming)),
        out_specs=[VMEM] * dps,
        out_shape=[jax.ShapeDtypeStruct((full, chans), F32)]
        + [jax.ShapeDtypeStruct((full, chans), BF16)] * (dps - 1),
        compiler_params=params(4),
        name="spread",
    )(info, token, keep, *incoming)

    def added(dtype, after, *arrays):
        return pl.pallas_call(
            add_kernel,
            in_specs=[ANY] + [VMEM] * len(arrays),
            out_specs=VMEM,
            out_shape=jax.ShapeDtypeStruct((full, chans), dtype),
            compiler_params=params(2),
            name="added",
        )(after, *arrays)

    incoming = exchanged(sends, "dp")
    token = cover(own, 2)
    total = added(BF16, token, own, *incoming)
    others = exchanged([total] * (spaces - 1), "space")
    token = cover(total, 4)
    total = added(BF16, token, total, *others)
    mine = [total] + exchanged([total] * (dps - 1), "dp")
    cover(total, len(pieces))
    shards = {(0, r): array for r, array in enumerate(mine)}
    for q in range(1, tms):
        for r, array in enumerate(mine):
            shards[q, r] = swap(array, "tm", q)
    final = 1 % dps
    order = sorted(shards, key=lambda key: key[1] == final)

    def collect(info_ref, *refs):
        shard_refs, piece_ref = refs[: len(order)], refs[len(order)]
        bias_ref, output_ref, out_ref, wide, sems = refs[-5:]
        copies = []
        for n, ((q, r), ref) in enumerate(zip(order, shard_refs)):
            at = (info_ref[4] ^ q) * dps + (info_ref[5] ^ r)
            wide[n] = ref[0:shard, :].astype(F32)
            copies.append(pltpu.make_async_copy(wide.at[n], out_ref.at[at], sems.at[n]))
            copies[-1].start()
        target = output_ref.at[where(len(pieces) - 1)]
        copies.append(pltpu.make_async_copy(piece_ref, target, sems.at[len(order)]))
        copies[-1].start()
        tail = shard_refs[0][shard : shard + TILE, :].astype(F32)
        bias_ref[...] = tail[0:1] + tail[1:2] + tail[2:3]
        for copy in copies:
            copy.wait()

    grad_bias, output, grad_kernel = pl.pallas_call(
        collect,
        in_specs=[SMEM] + [VMEM] * (len(order) + 1) + [ANY],
        out_specs=[VMEM, ANY, ANY],
        out_shape=[
            jax.ShapeDtypeStruct((1, chans), F32),
            whole,
            jax.ShapeDtypeStruct((shards_n, shard, chans), F32),
        ],
        scratch_shapes=[
            pltpu.VMEM((len(order), shard, chans), F32),
            pltpu.SemaphoreType.DMA((len(order) + 1,)),
        ],
        input_output_aliases={len(order) + 2: 1},
        compiler_params=params(4),
        name="collect",
    )(info, *[shards[key] for key in order], *done[-1])

    return output, grad_kernel.reshape(kernel.shape), grad_bias.reshape(chans)


def solution(mesh):
    return jax.shard_map(
        step_of,
        mesh=mesh,
        in_specs=(
            P("dp", "tm", "space", None, None),
            P("dp"),
            P(),
            P(),
            P(),
            P(),
            P("dp", "tm", "space", None, None),
        ),
        out_specs=(P("dp", "tm", "space", None, None), P(), P()),
        check_vma=False,
    )
```
